512 devices in a mesh: ctx: 32 (over y, x, core), tp: 16 (over z).
Axes of the slice: x: 4, y: 4, z: 16, core: 2. Of those that a mesh axis runs over, the one named last changes fastest.
Arguments:
- hidden: bfloat16 [16384, 4096], P('ctx', 'tp'), may hold values from -6 to 6
- norm_gain: float32 [4096], replicated, may hold values from 0.1 to 16
- query_weight: bfloat16 [4096, 4096], P('ctx', 'tp'), may hold values from -0.09375 to 0.09375
- key_weight: bfloat16 [1024, 4096], P(None, 'tp'), may hold values from -0.1875 to 0.1875
- value_weight: bfloat16 [1024, 4096], P(None, 'tp'), may hold values from -0.1875 to 0.1875
- out_weight: bfloat16 [4096, 4096], P('tp'), may hold values from -0.09375 to 0.09375
- encodings: bfloat16 [512, 128, 1024], P('ctx', 'tp'), may hold values from -70 to 70
- row_place: int32 [512], replicated, may hold values from 0 to 511, as said below
- neighbour_ids: int32 [256, 2], replicated, may hold values from 0 to 511, as said below
- neighbour_counts: int32 [256], replicated, may hold values from 1 to 2
Outputs:
- mixed: bfloat16 [16384, 4096], P(('ctx', 'tp'))
The draws below stay inside these ranges and needn't reach their ends.
Inputs may be any that keep to these rules, and one draw needn't show every extreme that they name: `row_place`: a permutation of 0 to 511. `neighbour_ids`: the 16 neighbour slots of the spans of one ctx index name neighbours stored on exactly 16 ctx indices, one slot for each of them; a neighbour may serve several slots.
All inputs are finite; a program needn't handle non-finite values.
Results may differ from the reference program's by a relative error of at most 0.039.
The reference program's roundings to bfloat16 on the way (of `normed`, `queries`, `keys`, `values`, `weights` and `attended`) count: a program that leaves them out, or rounds other values in their place, can miss the bound.
Values may be sent and summed in bfloat16 or wider, within the bound.
A program may use at most 128 MiB of HBM per device.

```python
import jax
import jax.numpy as jnp
from jax import lax

D = 4096
E = 1024
HS = 128
H = 32
CH = 64
NT = 128
KNB = 2
LENGTH = 8192
TOKENS = 16384
SPANS = 256
ROWS_DEV = 16
POOL = 512
N_CTX = 32
N_TP = 16


def neighbour_layout(key):
    slot_cap = (ROWS_DEV + N_CTX - 1) // N_CTX
    placement = jax.random.permutation(jax.random.fold_in(key, 11), POOL).astype(jnp.int32)
    extra_reward = jax.random.randint(jax.random.fold_in(key, 12), (N_CTX,), 0, 4) * (4 * N_CTX)
    random_jitter = jax.random.randint(jax.random.fold_in(key, 13), (N_CTX, N_CTX), 0, 4 * N_CTX)
    rank_order = (random_jitter + extra_reward[None, :]) * N_CTX + jnp.arange(N_CTX)[None, :]
    ordering = jnp.argsort(-rank_order, axis=1)
    chosen = ordering[:, :ROWS_DEV // slot_cap]
    sources = jnp.repeat(chosen, slot_cap, axis=1)
    mixing_keys = jax.random.randint(jax.random.fold_in(key, 14), (N_CTX, ROWS_DEV), 0, 1 << 20) * ROWS_DEV + jnp.arange(ROWS_DEV)[None, :]
    mixing = jnp.argsort(mixing_keys, axis=1)
    sources = jnp.take_along_axis(sources, mixing, axis=1)
    local_rows = jax.random.randint(jax.random.fold_in(key, 15), (N_CTX, ROWS_DEV), 0, ROWS_DEV)
    storage = (sources * ROWS_DEV + local_rows).reshape(-1)
    inverse = jnp.argsort(placement)
    neighbours = inverse[storage].reshape(SPANS, KNB).astype(jnp.int32)
    return (placement, neighbours)


def draw_row_place(key, part):
    return neighbour_layout(key)[0]


def draw_neighbour_ids(key, part):
    return neighbour_layout(key)[1]


def draw_norm_gain(key, part):
    result = 1.0 + 0.18 * jnp.clip(jax.random.normal(jax.random.fold_in(key, 32), (D,), jnp.float32), -5.0, 5.0)
    return result.astype(jnp.float32)


def draw_encodings(key, part):
    result = jnp.clip(jax.random.normal(jax.random.fold_in(key, 24), (POOL, NT, E), jnp.float32), -6.0, 6.0)
    return result.astype(jnp.bfloat16)


def with_ends(entries, rng, least, largest):
    longest = entries.shape.index(max(entries.shape))
    spots = []
    for shift in (0, 1):
        where = [jax.random.randint(jax.random.fold_in(rng, axis), (), 0, length) for axis, length in enumerate(entries.shape)]
        where[longest] = (where[longest] + shift) % entries.shape[longest]
        spots.append(tuple(where))
    return entries.at[spots[0]].set(least).at[spots[1]].set(largest)


def block_scale(stream_key, dims, shards, low, top_value):
    loudness = 1.0
    for dim, shards_of in shards:
        steps = jax.random.uniform(jax.random.fold_in(jax.random.fold_in(stream_key, 6), dim), (shards_of,), jnp.float32, low / len(shards), top_value / len(shards))
        loudness = loudness * jnp.repeat(jnp.exp(steps), dims[dim] // shards_of).reshape((-1,) + (1,) * (len(dims) - 1 - dim))
    return loudness


def gaussian(stream_key, extent, scale, most, cuts=(), dtype=jnp.bfloat16):
    drawn = scale * jax.random.normal(stream_key, extent, jnp.float32)
    if cuts:
        drawn = drawn * block_scale(stream_key, extent, cuts, -0.22, 0.18)
    return jnp.clip(drawn, -most, most).astype(dtype)


def setup_inputs(seed: int = 0) -> dict:
    key_list = jax.random.split(jax.random.key(seed), 11)
    return {
        "hidden": gaussian(key_list[0], (TOKENS, D), 1.0, 6.0, ((0, 32), (1, 16))),
        "norm_gain": draw_norm_gain(jax.random.fold_in(key_list[10], 71), 0),
        "query_weight": gaussian(key_list[2], (D, H * HS), D ** -0.5, 0.09375, ((0, 32), (1, 16))),
        "key_weight": gaussian(key_list[3], (E, H * HS), E ** -0.5, 0.1875, ((1, 16),)),
        "value_weight": gaussian(key_list[4], (E, H * HS), E ** -0.5, 0.1875, ((1, 16),)),
        "out_weight": gaussian(key_list[5], (H * HS, D), (H * HS) ** -0.5, 0.09375, ((0, 16),)),
        "encodings": draw_encodings(jax.random.fold_in(key_list[10], 71), 0),
        "row_place": draw_row_place(jax.random.fold_in(key_list[10], 71), 0),
        "neighbour_ids": draw_neighbour_ids(jax.random.fold_in(key_list[10], 71), 0),
        "neighbour_counts": with_ends(jax.random.randint(key_list[9], (SPANS,), 1, KNB + 1), jax.random.fold_in(key_list[9], 1), 1, KNB).astype(jnp.int32),
    }


epsilon = 1e-05
masked_score = -1e+30

def reference(hidden, norm_gain, query_weight, key_weight, value_weight, out_weight, encodings, row_place, neighbour_ids, neighbour_counts):
    head_width = H * HS
    values_wide = hidden.astype(jnp.float32)
    mean_square = lax.optimization_barrier(jnp.mean(values_wide * values_wide, axis=1, keepdims=True))
    normed = (values_wide * lax.rsqrt(mean_square + epsilon) * norm_gain[None, :]).astype(jnp.bfloat16)
    queries = (jnp.dot(normed, query_weight, preferred_element_type=jnp.float32) * HS ** (-0.5)).astype(jnp.bfloat16)
    shifted = jnp.concatenate([queries[CH - 1:], jnp.zeros((CH - 1, head_width), jnp.bfloat16)], axis=0)
    windows = shifted.reshape(SPANS, CH, H, HS)
    places = row_place[neighbour_ids]

    def single_span(operand):
        window, place_row, span_count = operand
        rows = encodings[place_row].reshape(KNB * NT, E)
        keys = jnp.dot(rows, key_weight, preferred_element_type=jnp.float32).astype(jnp.bfloat16).reshape(KNB * NT, H, HS)
        values = jnp.dot(rows, value_weight, preferred_element_type=jnp.float32).astype(jnp.bfloat16).reshape(KNB * NT, H, HS)
        scores = jnp.einsum('qhd,khd->hqk', window.astype(jnp.float32), keys.astype(jnp.float32))
        slot_of_key = jnp.arange(KNB * NT) // NT
        scores = jnp.where((slot_of_key < span_count)[None, None, :], scores, masked_score)
        peak = lax.optimization_barrier(jnp.max(scores, axis=2, keepdims=True))
        expos = jnp.exp(scores - peak)
        total = lax.optimization_barrier(jnp.sum(expos, axis=2))
        weights = expos.astype(jnp.bfloat16)
        blended = jnp.einsum('hqk,khd->qhd', weights.astype(jnp.float32), values.astype(jnp.float32))
        blended = blended / jnp.transpose(total)[:, :, None]
        return blended.reshape(CH, head_width)
    attended = lax.map(single_span, (windows, places, neighbour_counts))
    attended = attended.reshape(SPANS * CH, head_width)[:TOKENS - (CH - 1)]
    attended = jnp.concatenate([jnp.zeros((CH - 1, head_width), jnp.float32), attended], axis=0)
    position = jnp.arange(TOKENS)
    valid = position % LENGTH >= CH - 1
    attended = jnp.where(valid[:, None], attended, jnp.zeros_like(attended)).astype(jnp.bfloat16)
    group = head_width // N_TP
    result = jnp.zeros((TOKENS, D), jnp.float32)
    for index in range(N_TP):
        partial_sum = jnp.dot(attended[:, index * group:(index + 1) * group], out_weight[index * group:(index + 1) * group], preferred_element_type=jnp.float32).astype(jnp.bfloat16)
        partial_sum = lax.optimization_barrier(partial_sum)
        result = result + partial_sum.astype(jnp.float32)
    return result.astype(jnp.bfloat16)
```

```python
import jax
import jax.numpy as jnp
from jax import lax
from jax.sharding import PartitionSpec as P

HS = 128
CH = 64
KNB = 2
LENGTH = 8192


epsilon = 1e-05
masked_score = -1e30


def shifted(block, axis, distance):
    devices = range(lax.axis_size(axis))
    route = [(i - distance, i) for i in devices if i - distance in devices]
    return lax.ppermute(block, axis, route)


def ring_gather(block, axis, dim):
    count = lax.axis_size(axis)
    pieces = [block]
    right = block
    left = block
    for step in range(count // 2):
        right = lax.ppermute(
            right, axis, [(i, (i + 1) % count) for i in range(count)]
        )
        pieces.append(right)
        if step < count - 1 - count // 2:
            left = lax.ppermute(left, axis, [(i, (i - 1) % count) for i in range(count)])
            pieces.append(left)
    return jnp.concatenate(pieces, axis=dim)


def project_rows(rows, weight):
    flat = rows.reshape(-1, rows.shape[-1])
    return jnp.dot(flat, weight, preferred_element_type=jnp.float32).astype(jnp.bfloat16)


def local(
    hidden,
    norm_gain,
    query_weight,
    key_weight,
    value_weight,
    out_weight,
    encodings,
    row_place,
    neighbour_ids,
    neighbour_counts,
):
    ctx_count = lax.axis_size("ctx")
    ctx_index = lax.axis_index("ctx")
    tok_dev = hidden.shape[0]
    rows_dev = encodings.shape[0]
    slice_tokens = encodings.shape[1]
    enc_width = encodings.shape[2]
    span_dev = tok_dev // CH
    head_width = query_weight.shape[1]
    head_count = head_width // HS
    slot_cap = -(-rows_dev // ctx_count)
    whole = lax.all_gather(hidden, "tp", axis=1, tiled=True)
    values_wide = whole.astype(jnp.float32)
    mean_square = jnp.mean(values_wide * values_wide, axis=1, keepdims=True)
    normed = (values_wide * lax.rsqrt(mean_square + epsilon) * norm_gain[None, :]).astype(
        jnp.bfloat16
    )
    query_full = lax.all_to_all(
        jnp.broadcast_to(query_weight[None], (ctx_count,) + query_weight.shape),
        "ctx",
        split_axis=0,
        concat_axis=0,
        tiled=True,
    ).reshape(-1, query_weight.shape[1])
    query_sum = jnp.dot(normed, query_full, preferred_element_type=jnp.float32)
    queries = (query_sum * HS ** (-0.5)).astype(jnp.bfloat16)
    storage = row_place[neighbour_ids.reshape(-1)].reshape(ctx_count, rows_dev)
    sources = storage // rows_dev
    local_rows = storage % rows_dev
    from_here = sources == ctx_index
    rank_position = jnp.cumsum(from_here.astype(jnp.int32), axis=1) - 1
    picked_rows = from_here & (rank_position == 0)
    pick_list = [jnp.sum(jnp.where(picked_rows, local_rows, 0), axis=1)]
    fill_list = [jnp.any(picked_rows, axis=1)]
    pick_index = jnp.stack(pick_list, axis=1)
    fill_mask = jnp.stack(fill_list, axis=1)
    outgoing = encodings[pick_index] * fill_mask[:, :, None, None].astype(jnp.bfloat16)
    incoming = lax.all_to_all(outgoing, "ctx", split_axis=0, concat_axis=0, tiled=True)
    own_sources = lax.dynamic_index_in_dim(sources, ctx_index, 0, keepdims=False)
    slot_order = jnp.arange(rows_dev)
    earlier = (own_sources[:, None] == own_sources[None, :]) & (
        slot_order[None, :] < slot_order[:, None]
    )
    own_rank = jnp.sum(earlier.astype(jnp.int32), axis=1)
    flat_index = own_sources * slot_cap + own_rank
    picked = incoming.reshape(ctx_count * slot_cap, slice_tokens, enc_width)[flat_index]
    row_total = picked.shape[0]
    full_rows = ring_gather(picked, "tp", 1)
    keys = project_rows(full_rows, key_weight).reshape(row_total, -1, head_width)
    values = project_rows(full_rows, value_weight).reshape(row_total, -1, head_width)
    neighbour_len = keys.shape[1]
    prior_keys, prior_values = shifted(
        (keys[row_total - KNB :], values[row_total - KNB :]), "ctx", 1
    )
    key_stack = jnp.concatenate([prior_keys, keys], axis=0)
    value_stack = jnp.concatenate([prior_values, values], axis=0)
    key_blocks = key_stack.reshape(span_dev + 1, KNB * neighbour_len, head_count, HS)
    value_blocks = value_stack.reshape(span_dev + 1, KNB * neighbour_len, head_count, HS)
    first_span = ctx_index * span_dev
    local_counts = lax.dynamic_slice_in_dim(neighbour_counts, first_span, span_dev)
    prior_count = lax.dynamic_slice_in_dim(neighbour_counts, jnp.maximum(first_span - 1, 0), 1)
    block_counts = jnp.concatenate([prior_count, local_counts], axis=0)
    padded = jnp.concatenate(
        [
            jnp.zeros((1, head_width), jnp.bfloat16),
            queries,
            jnp.zeros((CH - 1, head_width), jnp.bfloat16),
        ],
        axis=0,
    )
    query_blocks = padded.reshape(span_dev + 1, CH, head_count, HS)
    scores = jnp.einsum(
        "wqhd,wkhd->whqk", query_blocks, key_blocks, preferred_element_type=jnp.float32
    )
    slot_of_key = jnp.arange(KNB * neighbour_len) // neighbour_len
    live = slot_of_key[None, :] < block_counts[:, None]
    scores = jnp.where(live[:, None, None, :], scores, masked_score)
    peak = jnp.max(scores, axis=3, keepdims=True)
    expos = jnp.exp(scores - peak)
    total = jnp.sum(expos, axis=3)
    weights = expos.astype(jnp.bfloat16)
    blended = jnp.einsum(
        "whqk,wkhd->wqhd", weights, value_blocks, preferred_element_type=jnp.float32
    )
    blended = blended / jnp.swapaxes(total, 1, 2)[:, :, :, None]
    blended = blended.reshape((span_dev + 1) * CH, head_width)[1 : tok_dev + 1]
    position = ctx_index * tok_dev + jnp.arange(tok_dev)
    valid = position % LENGTH >= CH - 1
    attended = jnp.where(valid[:, None], blended, jnp.zeros_like(blended)).astype(jnp.bfloat16)
    return lax.psum_scatter(
        jnp.dot(attended, out_weight, preferred_element_type=jnp.float32).astype(jnp.bfloat16),
        "tp",
        scatter_dimension=0,
        tiled=True,
    )


def solution(mesh):
    return jax.shard_map(
        local,
        mesh=mesh,
        in_specs=(
            P("ctx", "tp"),
            P(),
            P("ctx", "tp"),
            P(None, "tp"),
            P(None, "tp"),
            P("tp", None),
            P("ctx", "tp", None),
            P(),
            P(),
            P(),
        ),
        out_specs=P(("ctx", "tp"), None),
        check_vma=False,
    )
```

```python
import jax
import jax.numpy as jnp
from jax import lax
from jax.sharding import PartitionSpec as P

HS = 128
CH = 64
KNB = 2
LENGTH = 8192


epsilon = 1e-05
masked_score = -1e30


def shifted(block, axis, distance):
    devices = range(lax.axis_size(axis))
    route = [(i - distance, i) for i in devices if i - distance in devices]
    return lax.ppermute(block, axis, route)


def ring_shift(block, axis, distance):
    count = lax.axis_size(axis)
    return lax.ppermute(block, axis, [(i, (i + distance) % count) for i in range(count)])


def ring_gather(block, axis, dim):
    count = lax.axis_size(axis)
    before = []
    after = []
    right = block
    left = block
    for step in range(count // 2):
        right = ring_shift(right, axis, 1)
        before.insert(0, right)
        if step < count - 1 - count // 2:
            left = ring_shift(left, axis, -1)
            after.append(left)
    return jnp.concatenate(before + [block] + after, axis=dim)


def ring_reduce_scatter(partial, axis):
    count = lax.axis_size(axis)
    index = lax.axis_index(axis)
    rows = partial.shape[0] // count

    def part(offset):
        start = ((index + offset) % count) * rows
        return lax.dynamic_slice_in_dim(partial, start, rows).astype(jnp.float32)

    reach_right = count // 2
    reach_left = count - 1 - reach_right
    right = part(reach_right).astype(jnp.bfloat16)
    for step in range(1, reach_right + 1):
        right = ring_shift(right, axis, 1)
        if step < reach_right:
            right = (right.astype(jnp.float32) + part(reach_right - step)).astype(jnp.bfloat16)
    left = part(-reach_left).astype(jnp.bfloat16)
    for step in range(1, reach_left + 1):
        left = ring_shift(left, axis, -1)
        if step < reach_left:
            left = (left.astype(jnp.float32) + part(step - reach_left)).astype(jnp.bfloat16)
    total = part(0) + right.astype(jnp.float32) + left.astype(jnp.float32)
    return total.astype(jnp.bfloat16)


def project_rows(rows, weight):
    flat = rows.reshape(-1, rows.shape[-1])
    return jnp.dot(flat, weight, preferred_element_type=jnp.float32).astype(jnp.bfloat16)


def local(
    hidden,
    norm_gain,
    query_weight,
    key_weight,
    value_weight,
    out_weight,
    encodings,
    row_place,
    neighbour_ids,
    neighbour_counts,
):
    ctx_count = lax.axis_size("ctx")
    ctx_index = lax.axis_index("ctx")
    tok_dev = hidden.shape[0]
    rows_dev = encodings.shape[0]
    slice_tokens = encodings.shape[1]
    enc_width = encodings.shape[2]
    span_dev = tok_dev // CH
    head_width = query_weight.shape[1]
    head_count = head_width // HS
    slot_cap = -(-rows_dev // ctx_count)
    tp_count = lax.axis_size("tp")
    tp_index = lax.axis_index("tp")
    whole = ring_gather(hidden, "tp", 1)
    rotation = ((tp_index - tp_count // 2) % tp_count) * hidden.shape[1]
    gain = lax.dynamic_slice_in_dim(jnp.concatenate([norm_gain, norm_gain]), rotation, whole.shape[1])
    values_wide = whole.astype(jnp.float32)
    mean_square = jnp.mean(values_wide * values_wide, axis=1, keepdims=True)
    normed = (values_wide * lax.rsqrt(mean_square + epsilon) * gain[None, :]).astype(
        jnp.bfloat16
    )
    query_full = lax.all_to_all(
        jnp.broadcast_to(query_weight[None], (ctx_count,) + query_weight.shape),
        "ctx",
        split_axis=0,
        concat_axis=0,
        tiled=True,
    ).reshape(-1, query_weight.shape[1])
    query_full = lax.dynamic_slice_in_dim(
        jnp.concatenate([query_full, query_full]), rotation, query_full.shape[0]
    )
    query_sum = jnp.dot(normed, query_full, preferred_element_type=jnp.float32)
    queries = (query_sum * HS ** (-0.5)).astype(jnp.bfloat16)
    storage = row_place[neighbour_ids.reshape(-1)].reshape(ctx_count, rows_dev)
    sources = storage // rows_dev
    local_rows = storage % rows_dev
    from_here = sources == ctx_index
    rank_position = jnp.cumsum(from_here.astype(jnp.int32), axis=1) - 1
    picked_rows = from_here & (rank_position == 0)
    pick_list = [jnp.sum(jnp.where(picked_rows, local_rows, 0), axis=1)]
    fill_list = [jnp.any(picked_rows, axis=1)]
    pick_index = jnp.stack(pick_list, axis=1)
    fill_mask = jnp.stack(fill_list, axis=1)
    outgoing = encodings[pick_index] * fill_mask[:, :, None, None].astype(jnp.bfloat16)
    incoming = lax.all_to_all(outgoing, "ctx", split_axis=0, concat_axis=0, tiled=True)
    own_sources = lax.dynamic_index_in_dim(sources, ctx_index, 0, keepdims=False)
    slot_order = jnp.arange(rows_dev)
    earlier = (own_sources[:, None] == own_sources[None, :]) & (
        slot_order[None, :] < slot_order[:, None]
    )
    own_rank = jnp.sum(earlier.astype(jnp.int32), axis=1)
    flat_index = own_sources * slot_cap + own_rank
    picked = incoming.reshape(ctx_count * slot_cap, slice_tokens, enc_width)[flat_index]
    row_total = picked.shape[0]
    full_rows = ring_gather(picked, "tp", 1)
    keys = project_rows(full_rows, key_weight).reshape(row_total, -1, head_width)
    values = project_rows(full_rows, value_weight).reshape(row_total, -1, head_width)
    neighbour_len = keys.shape[1]
    prior_keys, prior_values = shifted(
        (keys[row_total - KNB :], values[row_total - KNB :]), "ctx", 1
    )
    key_stack = jnp.concatenate([prior_keys, keys], axis=0)
    value_stack = jnp.concatenate([prior_values, values], axis=0)
    key_blocks = key_stack.reshape(span_dev + 1, KNB * neighbour_len, head_count, HS)
    value_blocks = value_stack.reshape(span_dev + 1, KNB * neighbour_len, head_count, HS)
    first_span = ctx_index * span_dev
    local_counts = lax.dynamic_slice_in_dim(neighbour_counts, first_span, span_dev)
    prior_count = lax.dynamic_slice_in_dim(neighbour_counts, jnp.maximum(first_span - 1, 0), 1)
    block_counts = jnp.concatenate([prior_count, local_counts], axis=0)
    padded = jnp.concatenate(
        [
            jnp.zeros((1, head_width), jnp.bfloat16),
            queries,
            jnp.zeros((CH - 1, head_width), jnp.bfloat16),
        ],
        axis=0,
    )
    query_blocks = padded.reshape(span_dev + 1, CH, head_count, HS)
    scores = jnp.einsum(
        "wqhd,wkhd->whqk", query_blocks, key_blocks, preferred_element_type=jnp.float32
    )
    slot_of_key = jnp.arange(KNB * neighbour_len) // neighbour_len
    live = slot_of_key[None, :] < block_counts[:, None]
    scores = jnp.where(live[:, None, None, :], scores, masked_score)
    peak = jnp.max(scores, axis=3, keepdims=True)
    expos = jnp.exp(scores - peak)
    total = jnp.sum(expos, axis=3)
    weights = expos.astype(jnp.bfloat16)
    blended = jnp.einsum(
        "whqk,wkhd->wqhd", weights, value_blocks, preferred_element_type=jnp.float32
    )
    blended = blended / jnp.swapaxes(total, 1, 2)[:, :, :, None]
    blended = blended.reshape((span_dev + 1) * CH, head_width)[1 : tok_dev + 1]
    position = ctx_index * tok_dev + jnp.arange(tok_dev)
    valid = position % LENGTH >= CH - 1
    attended = jnp.where(valid[:, None], blended, jnp.zeros_like(blended)).astype(jnp.bfloat16)
    return ring_reduce_scatter(
        jnp.dot(attended, out_weight, preferred_element_type=jnp.float32).astype(jnp.bfloat16),
        "tp",
    )


def solution(mesh):
    return jax.shard_map(
        local,
        mesh=mesh,
        in_specs=(
            P("ctx", "tp"),
            P(),
            P("ctx", "tp"),
            P(None, "tp"),
            P(None, "tp"),
            P("tp", None),
            P("ctx", "tp", None),
            P(),
            P(),
            P(),
        ),
        out_specs=P(("ctx", "tp"), None),
        check_vma=False,
    )
```

```python
import functools

import jax
import jax.numpy as jnp
from jax import lax
from jax.experimental import pallas as pl
from jax.experimental.pallas import tpu as pltpu
from jax.sharding import PartitionSpec as P

HS = 128
CH = 64
KNB = 2
LENGTH = 8192


epsilon = 1e-05
masked_score = -1e30


def shifted(block, axis, distance):
    devices = range(lax.axis_size(axis))
    route = [(i - distance, i) for i in devices if i - distance in devices]
    return lax.ppermute(block, axis, route)


def ring_shift(block, axis, distance):
    count = lax.axis_size(axis)
    return lax.ppermute(block, axis, [(i, (i + distance) % count) for i in range(count)])


def ring_gather(block, axis, dim):
    count = lax.axis_size(axis)
    before = []
    after = []
    right = block
    left = block
    for step in range(count // 2):
        right = ring_shift(right, axis, 1)
        before.insert(0, right)
        if step < count - 1 - count // 2:
            left = ring_shift(left, axis, -1)
            after.append(left)
    return jnp.concatenate(before + [block] + after, axis=dim)


def ring_gather_kernel(x_ref, o_ref, send_sem, recv_sem, *, count, axis, other):
    me = lax.axis_index(axis)
    row = lax.axis_index(other)
    right = lax.rem(me + 1, count)
    left = lax.rem(me + count - 1, count)
    half = count // 2
    mesh_ids = pl.DeviceIdType.MESH
    barrier = pltpu.get_barrier_semaphore()
    for neighbour in (left, right):
        pl.semaphore_signal(barrier, inc=1, device_id=(row, neighbour), device_id_type=mesh_ids)
    pl.semaphore_wait(barrier, 2)
    o_ref[half] = x_ref[...]
    for step in range(1, half + 1):
        copies = []
        slot = half - step
        copies.append(
            pltpu.make_async_remote_copy(
                src_ref=x_ref if step == 1 else o_ref.at[slot + 1],
                dst_ref=o_ref.at[slot],
                send_sem=send_sem.at[slot],
                recv_sem=recv_sem.at[slot],
                device_id=(row, right),
                device_id_type=mesh_ids,
            )
        )
        if step < count - half:
            slot = half + step
            copies.append(
                pltpu.make_async_remote_copy(
                    src_ref=x_ref if step == 1 else o_ref.at[slot - 1],
                    dst_ref=o_ref.at[slot],
                    send_sem=send_sem.at[slot],
                    recv_sem=recv_sem.at[slot],
                    device_id=(row, left),
                    device_id_type=mesh_ids,
                )
            )
        for copy in copies:
            copy.start()
        for copy in copies:
            copy.wait_recv()
        for copy in copies:
            copy.wait_send()


def kernel_gather(block, axis, other, collective_id):
    count = lax.axis_size(axis)
    return pl.pallas_call(
        functools.partial(ring_gather_kernel, count=count, axis=axis, other=other),
        out_shape=jax.ShapeDtypeStruct((count,) + block.shape, block.dtype),
        in_specs=[pl.BlockSpec(memory_space=pltpu.VMEM)],
        out_specs=pl.BlockSpec(memory_space=pltpu.VMEM),
        scratch_shapes=[pltpu.SemaphoreType.DMA((count,)), pltpu.SemaphoreType.DMA((count,))],
        compiler_params=pltpu.CompilerParams(collective_id=collective_id, has_side_effects=True),
    )(block)


def ring_reduce_scatter(partial, axis):
    count = lax.axis_size(axis)
    index = lax.axis_index(axis)
    rows = partial.shape[0] // count

    def part(offset):
        start = ((index + offset) % count) * rows
        return lax.dynamic_slice_in_dim(partial, start, rows).astype(jnp.float32)

    reach_right = count // 2
    reach_left = count - 1 - reach_right
    right = part(reach_right).astype(jnp.bfloat16)
    for step in range(1, reach_right + 1):
        right = ring_shift(right, axis, 1)
        if step < reach_right:
            right = (right.astype(jnp.float32) + part(reach_right - step)).astype(jnp.bfloat16)
    left = part(-reach_left).astype(jnp.bfloat16)
    for step in range(1, reach_left + 1):
        left = ring_shift(left, axis, -1)
        if step < reach_left:
            left = (left.astype(jnp.float32) + part(step - reach_left)).astype(jnp.bfloat16)
    total = part(0) + right.astype(jnp.float32) + left.astype(jnp.float32)
    return total.astype(jnp.bfloat16)


def project_rows(rows, weight):
    flat = rows.reshape(-1, rows.shape[-1])
    return jnp.dot(flat, weight, preferred_element_type=jnp.float32).astype(jnp.bfloat16)


def local(
    hidden,
    norm_gain,
    query_weight,
    key_weight,
    value_weight,
    out_weight,
    encodings,
    row_place,
    neighbour_ids,
    neighbour_counts,
):
    ctx_count = lax.axis_size("ctx")
    ctx_index = lax.axis_index("ctx")
    tok_dev = hidden.shape[0]
    rows_dev = encodings.shape[0]
    slice_tokens = encodings.shape[1]
    enc_width = encodings.shape[2]
    span_dev = tok_dev // CH
    head_width = query_weight.shape[1]
    head_count = head_width // HS
    slot_cap = -(-rows_dev // ctx_count)
    tp_count = lax.axis_size("tp")
    tp_index = lax.axis_index("tp")
    whole = jnp.swapaxes(kernel_gather(hidden, "tp", "ctx", 0), 0, 1).reshape(hidden.shape[0], -1)
    rotation = ((tp_index - tp_count // 2) % tp_count) * hidden.shape[1]
    gain = lax.dynamic_slice_in_dim(jnp.concatenate([norm_gain, norm_gain]), rotation, whole.shape[1])
    values_wide = whole.astype(jnp.float32)
    mean_square = jnp.mean(values_wide * values_wide, axis=1, keepdims=True)
    normed = (values_wide * lax.rsqrt(mean_square + epsilon) * gain[None, :]).astype(
        jnp.bfloat16
    )
    query_full = lax.all_to_all(
        jnp.broadcast_to(query_weight[None], (ctx_count,) + query_weight.shape),
        "ctx",
        split_axis=0,
        concat_axis=0,
        tiled=True,
    ).reshape(-1, query_weight.shape[1])
    query_full = lax.dynamic_slice_in_dim(
        jnp.concatenate([query_full, query_full]), rotation, query_full.shape[0]
    )
    query_sum = jnp.dot(normed, query_full, preferred_element_type=jnp.float32)
    queries = (query_sum * HS ** (-0.5)).astype(jnp.bfloat16)
    storage = row_place[neighbour_ids.reshape(-1)].reshape(ctx_count, rows_dev)
    sources = storage // rows_dev
    local_rows = storage % rows_dev
    from_here = sources == ctx_index
    rank_position = jnp.cumsum(from_here.astype(jnp.int32), axis=1) - 1
    picked_rows = from_here & (rank_position == 0)
    pick_list = [jnp.sum(jnp.where(picked_rows, local_rows, 0), axis=1)]
    fill_list = [jnp.any(picked_rows, axis=1)]
    pick_index = jnp.stack(pick_list, axis=1)
    fill_mask = jnp.stack(fill_list, axis=1)
    outgoing = encodings[pick_index] * fill_mask[:, :, None, None].astype(jnp.bfloat16)
    incoming = lax.all_to_all(outgoing, "ctx", split_axis=0, concat_axis=0, tiled=True)
    own_sources = lax.dynamic_index_in_dim(sources, ctx_index, 0, keepdims=False)
    slot_order = jnp.arange(rows_dev)
    earlier = (own_sources[:, None] == own_sources[None, :]) & (
        slot_order[None, :] < slot_order[:, None]
    )
    own_rank = jnp.sum(earlier.astype(jnp.int32), axis=1)
    flat_index = own_sources * slot_cap + own_rank
    picked = incoming.reshape(ctx_count * slot_cap, slice_tokens, enc_width)[flat_index]
    row_total = picked.shape[0]
    full_rows = jnp.swapaxes(kernel_gather(picked, "tp", "ctx", 1), 0, 1).reshape(
        picked.shape[0], -1, picked.shape[2]
    )
    keys = project_rows(full_rows, key_weight).reshape(row_total, -1, head_width)
    values = project_rows(full_rows, value_weight).reshape(row_total, -1, head_width)
    neighbour_len = keys.shape[1]
    prior_keys, prior_values = shifted(
        (keys[row_total - KNB :], values[row_total - KNB :]), "ctx", 1
    )
    key_stack = jnp.concatenate([prior_keys, keys], axis=0)
    value_stack = jnp.concatenate([prior_values, values], axis=0)
    key_blocks = key_stack.reshape(span_dev + 1, KNB * neighbour_len, head_count, HS)
    value_blocks = value_stack.reshape(span_dev + 1, KNB * neighbour_len, head_count, HS)
    first_span = ctx_index * span_dev
    local_counts = lax.dynamic_slice_in_dim(neighbour_counts, first_span, span_dev)
    prior_count = lax.dynamic_slice_in_dim(neighbour_counts, jnp.maximum(first_span - 1, 0), 1)
    block_counts = jnp.concatenate([prior_count, local_counts], axis=0)
    padded = jnp.concatenate(
        [
            jnp.zeros((1, head_width), jnp.bfloat16),
            queries,
            jnp.zeros((CH - 1, head_width), jnp.bfloat16),
        ],
        axis=0,
    )
    query_blocks = padded.reshape(span_dev + 1, CH, head_count, HS)
    scores = jnp.einsum(
        "wqhd,wkhd->whqk", query_blocks, key_blocks, preferred_element_type=jnp.float32
    )
    slot_of_key = jnp.arange(KNB * neighbour_len) // neighbour_len
    live = slot_of_key[None, :] < block_counts[:, None]
    scores = jnp.where(live[:, None, None, :], scores, masked_score)
    peak = jnp.max(scores, axis=3, keepdims=True)
    expos = jnp.exp(scores - peak)
    total = jnp.sum(expos, axis=3)
    weights = expos.astype(jnp.bfloat16)
    blended = jnp.einsum(
        "whqk,wkhd->wqhd", weights, value_blocks, preferred_element_type=jnp.float32
    )
    blended = blended / jnp.swapaxes(total, 1, 2)[:, :, :, None]
    blended = blended.reshape((span_dev + 1) * CH, head_width)[1 : tok_dev + 1]
    position = ctx_index * tok_dev + jnp.arange(tok_dev)
    valid = position % LENGTH >= CH - 1
    attended = jnp.where(valid[:, None], blended, jnp.zeros_like(blended)).astype(jnp.bfloat16)
    return lax.psum_scatter(
        jnp.dot(attended, out_weight, preferred_element_type=jnp.float32).astype(jnp.bfloat16),
        "tp",
        scatter_dimension=0,
        tiled=True,
    )


def solution(mesh):
    return jax.shard_map(
        local,
        mesh=mesh,
        in_specs=(
            P("ctx", "tp"),
            P(),
            P("ctx", "tp"),
            P(None, "tp"),
            P(None, "tp"),
            P("tp", None),
            P("ctx", "tp", None),
            P(),
            P(),
            P(),
        ),
        out_specs=P(("ctx", "tp"), None),
        check_vma=False,
    )
```

```python
import functools

import jax
import jax.numpy as jnp
from jax import lax
from jax.experimental import pallas as pl
from jax.experimental.pallas import tpu as pltpu
from jax.sharding import PartitionSpec as P

HS = 128
CH = 64
KNB = 2
LENGTH = 8192


epsilon = 1e-05
masked_score = -1e30


def shifted(block, axis, distance):
    devices = range(lax.axis_size(axis))
    route = [(i - distance, i) for i in devices if i - distance in devices]
    return lax.ppermute(block, axis, route)


def ring_gather_kernel(x_ref, o_ref, send_sem, recv_sem, *, count, axis, other):
    me = lax.axis_index(axis)
    row = lax.axis_index(other)
    right = lax.rem(me + 1, count)
    left = lax.rem(me + count - 1, count)
    half = count // 2
    mesh_ids = pl.DeviceIdType.MESH
    barrier = pltpu.get_barrier_semaphore()
    for neighbour in (left, right):
        pl.semaphore_signal(barrier, inc=1, device_id=(row, neighbour), device_id_type=mesh_ids)
    pl.semaphore_wait(barrier, 2)
    o_ref[half] = x_ref[...]
    for step in range(1, half + 1):
        copies = []
        slot = half - step
        copies.append(
            pltpu.make_async_remote_copy(
                src_ref=x_ref if step == 1 else o_ref.at[slot + 1],
                dst_ref=o_ref.at[slot],
                send_sem=send_sem.at[slot],
                recv_sem=recv_sem.at[slot],
                device_id=(row, right),
                device_id_type=mesh_ids,
            )
        )
        if step < count - half:
            slot = half + step
            copies.append(
                pltpu.make_async_remote_copy(
                    src_ref=x_ref if step == 1 else o_ref.at[slot - 1],
                    dst_ref=o_ref.at[slot],
                    send_sem=send_sem.at[slot],
                    recv_sem=recv_sem.at[slot],
                    device_id=(row, left),
                    device_id_type=mesh_ids,
                )
            )
        for copy in copies:
            copy.start()
        for copy in copies:
            copy.wait_recv()
        for copy in copies:
            copy.wait_send()


def kernel_gather(block, axis, other, collective_id):
    count = lax.axis_size(axis)
    return pl.pallas_call(
        functools.partial(ring_gather_kernel, count=count, axis=axis, other=other),
        out_shape=jax.ShapeDtypeStruct((count,) + block.shape, block.dtype),
        in_specs=[pl.BlockSpec(memory_space=pltpu.VMEM)],
        out_specs=pl.BlockSpec(memory_space=pltpu.VMEM),
        scratch_shapes=[pltpu.SemaphoreType.DMA((count,)), pltpu.SemaphoreType.DMA((count,))],
        compiler_params=pltpu.CompilerParams(collective_id=collective_id, has_side_effects=True),
    )(block)


def project_rows(rows, weight):
    flat = rows.reshape(-1, rows.shape[-1])
    return jnp.dot(flat, weight, preferred_element_type=jnp.float32).astype(jnp.bfloat16)


def local(
    hidden,
    norm_gain,
    query_weight,
    key_weight,
    value_weight,
    out_weight,
    encodings,
    row_place,
    neighbour_ids,
    neighbour_counts,
):
    ctx_count = lax.axis_size("ctx")
    ctx_index = lax.axis_index("ctx")
    tok_dev = hidden.shape[0]
    rows_dev = encodings.shape[0]
    slice_tokens = encodings.shape[1]
    enc_width = encodings.shape[2]
    span_dev = tok_dev // CH
    head_width = query_weight.shape[1]
    head_count = head_width // HS
    slot_cap = -(-rows_dev // ctx_count)
    whole = lax.all_gather(hidden, "tp", axis=1, tiled=True)
    values_wide = whole.astype(jnp.float32)
    mean_square = jnp.mean(values_wide * values_wide, axis=1, keepdims=True)
    normed = (values_wide * lax.rsqrt(mean_square + epsilon) * norm_gain[None, :]).astype(
        jnp.bfloat16
    )
    query_full = lax.all_to_all(
        jnp.broadcast_to(query_weight[None], (ctx_count,) + query_weight.shape),
        "ctx",
        split_axis=0,
        concat_axis=0,
        tiled=True,
    ).reshape(-1, query_weight.shape[1])
    query_sum = jnp.dot(normed, query_full, preferred_element_type=jnp.float32)
    queries = (query_sum * HS ** (-0.5)).astype(jnp.bfloat16)
    storage = row_place[neighbour_ids.reshape(-1)].reshape(ctx_count, rows_dev)
    sources = storage // rows_dev
    local_rows = storage % rows_dev
    from_here = sources == ctx_index
    rank_position = jnp.cumsum(from_here.astype(jnp.int32), axis=1) - 1
    picked_rows = from_here & (rank_position == 0)
    pick_list = [jnp.sum(jnp.where(picked_rows, local_rows, 0), axis=1)]
    fill_list = [jnp.any(picked_rows, axis=1)]
    pick_index = jnp.stack(pick_list, axis=1)
    fill_mask = jnp.stack(fill_list, axis=1)
    outgoing = encodings[pick_index] * fill_mask[:, :, None, None].astype(jnp.bfloat16)
    incoming = lax.all_to_all(outgoing, "ctx", split_axis=0, concat_axis=0, tiled=True)
    own_sources = lax.dynamic_index_in_dim(sources, ctx_index, 0, keepdims=False)
    slot_order = jnp.arange(rows_dev)
    earlier = (own_sources[:, None] == own_sources[None, :]) & (
        slot_order[None, :] < slot_order[:, None]
    )
    own_rank = jnp.sum(earlier.astype(jnp.int32), axis=1)
    flat_index = own_sources * slot_cap + own_rank
    picked = incoming.reshape(ctx_count * slot_cap, slice_tokens, enc_width)[flat_index]
    row_total = picked.shape[0]
    full_rows = jnp.swapaxes(kernel_gather(picked, "tp", "ctx", 0), 0, 1).reshape(
        picked.shape[0], -1, picked.shape[2]
    )
    keys = project_rows(full_rows, key_weight).reshape(row_total, -1, head_width)
    values = project_rows(full_rows, value_weight).reshape(row_total, -1, head_width)
    neighbour_len = keys.shape[1]
    prior_keys, prior_values = shifted(
        (keys[row_total - KNB :], values[row_total - KNB :]), "ctx", 1
    )
    key_stack = jnp.concatenate([prior_keys, keys], axis=0)
    value_stack = jnp.concatenate([prior_values, values], axis=0)
    key_blocks = key_stack.reshape(span_dev + 1, KNB * neighbour_len, head_count, HS)
    value_blocks = value_stack.reshape(span_dev + 1, KNB * neighbour_len, head_count, HS)
    first_span = ctx_index * span_dev
    local_counts = lax.dynamic_slice_in_dim(neighbour_counts, first_span, span_dev)
    prior_count = lax.dynamic_slice_in_dim(neighbour_counts, jnp.maximum(first_span - 1, 0), 1)
    block_counts = jnp.concatenate([prior_count, local_counts], axis=0)
    padded = jnp.concatenate(
        [
            jnp.zeros((1, head_width), jnp.bfloat16),
            queries,
            jnp.zeros((CH - 1, head_width), jnp.bfloat16),
        ],
        axis=0,
    )
    query_blocks = padded.reshape(span_dev + 1, CH, head_count, HS)
    scores = jnp.einsum(
        "wqhd,wkhd->whqk", query_blocks, key_blocks, preferred_element_type=jnp.float32
    )
    slot_of_key = jnp.arange(KNB * neighbour_len) // neighbour_len
    live = slot_of_key[None, :] < block_counts[:, None]
    scores = jnp.where(live[:, None, None, :], scores, masked_score)
    peak = jnp.max(scores, axis=3, keepdims=True)
    expos = jnp.exp(scores - peak)
    total = jnp.sum(expos, axis=3)
    weights = expos.astype(jnp.bfloat16)
    blended = jnp.einsum(
        "whqk,wkhd->wqhd", weights, value_blocks, preferred_element_type=jnp.float32
    )
    blended = blended / jnp.swapaxes(total, 1, 2)[:, :, :, None]
    blended = blended.reshape((span_dev + 1) * CH, head_width)[1 : tok_dev + 1]
    position = ctx_index * tok_dev + jnp.arange(tok_dev)
    valid = position % LENGTH >= CH - 1
    attended = jnp.where(valid[:, None], blended, jnp.zeros_like(blended)).astype(jnp.bfloat16)
    return lax.psum_scatter(
        jnp.dot(attended, out_weight, preferred_element_type=jnp.float32).astype(jnp.bfloat16),
        "tp",
        scatter_dimension=0,
        tiled=True,
    )


def solution(mesh):
    return jax.shard_map(
        local,
        mesh=mesh,
        in_specs=(
            P("ctx", "tp"),
            P(),
            P("ctx", "tp"),
            P(None, "tp"),
            P(None, "tp"),
            P("tp", None),
            P("ctx", "tp", None),
            P(),
            P(),
            P(),
        ),
        out_specs=P(("ctx", "tp"), None),
        check_vma=False,
    )
```

```python
import functools

import jax
import jax.numpy as jnp
from jax import lax
from jax.experimental import pallas as pl
from jax.experimental.pallas import tpu as pltpu
from jax.sharding import PartitionSpec as P

HS = 128
CH = 64
KNB = 2
LENGTH = 8192


epsilon = 1e-05
masked_score = -1e30


def shifted(block, axis, distance):
    devices = range(lax.axis_size(axis))
    route = [(i - distance, i) for i in devices if i - distance in devices]
    return lax.ppermute(block, axis, route)


def ring_gather_kernel(x_ref, o_ref, send_sem, recv_sem, *, count, axis, other):
    me = lax.axis_index(axis)
    row = lax.axis_index(other)
    right = lax.rem(me + 1, count)
    left = lax.rem(me + count - 1, count)
    half = count // 2
    mesh_ids = pl.DeviceIdType.MESH
    barrier = pltpu.get_barrier_semaphore()
    for neighbour in (left, right):
        pl.semaphore_signal(barrier, inc=1, device_id=(row, neighbour), device_id_type=mesh_ids)
    pl.semaphore_wait(barrier, 2)
    o_ref[half] = x_ref[...]
    for step in range(1, half + 1):
        copies = []
        slot = half - step
        copies.append(
            pltpu.make_async_remote_copy(
                src_ref=x_ref if step == 1 else o_ref.at[slot + 1],
                dst_ref=o_ref.at[slot],
                send_sem=send_sem.at[slot],
                recv_sem=recv_sem.at[slot],
                device_id=(row, right),
                device_id_type=mesh_ids,
            )
        )
        if step < count - half:
            slot = half + step
            copies.append(
                pltpu.make_async_remote_copy(
                    src_ref=x_ref if step == 1 else o_ref.at[slot - 1],
                    dst_ref=o_ref.at[slot],
                    send_sem=send_sem.at[slot],
                    recv_sem=recv_sem.at[slot],
                    device_id=(row, left),
                    device_id_type=mesh_ids,
                )
            )
        for copy in copies:
            copy.start()
        for copy in copies:
            copy.wait_recv()
        for copy in copies:
            copy.wait_send()


def kernel_gather(block, axis, other, collective_id):
    count = lax.axis_size(axis)
    return pl.pallas_call(
        functools.partial(ring_gather_kernel, count=count, axis=axis, other=other),
        out_shape=jax.ShapeDtypeStruct((count,) + block.shape, block.dtype),
        in_specs=[pl.BlockSpec(memory_space=pltpu.VMEM)],
        out_specs=pl.BlockSpec(memory_space=pltpu.VMEM),
        scratch_shapes=[pltpu.SemaphoreType.DMA((count,)), pltpu.SemaphoreType.DMA((count,))],
        compiler_params=pltpu.CompilerParams(collective_id=collective_id, has_side_effects=True),
    )(block)


def ring_sum_kernel(
    p_ref, o_ref, right_in, right_out, left_in, left_out, sems, *, count, axis, other
):
    me = lax.axis_index(axis)
    row = lax.axis_index(other)
    right = lax.rem(me + 1, count)
    left = lax.rem(me + count - 1, count)
    reach_right = count // 2
    reach_left = count - 1 - reach_right
    mesh_ids = pl.DeviceIdType.MESH
    barrier = pltpu.get_barrier_semaphore()
    for neighbour in (left, right):
        pl.semaphore_signal(barrier, inc=1, device_id=(row, neighbour), device_id_type=mesh_ids)
    pl.semaphore_wait(barrier, 2)

    def own(offset):
        return p_ref[lax.rem(me + offset + 2 * count, count)].astype(jnp.float32)

    for step in range(1, reach_right + 1):
        copies = [
            pltpu.make_async_remote_copy(
                src_ref=p_ref.at[lax.rem(me + reach_right, count)]
                if step == 1
                else right_out.at[step - 2],
                dst_ref=right_in.at[step - 1],
                send_sem=sems.at[0, step - 1],
                recv_sem=sems.at[1, step - 1],
                device_id=(row, right),
                device_id_type=mesh_ids,
            )
        ]
        if step <= reach_left:
            copies.append(
                pltpu.make_async_remote_copy(
                    src_ref=p_ref.at[lax.rem(me + count - reach_left, count)]
                    if step == 1
                    else left_out.at[step - 2],
                    dst_ref=left_in.at[step - 1],
                    send_sem=sems.at[2, step - 1],
                    recv_sem=sems.at[3, step - 1],
                    device_id=(row, left),
                    device_id_type=mesh_ids,
                )
            )
        for copy in copies:
            copy.start()
        for copy in copies:
            copy.wait_recv()
        for copy in copies:
            copy.wait_send()
        if step < reach_right:
            right_out[step - 1] = (
                right_in[step - 1].astype(jnp.float32) + own(reach_right - step)
            ).astype(right_out.dtype)
        if step < reach_left:
            left_out[step - 1] = (
                left_in[step - 1].astype(jnp.float32) + own(step - reach_left)
            ).astype(left_out.dtype)
    total = own(0) + right_in[reach_right - 1].astype(jnp.float32)
    total = total + left_in[reach_left - 1].astype(jnp.float32)
    o_ref[...] = total.astype(o_ref.dtype)


def kernel_reduce_scatter(partial, axis, other, collective_id):
    count = lax.axis_size(axis)
    blocks = partial.reshape((count, partial.shape[0] // count) + partial.shape[1:])
    block = blocks.shape[1:]
    reach_right = count // 2
    reach_left = count - 1 - reach_right
    return pl.pallas_call(
        functools.partial(ring_sum_kernel, count=count, axis=axis, other=other),
        out_shape=jax.ShapeDtypeStruct(block, partial.dtype),
        in_specs=[pl.BlockSpec(memory_space=pltpu.VMEM)],
        out_specs=pl.BlockSpec(memory_space=pltpu.VMEM),
        scratch_shapes=[
            pltpu.VMEM((reach_right,) + block, partial.dtype),
            pltpu.VMEM((reach_right,) + block, partial.dtype),
            pltpu.VMEM((reach_left,) + block, partial.dtype),
            pltpu.VMEM((reach_left,) + block, partial.dtype),
            pltpu.SemaphoreType.DMA((4, reach_right)),
        ],
        compiler_params=pltpu.CompilerParams(collective_id=collective_id, has_side_effects=True),
    )(blocks)


def project_rows(rows, weight):
    flat = rows.reshape(-1, rows.shape[-1])
    return jnp.dot(flat, weight, preferred_element_type=jnp.float32).astype(jnp.bfloat16)


def local(
    hidden,
    norm_gain,
    query_weight,
    key_weight,
    value_weight,
    out_weight,
    encodings,
    row_place,
    neighbour_ids,
    neighbour_counts,
):
    ctx_count = lax.axis_size("ctx")
    ctx_index = lax.axis_index("ctx")
    tok_dev = hidden.shape[0]
    rows_dev = encodings.shape[0]
    slice_tokens = encodings.shape[1]
    enc_width = encodings.shape[2]
    span_dev = tok_dev // CH
    head_width = query_weight.shape[1]
    head_count = head_width // HS
    slot_cap = -(-rows_dev // ctx_count)
    whole = lax.all_gather(hidden, "tp", axis=1, tiled=True)
    values_wide = whole.astype(jnp.float32)
    mean_square = jnp.mean(values_wide * values_wide, axis=1, keepdims=True)
    normed = (values_wide * lax.rsqrt(mean_square + epsilon) * norm_gain[None, :]).astype(
        jnp.bfloat16
    )
    query_full = lax.all_to_all(
        jnp.broadcast_to(query_weight[None], (ctx_count,) + query_weight.shape),
        "ctx",
        split_axis=0,
        concat_axis=0,
        tiled=True,
    ).reshape(-1, query_weight.shape[1])
    query_sum = jnp.dot(normed, query_full, preferred_element_type=jnp.float32)
    queries = (query_sum * HS ** (-0.5)).astype(jnp.bfloat16)
    storage = row_place[neighbour_ids.reshape(-1)].reshape(ctx_count, rows_dev)
    sources = storage // rows_dev
    local_rows = storage % rows_dev
    from_here = sources == ctx_index
    rank_position = jnp.cumsum(from_here.astype(jnp.int32), axis=1) - 1
    picked_rows = from_here & (rank_position == 0)
    pick_list = [jnp.sum(jnp.where(picked_rows, local_rows, 0), axis=1)]
    fill_list = [jnp.any(picked_rows, axis=1)]
    pick_index = jnp.stack(pick_list, axis=1)
    fill_mask = jnp.stack(fill_list, axis=1)
    outgoing = encodings[pick_index] * fill_mask[:, :, None, None].astype(jnp.bfloat16)
    incoming = lax.all_to_all(outgoing, "ctx", split_axis=0, concat_axis=0, tiled=True)
    own_sources = lax.dynamic_index_in_dim(sources, ctx_index, 0, keepdims=False)
    slot_order = jnp.arange(rows_dev)
    earlier = (own_sources[:, None] == own_sources[None, :]) & (
        slot_order[None, :] < slot_order[:, None]
    )
    own_rank = jnp.sum(earlier.astype(jnp.int32), axis=1)
    flat_index = own_sources * slot_cap + own_rank
    picked = incoming.reshape(ctx_count * slot_cap, slice_tokens, enc_width)[flat_index]
    row_total = picked.shape[0]
    full_rows = jnp.swapaxes(kernel_gather(picked, "tp", "ctx", 0), 0, 1).reshape(
        picked.shape[0], -1, picked.shape[2]
    )
    keys = project_rows(full_rows, key_weight).reshape(row_total, -1, head_width)
    values = project_rows(full_rows, value_weight).reshape(row_total, -1, head_width)
    neighbour_len = keys.shape[1]
    prior_keys, prior_values = shifted(
        (keys[row_total - KNB :], values[row_total - KNB :]), "ctx", 1
    )
    key_stack = jnp.concatenate([prior_keys, keys], axis=0)
    value_stack = jnp.concatenate([prior_values, values], axis=0)
    key_blocks = key_stack.reshape(span_dev + 1, KNB * neighbour_len, head_count, HS)
    value_blocks = value_stack.reshape(span_dev + 1, KNB * neighbour_len, head_count, HS)
    first_span = ctx_index * span_dev
    local_counts = lax.dynamic_slice_in_dim(neighbour_counts, first_span, span_dev)
    prior_count = lax.dynamic_slice_in_dim(neighbour_counts, jnp.maximum(first_span - 1, 0), 1)
    block_counts = jnp.concatenate([prior_count, local_counts], axis=0)
    padded = jnp.concatenate(
        [
            jnp.zeros((1, head_width), jnp.bfloat16),
            queries,
            jnp.zeros((CH - 1, head_width), jnp.bfloat16),
        ],
        axis=0,
    )
    query_blocks = padded.reshape(span_dev + 1, CH, head_count, HS)
    scores = jnp.einsum(
        "wqhd,wkhd->whqk", query_blocks, key_blocks, preferred_element_type=jnp.float32
    )
    slot_of_key = jnp.arange(KNB * neighbour_len) // neighbour_len
    live = slot_of_key[None, :] < block_counts[:, None]
    scores = jnp.where(live[:, None, None, :], scores, masked_score)
    peak = jnp.max(scores, axis=3, keepdims=True)
    expos = jnp.exp(scores - peak)
    total = jnp.sum(expos, axis=3)
    weights = expos.astype(jnp.bfloat16)
    blended = jnp.einsum(
        "whqk,wkhd->wqhd", weights, value_blocks, preferred_element_type=jnp.float32
    )
    blended = blended / jnp.swapaxes(total, 1, 2)[:, :, :, None]
    blended = blended.reshape((span_dev + 1) * CH, head_width)[1 : tok_dev + 1]
    position = ctx_index * tok_dev + jnp.arange(tok_dev)
    valid = position % LENGTH >= CH - 1
    attended = jnp.where(valid[:, None], blended, jnp.zeros_like(blended)).astype(jnp.bfloat16)
    mixed_part = jnp.dot(attended, out_weight, preferred_element_type=jnp.float32).astype(
        jnp.bfloat16
    )
    split = mixed_part.shape[1] // 2
    return jnp.concatenate(
        [
            lax.psum_scatter(mixed_part[:, :split], "tp", scatter_dimension=0, tiled=True),
            kernel_reduce_scatter(mixed_part[:, split:], "tp", "ctx", 1),
        ],
        axis=1,
    )


def solution(mesh):
    return jax.shard_map(
        local,
        mesh=mesh,
        in_specs=(
            P("ctx", "tp"),
            P(),
            P("ctx", "tp"),
            P(None, "tp"),
            P(None, "tp"),
            P("tp", None),
            P("ctx", "tp", None),
            P(),
            P(),
            P(),
        ),
        out_specs=P(("ctx", "tp"), None),
        check_vma=False,
    )
```

```python
import functools

import jax
import jax.numpy as jnp
from jax import lax
from jax.experimental import pallas as pl
from jax.experimental.pallas import tpu as pltpu
from jax.sharding import PartitionSpec as P

HS = 128
CH = 64
KNB = 2
LENGTH = 8192


epsilon = 1e-05
masked_score = -1e30


def shifted(block, axis, distance):
    devices = range(lax.axis_size(axis))
    route = [(i - distance, i) for i in devices if i - distance in devices]
    return lax.ppermute(block, axis, route)


def greet_neighbours(me, row, count):
    right = lax.rem(me + 1, count)
    left = lax.rem(me + count - 1, count)
    barrier = pltpu.get_barrier_semaphore()
    for neighbour in (left, right):
        pl.semaphore_signal(
            barrier, inc=1, device_id=(row, neighbour), device_id_type=pl.DeviceIdType.MESH
        )
    pl.semaphore_wait(barrier, 2)
    return right, left


def ring_gather_kernel(x_ref, o_ref, send_sem, recv_sem, *, count, axis, other, pieces):
    me = lax.axis_index(axis)
    row = lax.axis_index(other)
    right, left = greet_neighbours(me, row, count)
    half = count // 2
    size = x_ref.shape[0] // pieces
    o_ref[half] = x_ref[...]
    copies = {}
    for step in range(1, half + 1):
        for piece in range(pieces):
            part = pl.ds(piece * size, size)
            for toward in (0, 1):
                if toward == 1 and step > count - 1 - half:
                    continue
                slot = half - step if toward == 0 else half + step
                source = slot + 1 if toward == 0 else slot - 1
                if step > 1:
                    copies[(step - 1, toward, piece)].wait_recv()
                copy = pltpu.make_async_remote_copy(
                    src_ref=x_ref.at[part] if step == 1 else o_ref.at[source, part],
                    dst_ref=o_ref.at[slot, part],
                    send_sem=send_sem.at[slot, piece],
                    recv_sem=recv_sem.at[slot, piece],
                    device_id=(row, right if toward == 0 else left),
                    device_id_type=pl.DeviceIdType.MESH,
                )
                copy.start()
                copies[(step, toward, piece)] = copy
    for piece in range(pieces):
        copies[(half, 0, piece)].wait_recv()
        copies[(count - 1 - half, 1, piece)].wait_recv()
    for copy in copies.values():
        copy.wait_send()


def kernel_gather(block, axis, other, collective_id, pieces=4):
    count = lax.axis_size(axis)
    return pl.pallas_call(
        functools.partial(
            ring_gather_kernel, count=count, axis=axis, other=other, pieces=pieces
        ),
        out_shape=jax.ShapeDtypeStruct((count,) + block.shape, block.dtype),
        in_specs=[pl.BlockSpec(memory_space=pltpu.VMEM)],
        out_specs=pl.BlockSpec(memory_space=pltpu.VMEM),
        scratch_shapes=[
            pltpu.SemaphoreType.DMA((count, pieces)),
            pltpu.SemaphoreType.DMA((count, pieces)),
        ],
        compiler_params=pltpu.CompilerParams(collective_id=collective_id, has_side_effects=True),
    )(block)


def ring_sum_kernel(p_ref, o_ref, sums_in, sums_out, sems, *, count, axis, other, pieces):
    me = lax.axis_index(axis)
    row = lax.axis_index(other)
    right, left = greet_neighbours(me, row, count)
    reach = (count // 2, count - 1 - count // 2)
    width = p_ref.shape[2] // pieces

    def own(offset, part):
        return p_ref[lax.rem(me + offset + 2 * count, count), :, part].astype(jnp.float32)

    copies = {}
    for step in range(1, reach[0] + 1):
        for piece in range(pieces):
            part = pl.ds(piece * width, width)
            for toward in (0, 1):
                if step > reach[toward]:
                    continue
                if step == 1:
                    first = reach[0] if toward == 0 else count - reach[1]
                    source = p_ref.at[lax.rem(me + first, count), :, part]
                else:
                    copies[(step - 1, toward, piece)].wait_recv()
                    offset = reach[0] - step + 1 if toward == 0 else step - 1 - reach[1]
                    sums_out[toward, step - 2, :, part] = (
                        sums_in[toward, step - 2, :, part].astype(jnp.float32) + own(offset, part)
                    ).astype(sums_out.dtype)
                    source = sums_out.at[toward, step - 2, :, part]
                copy = pltpu.make_async_remote_copy(
                    src_ref=source,
                    dst_ref=sums_in.at[toward, step - 1, :, part],
                    send_sem=sems.at[0, toward, step - 1, piece],
                    recv_sem=sems.at[1, toward, step - 1, piece],
                    device_id=(row, right if toward == 0 else left),
                    device_id_type=pl.DeviceIdType.MESH,
                )
                copy.start()
                copies[(step, toward, piece)] = copy
    for piece in range(pieces):
        copies[(reach[0], 0, piece)].wait_recv()
        copies[(reach[1], 1, piece)].wait_recv()
    for copy in copies.values():
        copy.wait_send()
    total = p_ref[me].astype(jnp.float32) + sums_in[0, reach[0] - 1].astype(jnp.float32)
    total = total + sums_in[1, reach[1] - 1].astype(jnp.float32)
    o_ref[...] = total.astype(o_ref.dtype)


def kernel_reduce_scatter(partial, axis, other, collective_id, pieces=4):
    count = lax.axis_size(axis)
    blocks = partial.reshape((count, partial.shape[0] // count) + partial.shape[1:])
    block = blocks.shape[1:]
    reach = count // 2
    return pl.pallas_call(
        functools.partial(
            ring_sum_kernel, count=count, axis=axis, other=other, pieces=pieces
        ),
        out_shape=jax.ShapeDtypeStruct(block, partial.dtype),
        in_specs=[pl.BlockSpec(memory_space=pltpu.VMEM)],
        out_specs=pl.BlockSpec(memory_space=pltpu.VMEM),
        scratch_shapes=[
            pltpu.VMEM((2, reach) + block, partial.dtype),
            pltpu.VMEM((2, reach) + block, partial.dtype),
            pltpu.SemaphoreType.DMA((2, 2, reach, pieces)),
        ],
        compiler_params=pltpu.CompilerParams(collective_id=collective_id, has_side_effects=True),
    )(blocks)


def project_rows(rows, weight):
    flat = rows.reshape(-1, rows.shape[-1])
    return jnp.dot(flat, weight, preferred_element_type=jnp.float32).astype(jnp.bfloat16)


def local(
    hidden,
    norm_gain,
    query_weight,
    key_weight,
    value_weight,
    out_weight,
    encodings,
    row_place,
    neighbour_ids,
    neighbour_counts,
):
    ctx_count = lax.axis_size("ctx")
    ctx_index = lax.axis_index("ctx")
    tok_dev = hidden.shape[0]
    rows_dev = encodings.shape[0]
    slice_tokens = encodings.shape[1]
    enc_width = encodings.shape[2]
    span_dev = tok_dev // CH
    head_width = query_weight.shape[1]
    head_count = head_width // HS
    slot_cap = -(-rows_dev // ctx_count)
    whole = lax.all_gather(hidden, "tp", axis=1, tiled=True)
    values_wide = whole.astype(jnp.float32)
    mean_square = jnp.mean(values_wide * values_wide, axis=1, keepdims=True)
    normed = (values_wide * lax.rsqrt(mean_square + epsilon) * norm_gain[None, :]).astype(
        jnp.bfloat16
    )
    query_full = lax.all_to_all(
        jnp.broadcast_to(query_weight[None], (ctx_count,) + query_weight.shape),
        "ctx",
        split_axis=0,
        concat_axis=0,
        tiled=True,
    ).reshape(-1, query_weight.shape[1])
    query_sum = jnp.dot(normed, query_full, preferred_element_type=jnp.float32)
    queries = (query_sum * HS ** (-0.5)).astype(jnp.bfloat16)
    storage = row_place[neighbour_ids.reshape(-1)].reshape(ctx_count, rows_dev)
    sources = storage // rows_dev
    local_rows = storage % rows_dev
    from_here = sources == ctx_index
    rank_position = jnp.cumsum(from_here.astype(jnp.int32), axis=1) - 1
    picked_rows = from_here & (rank_position == 0)
    pick_list = [jnp.sum(jnp.where(picked_rows, local_rows, 0), axis=1)]
    fill_list = [jnp.any(picked_rows, axis=1)]
    pick_index = jnp.stack(pick_list, axis=1)
    fill_mask = jnp.stack(fill_list, axis=1)
    outgoing = encodings[pick_index] * fill_mask[:, :, None, None].astype(jnp.bfloat16)
    incoming = lax.all_to_all(outgoing, "ctx", split_axis=0, concat_axis=0, tiled=True)
    own_sources = lax.dynamic_index_in_dim(sources, ctx_index, 0, keepdims=False)
    slot_order = jnp.arange(rows_dev)
    earlier = (own_sources[:, None] == own_sources[None, :]) & (
        slot_order[None, :] < slot_order[:, None]
    )
    own_rank = jnp.sum(earlier.astype(jnp.int32), axis=1)
    flat_index = own_sources * slot_cap + own_rank
    picked = incoming.reshape(ctx_count * slot_cap, slice_tokens, enc_width)[flat_index]
    row_total = picked.shape[0]
    full_rows = jnp.swapaxes(kernel_gather(picked, "tp", "ctx", 0), 0, 1).reshape(
        picked.shape[0], -1, picked.shape[2]
    )
    keys = project_rows(full_rows, key_weight).reshape(row_total, -1, head_width)
    values = project_rows(full_rows, value_weight).reshape(row_total, -1, head_width)
    neighbour_len = keys.shape[1]
    prior_keys, prior_values = shifted(
        (keys[row_total - KNB :], values[row_total - KNB :]), "ctx", 1
    )
    key_stack = jnp.concatenate([prior_keys, keys], axis=0)
    value_stack = jnp.concatenate([prior_values, values], axis=0)
    key_blocks = key_stack.reshape(span_dev + 1, KNB * neighbour_len, head_count, HS)
    value_blocks = value_stack.reshape(span_dev + 1, KNB * neighbour_len, head_count, HS)
    first_span = ctx_index * span_dev
    local_counts = lax.dynamic_slice_in_dim(neighbour_counts, first_span, span_dev)
    prior_count = lax.dynamic_slice_in_dim(neighbour_counts, jnp.maximum(first_span - 1, 0), 1)
    block_counts = jnp.concatenate([prior_count, local_counts], axis=0)
    padded = jnp.concatenate(
        [
            jnp.zeros((1, head_width), jnp.bfloat16),
            queries,
            jnp.zeros((CH - 1, head_width), jnp.bfloat16),
        ],
        axis=0,
    )
    query_blocks = padded.reshape(span_dev + 1, CH, head_count, HS)
    scores = jnp.einsum(
        "wqhd,wkhd->whqk", query_blocks, key_blocks, preferred_element_type=jnp.float32
    )
    slot_of_key = jnp.arange(KNB * neighbour_len) // neighbour_len
    live = slot_of_key[None, :] < block_counts[:, None]
    scores = jnp.where(live[:, None, None, :], scores, masked_score)
    peak = jnp.max(scores, axis=3, keepdims=True)
    expos = jnp.exp(scores - peak)
    total = jnp.sum(expos, axis=3)
    weights = expos.astype(jnp.bfloat16)
    blended = jnp.einsum(
        "whqk,wkhd->wqhd", weights, value_blocks, preferred_element_type=jnp.float32
    )
    blended = blended / jnp.swapaxes(total, 1, 2)[:, :, :, None]
    blended = blended.reshape((span_dev + 1) * CH, head_width)[1 : tok_dev + 1]
    position = ctx_index * tok_dev + jnp.arange(tok_dev)
    valid = position % LENGTH >= CH - 1
    attended = jnp.where(valid[:, None], blended, jnp.zeros_like(blended)).astype(jnp.bfloat16)
    mixed_part = jnp.dot(attended, out_weight, preferred_element_type=jnp.float32).astype(
        jnp.bfloat16
    )
    split = mixed_part.shape[1] // 2
    return jnp.concatenate(
        [
            lax.psum_scatter(mixed_part[:, :split], "tp", scatter_dimension=0, tiled=True),
            kernel_reduce_scatter(mixed_part[:, split:], "tp", "ctx", 1),
        ],
        axis=1,
    )


def solution(mesh):
    return jax.shard_map(
        local,
        mesh=mesh,
        in_specs=(
            P("ctx", "tp"),
            P(),
            P("ctx", "tp"),
            P(None, "tp"),
            P(None, "tp"),
            P("tp", None),
            P("ctx", "tp", None),
            P(),
            P(),
            P(),
        ),
        out_specs=P(("ctx", "tp"), None),
        check_vma=False,
    )
```

```python
import functools

import jax
import jax.numpy as jnp
from jax import lax
from jax.experimental import pallas as pl
from jax.experimental.pallas import tpu as pltpu
from jax.sharding import PartitionSpec as P

HS = 128
CH = 64
KNB = 2
LENGTH = 8192


epsilon = 1e-05
masked_score = -1e30


def shifted(block, axis, distance):
    devices = range(lax.axis_size(axis))
    route = [(i - distance, i) for i in devices if i - distance in devices]
    return lax.ppermute(block, axis, route)


def greet_neighbours(me, row, count):
    right = lax.rem(me + 1, count)
    left = lax.rem(me + count - 1, count)
    barrier = pltpu.get_barrier_semaphore()
    for neighbour in (left, right):
        pl.semaphore_signal(
            barrier, inc=1, device_id=(row, neighbour), device_id_type=pl.DeviceIdType.MESH
        )
    pl.semaphore_wait(barrier, 2)
    return right, left


def ring_gather_kernel(x_ref, o_ref, send_sem, recv_sem, *, count, axis, other, pieces):
    me = lax.axis_index(axis)
    row = lax.axis_index(other)
    right, left = greet_neighbours(me, row, count)
    half = count // 2
    size = x_ref.shape[0] // pieces
    o_ref[half] = x_ref[...]
    copies = {}
    for step in range(1, half + 1):
        for piece in range(pieces):
            part = pl.ds(piece * size, size)
            for toward in (0, 1):
                if toward == 1 and step > count - 1 - half:
                    continue
                slot = half - step if toward == 0 else half + step
                source = slot + 1 if toward == 0 else slot - 1
                if step > 1:
                    copies[(step - 1, toward, piece)].wait_recv()
                copy = pltpu.make_async_remote_copy(
                    src_ref=x_ref.at[part] if step == 1 else o_ref.at[source, part],
                    dst_ref=o_ref.at[slot, part],
                    send_sem=send_sem.at[slot, piece],
                    recv_sem=recv_sem.at[slot, piece],
                    device_id=(row, right if toward == 0 else left),
                    device_id_type=pl.DeviceIdType.MESH,
                )
                copy.start()
                copies[(step, toward, piece)] = copy
    for piece in range(pieces):
        copies[(half, 0, piece)].wait_recv()
        copies[(count - 1 - half, 1, piece)].wait_recv()
    for copy in copies.values():
        copy.wait_send()


def kernel_gather(block, axis, other, collective_id, pieces=4):
    count = lax.axis_size(axis)
    return pl.pallas_call(
        functools.partial(
            ring_gather_kernel, count=count, axis=axis, other=other, pieces=pieces
        ),
        out_shape=jax.ShapeDtypeStruct((count,) + block.shape, block.dtype),
        in_specs=[pl.BlockSpec(memory_space=pltpu.VMEM)],
        out_specs=pl.BlockSpec(memory_space=pltpu.VMEM),
        scratch_shapes=[
            pltpu.SemaphoreType.DMA((count, pieces)),
            pltpu.SemaphoreType.DMA((count, pieces)),
        ],
        compiler_params=pltpu.CompilerParams(collective_id=collective_id, has_side_effects=True),
    )(block)


def ring_sum_kernel(p_ref, o_ref, sums_in, sums_out, sems, *, count, axis, other, pieces):
    me = lax.axis_index(axis)
    row = lax.axis_index(other)
    right, left = greet_neighbours(me, row, count)
    reach = (count // 2, count - 1 - count // 2)
    width = p_ref.shape[2] // pieces

    def own(offset, part):
        return p_ref[lax.rem(me + offset + 2 * count, count), :, part].astype(jnp.float32)

    copies = {}
    for step in range(1, reach[0] + 1):
        for piece in range(pieces):
            part = pl.ds(piece * width, width)
            for toward in (0, 1):
                if step > reach[toward]:
                    continue
                if step == 1:
                    first = reach[0] if toward == 0 else count - reach[1]
                    source = p_ref.at[lax.rem(me + first, count), :, part]
                else:
                    copies[(step - 1, toward, piece)].wait_recv()
                    offset = reach[0] - step + 1 if toward == 0 else step - 1 - reach[1]
                    sums_out[toward, step - 2, :, part] = (
                        sums_in[toward, step - 2, :, part].astype(jnp.float32) + own(offset, part)
                    ).astype(sums_out.dtype)
                    source = sums_out.at[toward, step - 2, :, part]
                copy = pltpu.make_async_remote_copy(
                    src_ref=source,
                    dst_ref=sums_in.at[toward, step - 1, :, part],
                    send_sem=sems.at[0, toward, step - 1, piece],
                    recv_sem=sems.at[1, toward, step - 1, piece],
                    device_id=(row, right if toward == 0 else left),
                    device_id_type=pl.DeviceIdType.MESH,
                )
                copy.start()
                copies[(step, toward, piece)] = copy
    for piece in range(pieces):
        copies[(reach[0], 0, piece)].wait_recv()
        copies[(reach[1], 1, piece)].wait_recv()
    for copy in copies.values():
        copy.wait_send()
    total = p_ref[me].astype(jnp.float32) + sums_in[0, reach[0] - 1].astype(jnp.float32)
    total = total + sums_in[1, reach[1] - 1].astype(jnp.float32)
    o_ref[...] = total.astype(o_ref.dtype)


def kernel_reduce_scatter(partial, axis, other, collective_id, pieces=4):
    count = lax.axis_size(axis)
    blocks = partial.reshape((count, partial.shape[0] // count) + partial.shape[1:])
    block = blocks.shape[1:]
    reach = count // 2
    return pl.pallas_call(
        functools.partial(
            ring_sum_kernel, count=count, axis=axis, other=other, pieces=pieces
        ),
        out_shape=jax.ShapeDtypeStruct(block, partial.dtype),
        in_specs=[pl.BlockSpec(memory_space=pltpu.VMEM)],
        out_specs=pl.BlockSpec(memory_space=pltpu.VMEM),
        scratch_shapes=[
            pltpu.VMEM((2, reach) + block, partial.dtype),
            pltpu.VMEM((2, reach) + block, partial.dtype),
            pltpu.SemaphoreType.DMA((2, 2, reach, pieces)),
        ],
        compiler_params=pltpu.CompilerParams(collective_id=collective_id, has_side_effects=True),
    )(blocks)


def project_rows(rows, weight):
    flat = rows.reshape(-1, rows.shape[-1])
    return jnp.dot(flat, weight, preferred_element_type=jnp.float32).astype(jnp.bfloat16)


def local(
    hidden,
    norm_gain,
    query_weight,
    key_weight,
    value_weight,
    out_weight,
    encodings,
    row_place,
    neighbour_ids,
    neighbour_counts,
):
    ctx_count = lax.axis_size("ctx")
    ctx_index = lax.axis_index("ctx")
    tok_dev = hidden.shape[0]
    rows_dev = encodings.shape[0]
    slice_tokens = encodings.shape[1]
    enc_width = encodings.shape[2]
    span_dev = tok_dev // CH
    head_width = query_weight.shape[1]
    head_count = head_width // HS
    slot_cap = -(-rows_dev // ctx_count)
    whole = lax.all_gather(hidden, "tp", axis=1, tiled=True)
    values_wide = whole.astype(jnp.float32)
    mean_square = jnp.mean(values_wide * values_wide, axis=1, keepdims=True)
    normed = (values_wide * lax.rsqrt(mean_square + epsilon) * norm_gain[None, :]).astype(
        jnp.bfloat16
    )
    query_full = lax.all_to_all(
        jnp.broadcast_to(query_weight[None], (ctx_count,) + query_weight.shape),
        "ctx",
        split_axis=0,
        concat_axis=0,
        tiled=True,
    ).reshape(-1, query_weight.shape[1])
    query_sum = jnp.dot(normed, query_full, preferred_element_type=jnp.float32)
    queries = (query_sum * HS ** (-0.5)).astype(jnp.bfloat16)
    storage = row_place[neighbour_ids.reshape(-1)].reshape(ctx_count, rows_dev)
    sources = storage // rows_dev
    local_rows = storage % rows_dev
    from_here = sources == ctx_index
    rank_position = jnp.cumsum(from_here.astype(jnp.int32), axis=1) - 1
    picked_rows = from_here & (rank_position == 0)
    pick_list = [jnp.sum(jnp.where(picked_rows, local_rows, 0), axis=1)]
    fill_list = [jnp.any(picked_rows, axis=1)]
    pick_index = jnp.stack(pick_list, axis=1)
    fill_mask = jnp.stack(fill_list, axis=1)
    outgoing = encodings[pick_index] * fill_mask[:, :, None, None].astype(jnp.bfloat16)
    incoming = lax.all_to_all(outgoing, "ctx", split_axis=0, concat_axis=0, tiled=True)
    own_sources = lax.dynamic_index_in_dim(sources, ctx_index, 0, keepdims=False)
    slot_order = jnp.arange(rows_dev)
    earlier = (own_sources[:, None] == own_sources[None, :]) & (
        slot_order[None, :] < slot_order[:, None]
    )
    own_rank = jnp.sum(earlier.astype(jnp.int32), axis=1)
    flat_index = own_sources * slot_cap + own_rank
    picked = incoming.reshape(ctx_count * slot_cap, slice_tokens, enc_width)[flat_index]
    row_total = picked.shape[0]
    full_rows = jnp.swapaxes(kernel_gather(picked, "tp", "ctx", 0), 0, 1).reshape(
        picked.shape[0], -1, picked.shape[2]
    )
    keys = project_rows(full_rows, key_weight).reshape(row_total, -1, head_width)
    values = project_rows(full_rows, value_weight).reshape(row_total, -1, head_width)
    neighbour_len = keys.shape[1]
    prior_keys, prior_values = shifted(
        (keys[row_total - KNB :], values[row_total - KNB :]), "ctx", 1
    )
    key_stack = jnp.concatenate([prior_keys, keys], axis=0)
    value_stack = jnp.concatenate([prior_values, values], axis=0)
    key_blocks = key_stack.reshape(span_dev + 1, KNB * neighbour_len, head_count, HS)
    value_blocks = value_stack.reshape(span_dev + 1, KNB * neighbour_len, head_count, HS)
    first_span = ctx_index * span_dev
    local_counts = lax.dynamic_slice_in_dim(neighbour_counts, first_span, span_dev)
    prior_count = lax.dynamic_slice_in_dim(neighbour_counts, jnp.maximum(first_span - 1, 0), 1)
    block_counts = jnp.concatenate([prior_count, local_counts], axis=0)
    padded = jnp.concatenate(
        [
            jnp.zeros((1, head_width), jnp.bfloat16),
            queries,
            jnp.zeros((CH - 1, head_width), jnp.bfloat16),
        ],
        axis=0,
    )
    query_blocks = padded.reshape(span_dev + 1, CH, head_count, HS)
    scores = jnp.einsum(
        "wqhd,wkhd->whqk", query_blocks, key_blocks, preferred_element_type=jnp.float32
    )
    slot_of_key = jnp.arange(KNB * neighbour_len) // neighbour_len
    live = slot_of_key[None, :] < block_counts[:, None]
    scores = jnp.where(live[:, None, None, :], scores, masked_score)
    peak = jnp.max(scores, axis=3, keepdims=True)
    expos = jnp.exp(scores - peak)
    total = jnp.sum(expos, axis=3)
    weights = expos.astype(jnp.bfloat16)
    blended = jnp.einsum(
        "whqk,wkhd->wqhd", weights, value_blocks, preferred_element_type=jnp.float32
    )
    blended = blended / jnp.swapaxes(total, 1, 2)[:, :, :, None]
    blended = blended.reshape((span_dev + 1) * CH, head_width)[1 : tok_dev + 1]
    position = ctx_index * tok_dev + jnp.arange(tok_dev)
    valid = position % LENGTH >= CH - 1
    attended = jnp.where(valid[:, None], blended, jnp.zeros_like(blended)).astype(jnp.bfloat16)
    mixed_part = jnp.dot(attended, out_weight, preferred_element_type=jnp.float32).astype(
        jnp.bfloat16
    )
    return kernel_reduce_scatter(mixed_part, "tp", "ctx", 1)


def solution(mesh):
    return jax.shard_map(
        local,
        mesh=mesh,
        in_specs=(
            P("ctx", "tp"),
            P(),
            P("ctx", "tp"),
            P(None, "tp"),
            P(None, "tp"),
            P("tp", None),
            P("ctx", "tp", None),
            P(),
            P(),
            P(),
        ),
        out_specs=P(("ctx", "tp"), None),
        check_vma=False,
    )
```

```python
import functools

import jax
import jax.numpy as jnp
from jax import lax
from jax.experimental import pallas as pl
from jax.experimental.pallas import tpu as pltpu
from jax.sharding import PartitionSpec as P

HS = 128
CH = 64
KNB = 2
LENGTH = 8192


epsilon = 1e-05
masked_score = -1e30


def shifted(block, axis, distance):
    devices = range(lax.axis_size(axis))
    route = [(i - distance, i) for i in devices if i - distance in devices]
    return lax.ppermute(block, axis, route)


def greet_neighbours(me, row, count):
    right = lax.rem(me + 1, count)
    left = lax.rem(me + count - 1, count)
    barrier = pltpu.get_barrier_semaphore()
    for neighbour in (left, right):
        pl.semaphore_signal(
            barrier, inc=1, device_id=(row, neighbour), device_id_type=pl.DeviceIdType.MESH
        )
    pl.semaphore_wait(barrier, 2)
    return right, left


def ring_gather_kernel(x_ref, o_ref, send_sem, recv_sem, *, count, axis, other, pieces, view):
    me = lax.axis_index(axis)
    row = lax.axis_index(other)
    right, left = greet_neighbours(me, row, count)
    half = count // 2
    size = x_ref.shape[0] // pieces
    view(o_ref, half, pl.ds(0, x_ref.shape[0]))[...] = x_ref[...]
    copies = {}
    for step in range(1, half + 1):
        for piece in range(pieces):
            part = pl.ds(piece * size, size)
            for toward in (0, 1):
                if toward == 1 and step > count - 1 - half:
                    continue
                slot = half - step if toward == 0 else half + step
                source = slot + 1 if toward == 0 else slot - 1
                if step > 1:
                    copies[(step - 1, toward, piece)].wait_recv()
                copy = pltpu.make_async_remote_copy(
                    src_ref=x_ref.at[part] if step == 1 else view(o_ref, source, part),
                    dst_ref=view(o_ref, slot, part),
                    send_sem=send_sem.at[slot, piece],
                    recv_sem=recv_sem.at[slot, piece],
                    device_id=(row, right if toward == 0 else left),
                    device_id_type=pl.DeviceIdType.MESH,
                )
                copy.start()
                copies[(step, toward, piece)] = copy
    for piece in range(pieces):
        copies[(half, 0, piece)].wait_recv()
        copies[(count - 1 - half, 1, piece)].wait_recv()
    for copy in copies.values():
        copy.wait_send()


def slot_stack(ref, slot, part):
    return ref.at[part, slot]


def slot_stripe(ref, slot, part):
    width = ref.shape[1] // lax.axis_size("tp")
    return ref.at[part, pl.ds(slot * width, width)]


def kernel_gather(block, axis, other, collective_id, shape, view, pieces=4):
    count = lax.axis_size(axis)
    return pl.pallas_call(
        functools.partial(
            ring_gather_kernel, count=count, axis=axis, other=other, pieces=pieces, view=view
        ),
        out_shape=jax.ShapeDtypeStruct(shape, block.dtype),
        in_specs=[pl.BlockSpec(memory_space=pltpu.VMEM)],
        out_specs=pl.BlockSpec(memory_space=pltpu.VMEM),
        scratch_shapes=[
            pltpu.SemaphoreType.DMA((count, pieces)),
            pltpu.SemaphoreType.DMA((count, pieces)),
        ],
        compiler_params=pltpu.CompilerParams(collective_id=collective_id, has_side_effects=True),
    )(block)


def ring_sum_kernel(p_ref, o_ref, sums_in, sums_out, sems, *, count, axis, other, pieces):
    me = lax.axis_index(axis)
    row = lax.axis_index(other)
    right, left = greet_neighbours(me, row, count)
    reach = (count // 2, count - 1 - count // 2)
    width = p_ref.shape[2] // pieces

    def own(offset, part):
        return p_ref[lax.rem(me + offset + 2 * count, count), :, part].astype(jnp.float32)

    copies = {}
    for step in range(1, reach[0] + 1):
        for piece in range(pieces):
            part = pl.ds(piece * width, width)
            for toward in (0, 1):
                if step > reach[toward]:
                    continue
                if step == 1:
                    first = reach[0] if toward == 0 else count - reach[1]
                    source = p_ref.at[lax.rem(me + first, count), :, part]
                else:
                    copies[(step - 1, toward, piece)].wait_recv()
                    offset = reach[0] - step + 1 if toward == 0 else step - 1 - reach[1]
                    sums_out[toward, step - 2, :, part] = (
                        sums_in[toward, step - 2, :, part].astype(jnp.float32) + own(offset, part)
                    ).astype(sums_out.dtype)
                    source = sums_out.at[toward, step - 2, :, part]
                copy = pltpu.make_async_remote_copy(
                    src_ref=source,
                    dst_ref=sums_in.at[toward, step - 1, :, part],
                    send_sem=sems.at[0, toward, step - 1, piece],
                    recv_sem=sems.at[1, toward, step - 1, piece],
                    device_id=(row, right if toward == 0 else left),
                    device_id_type=pl.DeviceIdType.MESH,
                )
                copy.start()
                copies[(step, toward, piece)] = copy
    for piece in range(pieces):
        copies[(reach[0], 0, piece)].wait_recv()
        copies[(reach[1], 1, piece)].wait_recv()
    for copy in copies.values():
        copy.wait_send()
    total = p_ref[me].astype(jnp.float32) + sums_in[0, reach[0] - 1].astype(jnp.float32)
    total = total + sums_in[1, reach[1] - 1].astype(jnp.float32)
    o_ref[...] = total.astype(o_ref.dtype)


def kernel_reduce_scatter(partial, axis, other, collective_id, pieces=4):
    count = lax.axis_size(axis)
    blocks = partial.reshape((count, partial.shape[0] // count) + partial.shape[1:])
    block = blocks.shape[1:]
    reach = count // 2
    return pl.pallas_call(
        functools.partial(
            ring_sum_kernel, count=count, axis=axis, other=other, pieces=pieces
        ),
        out_shape=jax.ShapeDtypeStruct(block, partial.dtype),
        in_specs=[pl.BlockSpec(memory_space=pltpu.VMEM)],
        out_specs=pl.BlockSpec(memory_space=pltpu.VMEM),
        scratch_shapes=[
            pltpu.VMEM((2, reach) + block, partial.dtype),
            pltpu.VMEM((2, reach) + block, partial.dtype),
            pltpu.SemaphoreType.DMA((2, 2, reach, pieces)),
        ],
        compiler_params=pltpu.CompilerParams(collective_id=collective_id, has_side_effects=True),
    )(blocks)


def project_rows(rows, weight):
    flat = rows.reshape(-1, rows.shape[-1])
    return jnp.dot(flat, weight, preferred_element_type=jnp.float32).astype(jnp.bfloat16)


def local(
    hidden,
    norm_gain,
    query_weight,
    key_weight,
    value_weight,
    out_weight,
    encodings,
    row_place,
    neighbour_ids,
    neighbour_counts,
):
    ctx_count = lax.axis_size("ctx")
    ctx_index = lax.axis_index("ctx")
    tok_dev = hidden.shape[0]
    rows_dev = encodings.shape[0]
    slice_tokens = encodings.shape[1]
    enc_width = encodings.shape[2]
    span_dev = tok_dev // CH
    head_width = query_weight.shape[1]
    head_count = head_width // HS
    slot_cap = -(-rows_dev // ctx_count)
    tp_count = lax.axis_size("tp")
    tp_index = lax.axis_index("tp")
    whole = kernel_gather(
        hidden, "tp", "ctx", 2, (hidden.shape[0], tp_count * hidden.shape[1]), slot_stripe
    )
    rotation = ((tp_index - tp_count // 2) % tp_count) * hidden.shape[1]
    gain = lax.dynamic_slice_in_dim(jnp.concatenate([norm_gain, norm_gain]), rotation, whole.shape[1])
    values_wide = whole.astype(jnp.float32)
    mean_square = jnp.mean(values_wide * values_wide, axis=1, keepdims=True)
    normed = (values_wide * lax.rsqrt(mean_square + epsilon) * gain[None, :]).astype(
        jnp.bfloat16
    )
    query_full = lax.all_to_all(
        jnp.broadcast_to(query_weight[None], (ctx_count,) + query_weight.shape),
        "ctx",
        split_axis=0,
        concat_axis=0,
        tiled=True,
    ).reshape(-1, query_weight.shape[1])
    query_full = lax.dynamic_slice_in_dim(
        jnp.concatenate([query_full, query_full]), rotation, query_full.shape[0]
    )
    query_sum = jnp.dot(normed, query_full, preferred_element_type=jnp.float32)
    queries = (query_sum * HS ** (-0.5)).astype(jnp.bfloat16)
    storage = row_place[neighbour_ids.reshape(-1)].reshape(ctx_count, rows_dev)
    sources = storage // rows_dev
    local_rows = storage % rows_dev
    from_here = sources == ctx_index
    rank_position = jnp.cumsum(from_here.astype(jnp.int32), axis=1) - 1
    picked_rows = from_here & (rank_position == 0)
    pick_list = [jnp.sum(jnp.where(picked_rows, local_rows, 0), axis=1)]
    fill_list = [jnp.any(picked_rows, axis=1)]
    pick_index = jnp.stack(pick_list, axis=1)
    fill_mask = jnp.stack(fill_list, axis=1)
    outgoing = encodings[pick_index] * fill_mask[:, :, None, None].astype(jnp.bfloat16)
    incoming = lax.all_to_all(outgoing, "ctx", split_axis=0, concat_axis=0, tiled=True)
    own_sources = lax.dynamic_index_in_dim(sources, ctx_index, 0, keepdims=False)
    slot_order = jnp.arange(rows_dev)
    earlier = (own_sources[:, None] == own_sources[None, :]) & (
        slot_order[None, :] < slot_order[:, None]
    )
    own_rank = jnp.sum(earlier.astype(jnp.int32), axis=1)
    flat_index = own_sources * slot_cap + own_rank
    picked = incoming.reshape(ctx_count * slot_cap, slice_tokens, enc_width)[flat_index]
    row_total = picked.shape[0]
    full_rows = kernel_gather(
        picked,
        "tp",
        "ctx",
        0,
        (picked.shape[0], lax.axis_size("tp")) + picked.shape[1:],
        slot_stack,
    ).reshape(picked.shape[0], -1, picked.shape[2])
    keys = project_rows(full_rows, key_weight).reshape(row_total, -1, head_width)
    values = project_rows(full_rows, value_weight).reshape(row_total, -1, head_width)
    neighbour_len = keys.shape[1]
    prior_keys, prior_values = shifted(
        (keys[row_total - KNB :], values[row_total - KNB :]), "ctx", 1
    )
    key_stack = jnp.concatenate([prior_keys, keys], axis=0)
    value_stack = jnp.concatenate([prior_values, values], axis=0)
    key_blocks = key_stack.reshape(span_dev + 1, KNB * neighbour_len, head_count, HS)
    value_blocks = value_stack.reshape(span_dev + 1, KNB * neighbour_len, head_count, HS)
    first_span = ctx_index * span_dev
    local_counts = lax.dynamic_slice_in_dim(neighbour_counts, first_span, span_dev)
    prior_count = lax.dynamic_slice_in_dim(neighbour_counts, jnp.maximum(first_span - 1, 0), 1)
    block_counts = jnp.concatenate([prior_count, local_counts], axis=0)
    padded = jnp.concatenate(
        [
            jnp.zeros((1, head_width), jnp.bfloat16),
            queries,
            jnp.zeros((CH - 1, head_width), jnp.bfloat16),
        ],
        axis=0,
    )
    query_blocks = padded.reshape(span_dev + 1, CH, head_count, HS)
    scores = jnp.einsum(
        "wqhd,wkhd->whqk", query_blocks, key_blocks, preferred_element_type=jnp.float32
    )
    slot_of_key = jnp.arange(KNB * neighbour_len) // neighbour_len
    live = slot_of_key[None, :] < block_counts[:, None]
    scores = jnp.where(live[:, None, None, :], scores, masked_score)
    peak = jnp.max(scores, axis=3, keepdims=True)
    expos = jnp.exp(scores - peak)
    total = jnp.sum(expos, axis=3)
    weights = expos.astype(jnp.bfloat16)
    blended = jnp.einsum(
        "whqk,wkhd->wqhd", weights, value_blocks, preferred_element_type=jnp.float32
    )
    blended = blended / jnp.swapaxes(total, 1, 2)[:, :, :, None]
    blended = blended.reshape((span_dev + 1) * CH, head_width)[1 : tok_dev + 1]
    position = ctx_index * tok_dev + jnp.arange(tok_dev)
    valid = position % LENGTH >= CH - 1
    attended = jnp.where(valid[:, None], blended, jnp.zeros_like(blended)).astype(jnp.bfloat16)
    mixed_part = jnp.dot(attended, out_weight, preferred_element_type=jnp.float32).astype(
        jnp.bfloat16
    )
    return kernel_reduce_scatter(mixed_part, "tp", "ctx", 1)


def solution(mesh):
    return jax.shard_map(
        local,
        mesh=mesh,
        in_specs=(
            P("ctx", "tp"),
            P(),
            P("ctx", "tp"),
            P(None, "tp"),
            P(None, "tp"),
            P("tp", None),
            P("ctx", "tp", None),
            P(),
            P(),
            P(),
        ),
        out_specs=P(("ctx", "tp"), None),
        check_vma=False,
    )
```

```python
import functools

import jax
import jax.numpy as jnp
from jax import lax
from jax.experimental import pallas as pl
from jax.experimental.pallas import tpu as pltpu
from jax.sharding import PartitionSpec as P

HS = 128
CH = 64
KNB = 2
LENGTH = 8192


epsilon = 1e-05
masked_score = -1e30


def shifted(block, axis, distance):
    devices = range(lax.axis_size(axis))
    route = [(i - distance, i) for i in devices if i - distance in devices]
    return lax.ppermute(block, axis, route)


def greet_neighbours(me, row, count):
    right = lax.rem(me + 1, count)
    left = lax.rem(me + count - 1, count)
    barrier = pltpu.get_barrier_semaphore()
    for neighbour in (left, right):
        pl.semaphore_signal(
            barrier, inc=1, device_id=(row, neighbour), device_id_type=pl.DeviceIdType.MESH
        )
    pl.semaphore_wait(barrier, 2)
    return right, left


def ring_gather_kernel(x_ref, o_ref, send_sem, recv_sem, *, count, axis, other, pieces, view):
    me = lax.axis_index(axis)
    row = lax.axis_index(other)
    right, left = greet_neighbours(me, row, count)
    half = count // 2
    size = x_ref.shape[0] // pieces
    view(o_ref, half, pl.ds(0, x_ref.shape[0]))[...] = x_ref[...]
    copies = {}
    for step in range(1, half + 1):
        for piece in range(pieces):
            part = pl.ds(piece * size, size)
            for toward in (0, 1):
                if toward == 1 and step > count - 1 - half:
                    continue
                slot = half - step if toward == 0 else half + step
                source = slot + 1 if toward == 0 else slot - 1
                if step > 1:
                    copies[(step - 1, toward, piece)].wait_recv()
                copy = pltpu.make_async_remote_copy(
                    src_ref=x_ref.at[part] if step == 1 else view(o_ref, source, part),
                    dst_ref=view(o_ref, slot, part),
                    send_sem=send_sem.at[slot, piece],
                    recv_sem=recv_sem.at[slot, piece],
                    device_id=(row, right if toward == 0 else left),
                    device_id_type=pl.DeviceIdType.MESH,
                )
                copy.start()
                copies[(step, toward, piece)] = copy
    for piece in range(pieces):
        copies[(half, 0, piece)].wait_recv()
        copies[(count - 1 - half, 1, piece)].wait_recv()
    for copy in copies.values():
        copy.wait_send()


def slot_stack(ref, slot, part):
    return ref.at[part, slot]


def kernel_gather(block, axis, other, collective_id, shape, view, pieces=4):
    count = lax.axis_size(axis)
    return pl.pallas_call(
        functools.partial(
            ring_gather_kernel, count=count, axis=axis, other=other, pieces=pieces, view=view
        ),
        out_shape=jax.ShapeDtypeStruct(shape, block.dtype),
        in_specs=[pl.BlockSpec(memory_space=pltpu.VMEM)],
        out_specs=pl.BlockSpec(memory_space=pltpu.VMEM),
        scratch_shapes=[
            pltpu.SemaphoreType.DMA((count, pieces)),
            pltpu.SemaphoreType.DMA((count, pieces)),
        ],
        compiler_params=pltpu.CompilerParams(collective_id=collective_id, has_side_effects=True),
    )(block)


def ring_sum_kernel(p_ref, o_ref, sums_in, sums_out, sems, *, count, axis, other, pieces):
    me = lax.axis_index(axis)
    row = lax.axis_index(other)
    right, left = greet_neighbours(me, row, count)
    reach = (count // 2, count - 1 - count // 2)
    width = p_ref.shape[2] // pieces

    def own(offset, part):
        return p_ref[lax.rem(me + offset + 2 * count, count), :, part].astype(jnp.float32)

    copies = {}
    for step in range(1, reach[0] + 1):
        for piece in range(pieces):
            part = pl.ds(piece * width, width)
            for toward in (0, 1):
                if step > reach[toward]:
                    continue
                if step == 1:
                    first = reach[0] if toward == 0 else count - reach[1]
                    source = p_ref.at[lax.rem(me + first, count), :, part]
                else:
                    copies[(step - 1, toward, piece)].wait_recv()
                    offset = reach[0] - step + 1 if toward == 0 else step - 1 - reach[1]
                    sums_out[toward, step - 2, :, part] = (
                        sums_in[toward, step - 2, :, part].astype(jnp.float32) + own(offset, part)
                    ).astype(sums_out.dtype)
                    source = sums_out.at[toward, step - 2, :, part]
                copy = pltpu.make_async_remote_copy(
                    src_ref=source,
                    dst_ref=sums_in.at[toward, step - 1, :, part],
                    send_sem=sems.at[0, toward, step - 1, piece],
                    recv_sem=sems.at[1, toward, step - 1, piece],
                    device_id=(row, right if toward == 0 else left),
                    device_id_type=pl.DeviceIdType.MESH,
                )
                copy.start()
                copies[(step, toward, piece)] = copy
    for piece in range(pieces):
        copies[(reach[0], 0, piece)].wait_recv()
        copies[(reach[1], 1, piece)].wait_recv()
    for copy in copies.values():
        copy.wait_send()
    total = p_ref[me].astype(jnp.float32) + sums_in[0, reach[0] - 1].astype(jnp.float32)
    total = total + sums_in[1, reach[1] - 1].astype(jnp.float32)
    o_ref[...] = total.astype(o_ref.dtype)


def kernel_reduce_scatter(partial, axis, other, collective_id, pieces=4):
    count = lax.axis_size(axis)
    blocks = partial.reshape((count, partial.shape[0] // count) + partial.shape[1:])
    block = blocks.shape[1:]
    reach = count // 2
    return pl.pallas_call(
        functools.partial(
            ring_sum_kernel, count=count, axis=axis, other=other, pieces=pieces
        ),
        out_shape=jax.ShapeDtypeStruct(block, partial.dtype),
        in_specs=[pl.BlockSpec(memory_space=pltpu.VMEM)],
        out_specs=pl.BlockSpec(memory_space=pltpu.VMEM),
        scratch_shapes=[
            pltpu.VMEM((2, reach) + block, partial.dtype),
            pltpu.VMEM((2, reach) + block, partial.dtype),
            pltpu.SemaphoreType.DMA((2, 2, reach, pieces)),
        ],
        compiler_params=pltpu.CompilerParams(collective_id=collective_id, has_side_effects=True),
    )(blocks)


def project_rows(rows, weight):
    flat = rows.reshape(-1, rows.shape[-1])
    return jnp.dot(flat, weight, preferred_element_type=jnp.float32).astype(jnp.bfloat16)


def local(
    hidden,
    norm_gain,
    query_weight,
    key_weight,
    value_weight,
    out_weight,
    encodings,
    row_place,
    neighbour_ids,
    neighbour_counts,
):
    ctx_count = lax.axis_size("ctx")
    ctx_index = lax.axis_index("ctx")
    tok_dev = hidden.shape[0]
    rows_dev = encodings.shape[0]
    slice_tokens = encodings.shape[1]
    enc_width = encodings.shape[2]
    span_dev = tok_dev // CH
    head_width = query_weight.shape[1]
    head_count = head_width // HS
    slot_cap = -(-rows_dev // ctx_count)
    whole = lax.all_gather(hidden, "tp", axis=1, tiled=True)
    values_wide = whole.astype(jnp.float32)
    mean_square = jnp.mean(values_wide * values_wide, axis=1, keepdims=True)
    normed = (values_wide * lax.rsqrt(mean_square + epsilon) * norm_gain[None, :]).astype(
        jnp.bfloat16
    )
    query_full = lax.all_to_all(
        jnp.broadcast_to(query_weight[None], (ctx_count,) + query_weight.shape),
        "ctx",
        split_axis=0,
        concat_axis=0,
        tiled=True,
    ).reshape(-1, query_weight.shape[1])
    query_sum = jnp.dot(normed, query_full, preferred_element_type=jnp.float32)
    queries = (query_sum * HS ** (-0.5)).astype(jnp.bfloat16)
    storage = row_place[neighbour_ids.reshape(-1)].reshape(ctx_count, rows_dev)
    sources = storage // rows_dev
    local_rows = storage % rows_dev
    from_here = sources == ctx_index
    rank_position = jnp.cumsum(from_here.astype(jnp.int32), axis=1) - 1
    picked_rows = from_here & (rank_position == 0)
    pick_list = [jnp.sum(jnp.where(picked_rows, local_rows, 0), axis=1)]
    fill_list = [jnp.any(picked_rows, axis=1)]
    pick_index = jnp.stack(pick_list, axis=1)
    fill_mask = jnp.stack(fill_list, axis=1)
    outgoing = encodings[pick_index] * fill_mask[:, :, None, None].astype(jnp.bfloat16)
    incoming = lax.all_to_all(outgoing, "ctx", split_axis=0, concat_axis=0, tiled=True)
    own_sources = lax.dynamic_index_in_dim(sources, ctx_index, 0, keepdims=False)
    slot_order = jnp.arange(rows_dev)
    earlier = (own_sources[:, None] == own_sources[None, :]) & (
        slot_order[None, :] < slot_order[:, None]
    )
    own_rank = jnp.sum(earlier.astype(jnp.int32), axis=1)
    flat_index = own_sources * slot_cap + own_rank
    picked = incoming.reshape(ctx_count * slot_cap, slice_tokens, enc_width)[flat_index]
    row_total = picked.shape[0]
    full_rows = kernel_gather(
        picked,
        "tp",
        "ctx",
        0,
        (picked.shape[0], lax.axis_size("tp")) + picked.shape[1:],
        slot_stack,
        pieces=8,
    ).reshape(picked.shape[0], -1, picked.shape[2])
    keys = project_rows(full_rows, key_weight).reshape(row_total, -1, head_width)
    values = project_rows(full_rows, value_weight).reshape(row_total, -1, head_width)
    neighbour_len = keys.shape[1]
    prior_keys, prior_values = shifted(
        (keys[row_total - KNB :], values[row_total - KNB :]), "ctx", 1
    )
    key_stack = jnp.concatenate([prior_keys, keys], axis=0)
    value_stack = jnp.concatenate([prior_values, values], axis=0)
    key_blocks = key_stack.reshape(span_dev + 1, KNB * neighbour_len, head_count, HS)
    value_blocks = value_stack.reshape(span_dev + 1, KNB * neighbour_len, head_count, HS)
    first_span = ctx_index * span_dev
    local_counts = lax.dynamic_slice_in_dim(neighbour_counts, first_span, span_dev)
    prior_count = lax.dynamic_slice_in_dim(neighbour_counts, jnp.maximum(first_span - 1, 0), 1)
    block_counts = jnp.concatenate([prior_count, local_counts], axis=0)
    padded = jnp.concatenate(
        [
            jnp.zeros((1, head_width), jnp.bfloat16),
            queries,
            jnp.zeros((CH - 1, head_width), jnp.bfloat16),
        ],
        axis=0,
    )
    query_blocks = padded.reshape(span_dev + 1, CH, head_count, HS)
    scores = jnp.einsum(
        "wqhd,wkhd->whqk", query_blocks, key_blocks, preferred_element_type=jnp.float32
    )
    slot_of_key = jnp.arange(KNB * neighbour_len) // neighbour_len
    live = slot_of_key[None, :] < block_counts[:, None]
    scores = jnp.where(live[:, None, None, :], scores, masked_score)
    peak = jnp.max(scores, axis=3, keepdims=True)
    expos = jnp.exp(scores - peak)
    total = jnp.sum(expos, axis=3)
    weights = expos.astype(jnp.bfloat16)
    blended = jnp.einsum(
        "whqk,wkhd->wqhd", weights, value_blocks, preferred_element_type=jnp.float32
    )
    blended = blended / jnp.swapaxes(total, 1, 2)[:, :, :, None]
    blended = blended.reshape((span_dev + 1) * CH, head_width)[1 : tok_dev + 1]
    position = ctx_index * tok_dev + jnp.arange(tok_dev)
    valid = position % LENGTH >= CH - 1
    attended = jnp.where(valid[:, None], blended, jnp.zeros_like(blended)).astype(jnp.bfloat16)
    mixed_part = jnp.dot(attended, out_weight, preferred_element_type=jnp.float32).astype(
        jnp.bfloat16
    )
    return kernel_reduce_scatter(mixed_part, "tp", "ctx", 1, pieces=8)


def solution(mesh):
    return jax.shard_map(
        local,
        mesh=mesh,
        in_specs=(
            P("ctx", "tp"),
            P(),
            P("ctx", "tp"),
            P(None, "tp"),
            P(None, "tp"),
            P("tp", None),
            P("ctx", "tp", None),
            P(),
            P(),
            P(),
        ),
        out_specs=P(("ctx", "tp"), None),
        check_vma=False,
    )
```

```python
import functools

import jax
import jax.numpy as jnp
from jax import lax
from jax.experimental import pallas as pl
from jax.experimental.pallas import tpu as pltpu
from jax.sharding import PartitionSpec as P

HS = 128
CH = 64
KNB = 2
LENGTH = 8192


epsilon = 1e-05
masked_score = -1e30


def shifted(block, axis, distance):
    devices = range(lax.axis_size(axis))
    route = [(i - distance, i) for i in devices if i - distance in devices]
    return lax.ppermute(block, axis, route)


def greet_neighbours(me, row, count):
    right = lax.rem(me + 1, count)
    left = lax.rem(me + count - 1, count)
    barrier = pltpu.get_barrier_semaphore()
    for neighbour in (left, right):
        pl.semaphore_signal(
            barrier, inc=1, device_id=(row, neighbour), device_id_type=pl.DeviceIdType.MESH
        )
    pl.semaphore_wait(barrier, 2)
    return right, left


def ring_gather_kernel(x_ref, o_ref, send_sem, recv_sem, *, count, axis, other, pieces):
    me = lax.axis_index(axis)
    row = lax.axis_index(other)
    right, left = greet_neighbours(me, row, count)
    half = count // 2
    size = x_ref.shape[0] // pieces
    o_ref[half] = x_ref[...]
    copies = {}
    for step in range(1, half + 1):
        for piece in range(pieces):
            part = pl.ds(piece * size, size)
            for toward in (0, 1):
                if toward == 1 and step > count - 1 - half:
                    continue
                slot = half - step if toward == 0 else half + step
                source = slot + 1 if toward == 0 else slot - 1
                if step > 1:
                    copies[(step - 1, toward, piece)].wait_recv()
                copy = pltpu.make_async_remote_copy(
                    src_ref=x_ref.at[part] if step == 1 else o_ref.at[source, part],
                    dst_ref=o_ref.at[slot, part],
                    send_sem=send_sem.at[slot, piece],
                    recv_sem=recv_sem.at[slot, piece],
                    device_id=(row, right if toward == 0 else left),
                    device_id_type=pl.DeviceIdType.MESH,
                )
                copy.start()
                copies[(step, toward, piece)] = copy
    for piece in range(pieces):
        copies[(half, 0, piece)].wait_recv()
        copies[(count - 1 - half, 1, piece)].wait_recv()
    for copy in copies.values():
        copy.wait_send()


def kernel_gather(block, axis, other, collective_id, pieces=4):
    count = lax.axis_size(axis)
    return pl.pallas_call(
        functools.partial(
            ring_gather_kernel, count=count, axis=axis, other=other, pieces=pieces
        ),
        out_shape=jax.ShapeDtypeStruct((count,) + block.shape, block.dtype),
        in_specs=[pl.BlockSpec(memory_space=pltpu.VMEM)],
        out_specs=pl.BlockSpec(memory_space=pltpu.VMEM),
        scratch_shapes=[
            pltpu.SemaphoreType.DMA((count, pieces)),
            pltpu.SemaphoreType.DMA((count, pieces)),
        ],
        compiler_params=pltpu.CompilerParams(collective_id=collective_id, has_side_effects=True),
    )(block)


def ring_sum_kernel(p_ref, o_ref, sums_in, sums_out, sems, *, count, axis, other, pieces):
    me = lax.axis_index(axis)
    row = lax.axis_index(other)
    right, left = greet_neighbours(me, row, count)
    reach = (count // 2, count - 1 - count // 2)
    width = p_ref.shape[2] // pieces

    def own(offset, part):
        return p_ref[lax.rem(me + offset + 2 * count, count), :, part].astype(jnp.float32)

    copies = {}
    for step in range(1, reach[0] + 1):
        for piece in range(pieces):
            part = pl.ds(piece * width, width)
            for toward in (0, 1):
                if step > reach[toward]:
                    continue
                if step == 1:
                    first = reach[0] if toward == 0 else count - reach[1]
                    source = p_ref.at[lax.rem(me + first, count), :, part]
                else:
                    copies[(step - 1, toward, piece)].wait_recv()
                    offset = reach[0] - step + 1 if toward == 0 else step - 1 - reach[1]
                    sums_out[toward, step - 2, :, part] = (
                        sums_in[toward, step - 2, :, part].astype(jnp.float32) + own(offset, part)
                    ).astype(sums_out.dtype)
                    source = sums_out.at[toward, step - 2, :, part]
                copy = pltpu.make_async_remote_copy(
                    src_ref=source,
                    dst_ref=sums_in.at[toward, step - 1, :, part],
                    send_sem=sems.at[0, toward, step - 1, piece],
                    recv_sem=sems.at[1, toward, step - 1, piece],
                    device_id=(row, right if toward == 0 else left),
                    device_id_type=pl.DeviceIdType.MESH,
                )
                copy.start()
                copies[(step, toward, piece)] = copy
    for piece in range(pieces):
        copies[(reach[0], 0, piece)].wait_recv()
        copies[(reach[1], 1, piece)].wait_recv()
    for copy in copies.values():
        copy.wait_send()
    total = p_ref[me].astype(jnp.float32) + sums_in[0, reach[0] - 1].astype(jnp.float32)
    total = total + sums_in[1, reach[1] - 1].astype(jnp.float32)
    o_ref[...] = total.astype(o_ref.dtype)


def kernel_reduce_scatter(partial, axis, other, collective_id, pieces=4):
    count = lax.axis_size(axis)
    blocks = partial.reshape((count, partial.shape[0] // count) + partial.shape[1:])
    block = blocks.shape[1:]
    reach = count // 2
    return pl.pallas_call(
        functools.partial(
            ring_sum_kernel, count=count, axis=axis, other=other, pieces=pieces
        ),
        out_shape=jax.ShapeDtypeStruct(block, partial.dtype),
        in_specs=[pl.BlockSpec(memory_space=pltpu.VMEM)],
        out_specs=pl.BlockSpec(memory_space=pltpu.VMEM),
        scratch_shapes=[
            pltpu.VMEM((2, reach) + block, partial.dtype),
            pltpu.VMEM((2, reach) + block, partial.dtype),
            pltpu.SemaphoreType.DMA((2, 2, reach, pieces)),
        ],
        compiler_params=pltpu.CompilerParams(collective_id=collective_id, has_side_effects=True),
    )(blocks)


def project_rows(rows, weight):
    flat = rows.reshape(-1, rows.shape[-1])
    return jnp.dot(flat, weight, preferred_element_type=jnp.float32).astype(jnp.bfloat16)


def local(
    hidden,
    norm_gain,
    query_weight,
    key_weight,
    value_weight,
    out_weight,
    encodings,
    row_place,
    neighbour_ids,
    neighbour_counts,
):
    ctx_count = lax.axis_size("ctx")
    ctx_index = lax.axis_index("ctx")
    tok_dev = hidden.shape[0]
    rows_dev = encodings.shape[0]
    slice_tokens = encodings.shape[1]
    enc_width = encodings.shape[2]
    span_dev = tok_dev // CH
    head_width = query_weight.shape[1]
    head_count = head_width // HS
    slot_cap = -(-rows_dev // ctx_count)
    whole = lax.all_gather(hidden, "tp", axis=1, tiled=True)
    values_wide = whole.astype(jnp.float32)
    mean_square = jnp.mean(values_wide * values_wide, axis=1, keepdims=True)
    normed = (values_wide * lax.rsqrt(mean_square + epsilon) * norm_gain[None, :]).astype(
        jnp.bfloat16
    )
    query_full = lax.all_to_all(
        jnp.broadcast_to(query_weight[None], (ctx_count,) + query_weight.shape),
        "ctx",
        split_axis=0,
        concat_axis=0,
        tiled=True,
    ).reshape(-1, query_weight.shape[1])
    query_sum = jnp.dot(normed, query_full, preferred_element_type=jnp.float32)
    queries = (query_sum * HS ** (-0.5)).astype(jnp.bfloat16)
    storage = row_place[neighbour_ids.reshape(-1)].reshape(ctx_count, rows_dev)
    sources = storage // rows_dev
    local_rows = storage % rows_dev
    from_here = sources == ctx_index
    rank_position = jnp.cumsum(from_here.astype(jnp.int32), axis=1) - 1
    picked_rows = from_here & (rank_position == 0)
    pick_list = [jnp.sum(jnp.where(picked_rows, local_rows, 0), axis=1)]
    fill_list = [jnp.any(picked_rows, axis=1)]
    pick_index = jnp.stack(pick_list, axis=1)
    fill_mask = jnp.stack(fill_list, axis=1)
    outgoing = encodings[pick_index] * fill_mask[:, :, None, None].astype(jnp.bfloat16)
    incoming = lax.all_to_all(outgoing, "ctx", split_axis=0, concat_axis=0, tiled=True)
    own_sources = lax.dynamic_index_in_dim(sources, ctx_index, 0, keepdims=False)
    slot_order = jnp.arange(rows_dev)
    earlier = (own_sources[:, None] == own_sources[None, :]) & (
        slot_order[None, :] < slot_order[:, None]
    )
    own_rank = jnp.sum(earlier.astype(jnp.int32), axis=1)
    flat_index = own_sources * slot_cap + own_rank
    picked = incoming.reshape(ctx_count * slot_cap, slice_tokens, enc_width)[flat_index]
    row_total = picked.shape[0]
    full_rows = jnp.swapaxes(kernel_gather(picked, "tp", "ctx", 0), 0, 1).reshape(
        picked.shape[0], -1, picked.shape[2]
    )
    keys = project_rows(full_rows, key_weight).reshape(row_total, -1, head_width)
    values = project_rows(full_rows, value_weight).reshape(row_total, -1, head_width)
    neighbour_len = keys.shape[1]
    prior = shifted(
        jnp.stack([keys[row_total - KNB :], values[row_total - KNB :]]), "ctx", 1
    )
    key_blocks = jnp.concatenate([prior[0], keys], axis=0).reshape(
        span_dev + 1, KNB * neighbour_len, head_width
    )
    value_blocks = jnp.concatenate([prior[1], values], axis=0).reshape(
        span_dev + 1, KNB * neighbour_len, head_width
    )
    first_span = ctx_index * span_dev
    local_counts = lax.dynamic_slice_in_dim(neighbour_counts, first_span, span_dev)
    prior_count = lax.dynamic_slice_in_dim(neighbour_counts, jnp.maximum(first_span - 1, 0), 1)
    block_counts = jnp.concatenate([prior_count, local_counts], axis=0)
    padded = jnp.concatenate(
        [
            jnp.zeros((1, head_width), jnp.bfloat16),
            queries,
            jnp.zeros((CH - 1, head_width), jnp.bfloat16),
        ],
        axis=0,
    )
    query_blocks = padded.reshape(span_dev + 1, CH, head_width)
    slot_of_key = jnp.arange(KNB * neighbour_len) // neighbour_len
    live = slot_of_key[None, :] < block_counts[:, None]
    heads = []
    for head in range(head_count):
        lanes = slice(head * HS, (head + 1) * HS)
        scores = jnp.einsum(
            "wqd,wkd->wqk",
            query_blocks[:, :, lanes],
            key_blocks[:, :, lanes],
            preferred_element_type=jnp.float32,
        )
        scores = jnp.where(live[:, None, :], scores, masked_score)
        peak = jnp.max(scores, axis=2, keepdims=True)
        expos = jnp.exp(scores - peak)
        total = jnp.sum(expos, axis=2, keepdims=True)
        weights = expos.astype(jnp.bfloat16)
        blended = jnp.einsum(
            "wqk,wkd->wqd", weights, value_blocks[:, :, lanes], preferred_element_type=jnp.float32
        )
        heads.append(blended / total)
    blended = jnp.concatenate(heads, axis=2)
    blended = blended.reshape((span_dev + 1) * CH, head_width)[1 : tok_dev + 1]
    position = ctx_index * tok_dev + jnp.arange(tok_dev)
    valid = position % LENGTH >= CH - 1
    attended = jnp.where(valid[:, None], blended, jnp.zeros_like(blended)).astype(jnp.bfloat16)
    mixed_part = jnp.dot(attended, out_weight, preferred_element_type=jnp.float32).astype(
        jnp.bfloat16
    )
    return kernel_reduce_scatter(mixed_part, "tp", "ctx", 1)


def solution(mesh):
    return jax.shard_map(
        local,
        mesh=mesh,
        in_specs=(
            P("ctx", "tp"),
            P(),
            P("ctx", "tp"),
            P(None, "tp"),
            P(None, "tp"),
            P("tp", None),
            P("ctx", "tp", None),
            P(),
            P(),
            P(),
        ),
        out_specs=P(("ctx", "tp"), None),
        check_vma=False,
    )
```

```python
import functools

import jax
import jax.numpy as jnp
from jax import lax
from jax.experimental import pallas as pl
from jax.experimental.pallas import tpu as pltpu
from jax.sharding import PartitionSpec as P

HS = 128
CH = 64
KNB = 2
LENGTH = 8192


epsilon = 1e-05
masked_score = -1e30


def shifted(block, axis, distance):
    devices = range(lax.axis_size(axis))
    route = [(i - distance, i) for i in devices if i - distance in devices]
    return lax.ppermute(block, axis, route)


def greet_neighbours(me, row, count):
    right = lax.rem(me + 1, count)
    left = lax.rem(me + count - 1, count)
    barrier = pltpu.get_barrier_semaphore()
    for neighbour in (left, right):
        pl.semaphore_signal(
            barrier, inc=1, device_id=(row, neighbour), device_id_type=pl.DeviceIdType.MESH
        )
    pl.semaphore_wait(barrier, 2)
    return right, left


def ring_reach(count, piece, pieces):
    far = count // 2
    if count % 2 == 0 and piece >= pieces // 2:
        return (far - 1, far)
    return (far, count - 1 - far)


def ring_gather_kernel(x_ref, o_ref, send_sem, recv_sem, *, count, axis, other, pieces):
    me = lax.axis_index(axis)
    row = lax.axis_index(other)
    right, left = greet_neighbours(me, row, count)
    half = count // 2
    size = x_ref.shape[0] // pieces
    o_ref[half] = x_ref[...]
    copies = {}
    for step in range(1, half + 1):
        for piece in range(pieces):
            part = pl.ds(piece * size, size)
            reach = ring_reach(count, piece, pieces)
            for toward in (0, 1):
                if step > reach[toward]:
                    continue
                slot = (half - step) % count if toward == 0 else (half + step) % count
                source = (slot + 1) % count if toward == 0 else (slot - 1) % count
                if step > 1:
                    copies[(step - 1, toward, piece)].wait_recv()
                copy = pltpu.make_async_remote_copy(
                    src_ref=x_ref.at[part] if step == 1 else o_ref.at[source, part],
                    dst_ref=o_ref.at[slot, part],
                    send_sem=send_sem.at[toward, step - 1, piece],
                    recv_sem=recv_sem.at[toward, step - 1, piece],
                    device_id=(row, right if toward == 0 else left),
                    device_id_type=pl.DeviceIdType.MESH,
                )
                copy.start()
                copies[(step, toward, piece)] = copy
    for piece in range(pieces):
        reach = ring_reach(count, piece, pieces)
        copies[(reach[0], 0, piece)].wait_recv()
        copies[(reach[1], 1, piece)].wait_recv()
    for copy in copies.values():
        copy.wait_send()


def kernel_gather(block, axis, other, collective_id, pieces=4):
    count = lax.axis_size(axis)
    return pl.pallas_call(
        functools.partial(
            ring_gather_kernel, count=count, axis=axis, other=other, pieces=pieces
        ),
        out_shape=jax.ShapeDtypeStruct((count,) + block.shape, block.dtype),
        in_specs=[pl.BlockSpec(memory_space=pltpu.VMEM)],
        out_specs=pl.BlockSpec(memory_space=pltpu.VMEM),
        scratch_shapes=[
            pltpu.SemaphoreType.DMA((2, count // 2, pieces)),
            pltpu.SemaphoreType.DMA((2, count // 2, pieces)),
        ],
        compiler_params=pltpu.CompilerParams(collective_id=collective_id, has_side_effects=True),
    )(block)


def ring_sum_kernel(p_ref, o_ref, sums_in, sums_out, sems, *, count, axis, other, pieces):
    me = lax.axis_index(axis)
    row = lax.axis_index(other)
    right, left = greet_neighbours(me, row, count)
    width = p_ref.shape[2] // pieces

    def own(offset, part):
        return p_ref[lax.rem(me + offset + 2 * count, count), :, part].astype(jnp.float32)

    copies = {}
    for step in range(1, count // 2 + 1):
        for piece in range(pieces):
            part = pl.ds(piece * width, width)
            reach = ring_reach(count, piece, pieces)
            for toward in (0, 1):
                if step > reach[toward]:
                    continue
                if step == 1:
                    first = reach[0] if toward == 0 else count - reach[1]
                    source = p_ref.at[lax.rem(me + first, count), :, part]
                else:
                    copies[(step - 1, toward, piece)].wait_recv()
                    offset = reach[0] - step + 1 if toward == 0 else step - 1 - reach[1]
                    sums_out[toward, step - 2, :, part] = (
                        sums_in[toward, step - 2, :, part].astype(jnp.float32) + own(offset, part)
                    ).astype(sums_out.dtype)
                    source = sums_out.at[toward, step - 2, :, part]
                copy = pltpu.make_async_remote_copy(
                    src_ref=source,
                    dst_ref=sums_in.at[toward, step - 1, :, part],
                    send_sem=sems.at[0, toward, step - 1, piece],
                    recv_sem=sems.at[1, toward, step - 1, piece],
                    device_id=(row, right if toward == 0 else left),
                    device_id_type=pl.DeviceIdType.MESH,
                )
                copy.start()
                copies[(step, toward, piece)] = copy
    for piece in range(pieces):
        reach = ring_reach(count, piece, pieces)
        copies[(reach[0], 0, piece)].wait_recv()
        copies[(reach[1], 1, piece)].wait_recv()
    for copy in copies.values():
        copy.wait_send()
    for piece in range(pieces):
        part = pl.ds(piece * width, width)
        reach = ring_reach(count, piece, pieces)
        total = own(0, part) + sums_in[0, reach[0] - 1, :, part].astype(jnp.float32)
        total = total + sums_in[1, reach[1] - 1, :, part].astype(jnp.float32)
        o_ref[:, part] = total.astype(o_ref.dtype)


def kernel_reduce_scatter(partial, axis, other, collective_id, pieces=4):
    count = lax.axis_size(axis)
    blocks = partial.reshape((count, partial.shape[0] // count) + partial.shape[1:])
    block = blocks.shape[1:]
    reach = count // 2
    return pl.pallas_call(
        functools.partial(
            ring_sum_kernel, count=count, axis=axis, other=other, pieces=pieces
        ),
        out_shape=jax.ShapeDtypeStruct(block, partial.dtype),
        in_specs=[pl.BlockSpec(memory_space=pltpu.VMEM)],
        out_specs=pl.BlockSpec(memory_space=pltpu.VMEM),
        scratch_shapes=[
            pltpu.VMEM((2, reach) + block, partial.dtype),
            pltpu.VMEM((2, reach) + block, partial.dtype),
            pltpu.SemaphoreType.DMA((2, 2, reach, pieces)),
        ],
        compiler_params=pltpu.CompilerParams(collective_id=collective_id, has_side_effects=True),
    )(blocks)


def project_rows(rows, weight):
    flat = rows.reshape(-1, rows.shape[-1])
    return jnp.dot(flat, weight, preferred_element_type=jnp.float32).astype(jnp.bfloat16)


def local(
    hidden,
    norm_gain,
    query_weight,
    key_weight,
    value_weight,
    out_weight,
    encodings,
    row_place,
    neighbour_ids,
    neighbour_counts,
):
    ctx_count = lax.axis_size("ctx")
    ctx_index = lax.axis_index("ctx")
    tok_dev = hidden.shape[0]
    rows_dev = encodings.shape[0]
    slice_tokens = encodings.shape[1]
    enc_width = encodings.shape[2]
    span_dev = tok_dev // CH
    head_width = query_weight.shape[1]
    head_count = head_width // HS
    slot_cap = -(-rows_dev // ctx_count)
    whole = lax.all_gather(hidden, "tp", axis=1, tiled=True)
    values_wide = whole.astype(jnp.float32)
    mean_square = jnp.mean(values_wide * values_wide, axis=1, keepdims=True)
    normed = (values_wide * lax.rsqrt(mean_square + epsilon) * norm_gain[None, :]).astype(
        jnp.bfloat16
    )
    query_full = lax.all_to_all(
        jnp.broadcast_to(query_weight[None], (ctx_count,) + query_weight.shape),
        "ctx",
        split_axis=0,
        concat_axis=0,
        tiled=True,
    ).reshape(-1, query_weight.shape[1])
    query_sum = jnp.dot(normed, query_full, preferred_element_type=jnp.float32)
    queries = (query_sum * HS ** (-0.5)).astype(jnp.bfloat16)
    storage = row_place[neighbour_ids.reshape(-1)].reshape(ctx_count, rows_dev)
    sources = storage // rows_dev
    local_rows = storage % rows_dev
    from_here = sources == ctx_index
    rank_position = jnp.cumsum(from_here.astype(jnp.int32), axis=1) - 1
    picked_rows = from_here & (rank_position == 0)
    pick_list = [jnp.sum(jnp.where(picked_rows, local_rows, 0), axis=1)]
    fill_list = [jnp.any(picked_rows, axis=1)]
    pick_index = jnp.stack(pick_list, axis=1)
    fill_mask = jnp.stack(fill_list, axis=1)
    outgoing = encodings[pick_index] * fill_mask[:, :, None, None].astype(jnp.bfloat16)
    incoming = lax.all_to_all(outgoing, "ctx", split_axis=0, concat_axis=0, tiled=True)
    own_sources = lax.dynamic_index_in_dim(sources, ctx_index, 0, keepdims=False)
    slot_order = jnp.arange(rows_dev)
    earlier = (own_sources[:, None] == own_sources[None, :]) & (
        slot_order[None, :] < slot_order[:, None]
    )
    own_rank = jnp.sum(earlier.astype(jnp.int32), axis=1)
    flat_index = own_sources * slot_cap + own_rank
    picked = incoming.reshape(ctx_count * slot_cap, slice_tokens, enc_width)[flat_index]
    row_total = picked.shape[0]
    full_rows = jnp.swapaxes(kernel_gather(picked, "tp", "ctx", 0), 0, 1).reshape(
        picked.shape[0], -1, picked.shape[2]
    )
    keys = project_rows(full_rows, key_weight).reshape(row_total, -1, head_width)
    values = project_rows(full_rows, value_weight).reshape(row_total, -1, head_width)
    neighbour_len = keys.shape[1]
    prior = shifted(
        jnp.stack([keys[row_total - KNB :], values[row_total - KNB :]]), "ctx", 1
    )
    key_blocks = jnp.concatenate([prior[0], keys], axis=0).reshape(
        span_dev + 1, KNB * neighbour_len, head_width
    )
    value_blocks = jnp.concatenate([prior[1], values], axis=0).reshape(
        span_dev + 1, KNB * neighbour_len, head_width
    )
    first_span = ctx_index * span_dev
    local_counts = lax.dynamic_slice_in_dim(neighbour_counts, first_span, span_dev)
    prior_count = lax.dynamic_slice_in_dim(neighbour_counts, jnp.maximum(first_span - 1, 0), 1)
    block_counts = jnp.concatenate([prior_count, local_counts], axis=0)
    padded = jnp.concatenate(
        [
            jnp.zeros((1, head_width), jnp.bfloat16),
            queries,
            jnp.zeros((CH - 1, head_width), jnp.bfloat16),
        ],
        axis=0,
    )
    query_blocks = padded.reshape(span_dev + 1, CH, head_width)
    slot_of_key = jnp.arange(KNB * neighbour_len) // neighbour_len
    live = slot_of_key[None, :] < block_counts[:, None]
    heads = []
    for head in range(head_count):
        lanes = slice(head * HS, (head + 1) * HS)
        scores = jnp.einsum(
            "wqd,wkd->wqk",
            query_blocks[:, :, lanes],
            key_blocks[:, :, lanes],
            preferred_element_type=jnp.float32,
        )
        scores = jnp.where(live[:, None, :], scores, masked_score)
        peak = jnp.max(scores, axis=2, keepdims=True)
        expos = jnp.exp(scores - peak)
        total = jnp.sum(expos, axis=2, keepdims=True)
        weights = expos.astype(jnp.bfloat16)
        blended = jnp.einsum(
            "wqk,wkd->wqd", weights, value_blocks[:, :, lanes], preferred_element_type=jnp.float32
        )
        heads.append(blended / total)
    blended = jnp.concatenate(heads, axis=2)
    blended = blended.reshape((span_dev + 1) * CH, head_width)[1 : tok_dev + 1]
    position = ctx_index * tok_dev + jnp.arange(tok_dev)
    valid = position % LENGTH >= CH - 1
    attended = jnp.where(valid[:, None], blended, jnp.zeros_like(blended)).astype(jnp.bfloat16)
    mixed_part = jnp.dot(attended, out_weight, preferred_element_type=jnp.float32).astype(
        jnp.bfloat16
    )
    return kernel_reduce_scatter(mixed_part, "tp", "ctx", 1)


def solution(mesh):
    return jax.shard_map(
        local,
        mesh=mesh,
        in_specs=(
            P("ctx", "tp"),
            P(),
            P("ctx", "tp"),
            P(None, "tp"),
            P(None, "tp"),
            P("tp", None),
            P("ctx", "tp", None),
            P(),
            P(),
            P(),
        ),
        out_specs=P(("ctx", "tp"), None),
        check_vma=False,
    )
```

```python
import functools

import jax
import jax.numpy as jnp
from jax import lax
from jax.experimental import pallas as pl
from jax.experimental.pallas import tpu as pltpu
from jax.sharding import PartitionSpec as P

HS = 128
CH = 64
KNB = 2
LENGTH = 8192


epsilon = 1e-05
masked_score = -1e30


def shifted(block, axis, distance):
    devices = range(lax.axis_size(axis))
    route = [(i - distance, i) for i in devices if i - distance in devices]
    return lax.ppermute(block, axis, route)


def greet_neighbours(me, row, count):
    right = lax.rem(me + 1, count)
    left = lax.rem(me + count - 1, count)
    barrier = pltpu.get_barrier_semaphore()
    for neighbour in (left, right):
        pl.semaphore_signal(
            barrier, inc=1, device_id=(row, neighbour), device_id_type=pl.DeviceIdType.MESH
        )
    pl.semaphore_wait(barrier, 2)
    return right, left


def ring_reach(count, piece, pieces):
    far = count // 2
    if count % 2 == 0 and piece >= pieces // 2:
        return (far - 1, far)
    return (far, count - 1 - far)


def ring_gather_kernel(x_ref, o_ref, send_sem, recv_sem, *, count, axis, other, pieces):
    me = lax.axis_index(axis)
    row = lax.axis_index(other)
    right, left = greet_neighbours(me, row, count)
    half = count // 2
    size = x_ref.shape[0] // pieces
    o_ref[half] = x_ref[...]
    copies = {}
    for step in range(1, half + 1):
        for piece in range(pieces):
            part = pl.ds(piece * size, size)
            reach = ring_reach(count, piece, pieces)
            for toward in (0, 1):
                if step > reach[toward]:
                    continue
                slot = (half - step) % count if toward == 0 else (half + step) % count
                source = (slot + 1) % count if toward == 0 else (slot - 1) % count
                if step > 1:
                    copies[(step - 1, toward, piece)].wait_recv()
                copy = pltpu.make_async_remote_copy(
                    src_ref=x_ref.at[part] if step == 1 else o_ref.at[source, part],
                    dst_ref=o_ref.at[slot, part],
                    send_sem=send_sem.at[toward, step - 1, piece],
                    recv_sem=recv_sem.at[toward, step - 1, piece],
                    device_id=(row, right if toward == 0 else left),
                    device_id_type=pl.DeviceIdType.MESH,
                )
                copy.start()
                copies[(step, toward, piece)] = copy
    for piece in range(pieces):
        reach = ring_reach(count, piece, pieces)
        copies[(reach[0], 0, piece)].wait_recv()
        copies[(reach[1], 1, piece)].wait_recv()
    for copy in copies.values():
        copy.wait_send()


def kernel_gather(block, axis, other, collective_id, pieces=4):
    count = lax.axis_size(axis)
    return pl.pallas_call(
        functools.partial(
            ring_gather_kernel, count=count, axis=axis, other=other, pieces=pieces
        ),
        out_shape=jax.ShapeDtypeStruct((count,) + block.shape, block.dtype),
        in_specs=[pl.BlockSpec(memory_space=pltpu.VMEM)],
        out_specs=pl.BlockSpec(memory_space=pltpu.VMEM),
        scratch_shapes=[
            pltpu.SemaphoreType.DMA((2, count // 2, pieces)),
            pltpu.SemaphoreType.DMA((2, count // 2, pieces)),
        ],
        compiler_params=pltpu.CompilerParams(collective_id=collective_id, has_side_effects=True),
    )(block)


def ring_sum_kernel(p_ref, o_ref, sums_in, sums_out, sems, *, count, axis, other, pieces):
    me = lax.axis_index(axis)
    row = lax.axis_index(other)
    right, left = greet_neighbours(me, row, count)
    width = p_ref.shape[2] // pieces

    def own(offset, part):
        return p_ref[lax.rem(me + offset + 2 * count, count), :, part].astype(jnp.float32)

    copies = {}
    for step in range(1, count // 2 + 1):
        for piece in range(pieces):
            part = pl.ds(piece * width, width)
            reach = ring_reach(count, piece, pieces)
            for toward in (0, 1):
                if step > reach[toward]:
                    continue
                if step == 1:
                    first = reach[0] if toward == 0 else count - reach[1]
                    source = p_ref.at[lax.rem(me + first, count), :, part]
                else:
                    copies[(step - 1, toward, piece)].wait_recv()
                    offset = reach[0] - step + 1 if toward == 0 else step - 1 - reach[1]
                    sums_out[toward, step - 2, :, part] = (
                        sums_in[toward, step - 2, :, part].astype(jnp.float32) + own(offset, part)
                    ).astype(sums_out.dtype)
                    source = sums_out.at[toward, step - 2, :, part]
                copy = pltpu.make_async_remote_copy(
                    src_ref=source,
                    dst_ref=sums_in.at[toward, step - 1, :, part],
                    send_sem=sems.at[0, toward, step - 1, piece],
                    recv_sem=sems.at[1, toward, step - 1, piece],
                    device_id=(row, right if toward == 0 else left),
                    device_id_type=pl.DeviceIdType.MESH,
                )
                copy.start()
                copies[(step, toward, piece)] = copy
    for piece in range(pieces):
        reach = ring_reach(count, piece, pieces)
        copies[(reach[0], 0, piece)].wait_recv()
        copies[(reach[1], 1, piece)].wait_recv()
    for copy in copies.values():
        copy.wait_send()
    for piece in range(pieces):
        part = pl.ds(piece * width, width)
        reach = ring_reach(count, piece, pieces)
        total = own(0, part) + sums_in[0, reach[0] - 1, :, part].astype(jnp.float32)
        total = total + sums_in[1, reach[1] - 1, :, part].astype(jnp.float32)
        o_ref[:, part] = total.astype(o_ref.dtype)


def kernel_reduce_scatter(partial, axis, other, collective_id, pieces=4):
    count = lax.axis_size(axis)
    blocks = partial.reshape((count, partial.shape[0] // count) + partial.shape[1:])
    block = blocks.shape[1:]
    reach = count // 2
    return pl.pallas_call(
        functools.partial(
            ring_sum_kernel, count=count, axis=axis, other=other, pieces=pieces
        ),
        out_shape=jax.ShapeDtypeStruct(block, partial.dtype),
        in_specs=[pl.BlockSpec(memory_space=pltpu.VMEM)],
        out_specs=pl.BlockSpec(memory_space=pltpu.VMEM),
        scratch_shapes=[
            pltpu.VMEM((2, reach) + block, partial.dtype),
            pltpu.VMEM((2, reach) + block, partial.dtype),
            pltpu.SemaphoreType.DMA((2, 2, reach, pieces)),
        ],
        compiler_params=pltpu.CompilerParams(collective_id=collective_id, has_side_effects=True),
    )(blocks)


def project_rows(rows, weight):
    flat = rows.reshape(-1, rows.shape[-1])
    return jnp.dot(flat, weight, preferred_element_type=jnp.float32).astype(jnp.bfloat16)


def local(
    hidden,
    norm_gain,
    query_weight,
    key_weight,
    value_weight,
    out_weight,
    encodings,
    row_place,
    neighbour_ids,
    neighbour_counts,
):
    ctx_count = lax.axis_size("ctx")
    ctx_index = lax.axis_index("ctx")
    tok_dev = hidden.shape[0]
    rows_dev = encodings.shape[0]
    slice_tokens = encodings.shape[1]
    enc_width = encodings.shape[2]
    span_dev = tok_dev // CH
    head_width = query_weight.shape[1]
    head_count = head_width // HS
    slot_cap = -(-rows_dev // ctx_count)
    whole = lax.all_gather(hidden, "tp", axis=1, tiled=True)
    values_wide = whole.astype(jnp.float32)
    mean_square = jnp.mean(values_wide * values_wide, axis=1, keepdims=True)
    normed = (values_wide * lax.rsqrt(mean_square + epsilon) * norm_gain[None, :]).astype(
        jnp.bfloat16
    )
    query_full = lax.all_to_all(
        jnp.broadcast_to(query_weight[None], (ctx_count,) + query_weight.shape),
        "ctx",
        split_axis=0,
        concat_axis=0,
        tiled=True,
    ).reshape(-1, query_weight.shape[1])
    query_sum = jnp.dot(normed, query_full, preferred_element_type=jnp.float32)
    queries = (query_sum * HS ** (-0.5)).astype(jnp.bfloat16)
    matches = neighbour_ids.reshape(-1)[:, None] == jnp.arange(row_place.shape[0])[None, :]
    storage = jnp.sum(jnp.where(matches, row_place[None, :], 0), axis=1).reshape(
        ctx_count, rows_dev
    )
    sources = storage // rows_dev
    local_rows = storage % rows_dev
    from_here = sources == ctx_index
    rank_position = jnp.cumsum(from_here.astype(jnp.int32), axis=1) - 1
    picked_rows = from_here & (rank_position == 0)
    pick_list = [jnp.sum(jnp.where(picked_rows, local_rows, 0), axis=1)]
    fill_list = [jnp.any(picked_rows, axis=1)]
    pick_index = jnp.stack(pick_list, axis=1)
    fill_mask = jnp.stack(fill_list, axis=1)
    outgoing = encodings[pick_index] * fill_mask[:, :, None, None].astype(jnp.bfloat16)
    incoming = lax.all_to_all(outgoing, "ctx", split_axis=0, concat_axis=0, tiled=True)
    own_sources = lax.dynamic_index_in_dim(sources, ctx_index, 0, keepdims=False)
    slot_order = jnp.arange(rows_dev)
    earlier = (own_sources[:, None] == own_sources[None, :]) & (
        slot_order[None, :] < slot_order[:, None]
    )
    own_rank = jnp.sum(earlier.astype(jnp.int32), axis=1)
    flat_index = own_sources * slot_cap + own_rank
    picked = incoming.reshape(ctx_count * slot_cap, slice_tokens, enc_width)[flat_index]
    row_total = picked.shape[0]
    full_rows = jnp.swapaxes(kernel_gather(picked, "tp", "ctx", 0), 0, 1).reshape(
        picked.shape[0], -1, picked.shape[2]
    )
    keys = project_rows(full_rows, key_weight).reshape(row_total, -1, head_width)
    values = project_rows(full_rows, value_weight).reshape(row_total, -1, head_width)
    neighbour_len = keys.shape[1]
    prior = shifted(
        jnp.stack([keys[row_total - KNB :], values[row_total - KNB :]]), "ctx", 1
    )
    key_blocks = jnp.concatenate([prior[0], keys], axis=0).reshape(
        span_dev + 1, KNB * neighbour_len, head_width
    )
    value_blocks = jnp.concatenate([prior[1], values], axis=0).reshape(
        span_dev + 1, KNB * neighbour_len, head_width
    )
    first_span = ctx_index * span_dev
    local_counts = lax.dynamic_slice_in_dim(neighbour_counts, first_span, span_dev)
    prior_count = lax.dynamic_slice_in_dim(neighbour_counts, jnp.maximum(first_span - 1, 0), 1)
    block_counts = jnp.concatenate([prior_count, local_counts], axis=0)
    padded = jnp.concatenate(
        [
            jnp.zeros((1, head_width), jnp.bfloat16),
            queries,
            jnp.zeros((CH - 1, head_width), jnp.bfloat16),
        ],
        axis=0,
    )
    query_blocks = padded.reshape(span_dev + 1, CH, head_width)
    slot_of_key = jnp.arange(KNB * neighbour_len) // neighbour_len
    live = slot_of_key[None, :] < block_counts[:, None]
    heads = []
    for head in range(head_count):
        lanes = slice(head * HS, (head + 1) * HS)
        scores = jnp.einsum(
            "wqd,wkd->wqk",
            query_blocks[:, :, lanes],
            key_blocks[:, :, lanes],
            preferred_element_type=jnp.float32,
        )
        scores = jnp.where(live[:, None, :], scores, masked_score)
        peak = jnp.max(scores, axis=2, keepdims=True)
        expos = jnp.exp(scores - peak)
        total = jnp.sum(expos, axis=2, keepdims=True)
        weights = expos.astype(jnp.bfloat16)
        blended = jnp.einsum(
            "wqk,wkd->wqd", weights, value_blocks[:, :, lanes], preferred_element_type=jnp.float32
        )
        heads.append(blended / total)
    blended = jnp.concatenate(heads, axis=2)
    blended = blended.reshape((span_dev + 1) * CH, head_width)[1 : tok_dev + 1]
    position = ctx_index * tok_dev + jnp.arange(tok_dev)
    valid = position % LENGTH >= CH - 1
    attended = jnp.where(valid[:, None], blended, jnp.zeros_like(blended)).astype(jnp.bfloat16)
    mixed_part = jnp.dot(attended, out_weight, preferred_element_type=jnp.float32).astype(
        jnp.bfloat16
    )
    return kernel_reduce_scatter(mixed_part, "tp", "ctx", 1)


def solution(mesh):
    return jax.shard_map(
        local,
        mesh=mesh,
        in_specs=(
            P("ctx", "tp"),
            P(),
            P("ctx", "tp"),
            P(None, "tp"),
            P(None, "tp"),
            P("tp", None),
            P("ctx", "tp", None),
            P(),
            P(),
            P(),
        ),
        out_specs=P(("ctx", "tp"), None),
        check_vma=False,
    )
```

```python
import functools

import jax
import jax.numpy as jnp
from jax import lax
from jax.experimental import pallas as pl
from jax.experimental.pallas import tpu as pltpu
from jax.sharding import PartitionSpec as P

HS = 128
CH = 64
KNB = 2
LENGTH = 8192


epsilon = 1e-05
masked_score = -1e30


def shifted(block, axis, distance):
    devices = range(lax.axis_size(axis))
    route = [(i - distance, i) for i in devices if i - distance in devices]
    return lax.ppermute(block, axis, route)


def greet_neighbours(me, row, count):
    right = lax.rem(me + 1, count)
    left = lax.rem(me + count - 1, count)
    barrier = pltpu.get_barrier_semaphore()
    for neighbour in (left, right):
        pl.semaphore_signal(
            barrier, inc=1, device_id=(row, neighbour), device_id_type=pl.DeviceIdType.MESH
        )
    pl.semaphore_wait(barrier, 2)
    return right, left


def ring_reach(count, piece, pieces):
    far = count // 2
    if count % 2 == 0 and piece >= pieces // 2:
        return (far - 1, far)
    return (far, count - 1 - far)


def ring_gather_kernel(x_ref, o_ref, send_sem, recv_sem, *, count, axis, other, pieces):
    me = lax.axis_index(axis)
    row = lax.axis_index(other)
    right, left = greet_neighbours(me, row, count)
    half = count // 2
    size = x_ref.shape[0] // pieces
    o_ref[half] = x_ref[...]
    copies = {}
    for step in range(1, half + 1):
        for piece in range(pieces):
            part = pl.ds(piece * size, size)
            reach = ring_reach(count, piece, pieces)
            for toward in (0, 1):
                if step > reach[toward]:
                    continue
                slot = (half - step) % count if toward == 0 else (half + step) % count
                source = (slot + 1) % count if toward == 0 else (slot - 1) % count
                if step > 1:
                    copies[(step - 1, toward, piece)].wait_recv()
                copy = pltpu.make_async_remote_copy(
                    src_ref=x_ref.at[part] if step == 1 else o_ref.at[source, part],
                    dst_ref=o_ref.at[slot, part],
                    send_sem=send_sem.at[toward, step - 1, piece],
                    recv_sem=recv_sem.at[toward, step - 1, piece],
                    device_id=(row, right if toward == 0 else left),
                    device_id_type=pl.DeviceIdType.MESH,
                )
                copy.start()
                copies[(step, toward, piece)] = copy
    for piece in range(pieces):
        reach = ring_reach(count, piece, pieces)
        copies[(reach[0], 0, piece)].wait_recv()
        copies[(reach[1], 1, piece)].wait_recv()
    for copy in copies.values():
        copy.wait_send()


def kernel_gather(block, axis, other, collective_id, pieces=4):
    count = lax.axis_size(axis)
    return pl.pallas_call(
        functools.partial(
            ring_gather_kernel, count=count, axis=axis, other=other, pieces=pieces
        ),
        out_shape=jax.ShapeDtypeStruct((count,) + block.shape, block.dtype),
        in_specs=[pl.BlockSpec(memory_space=pltpu.VMEM)],
        out_specs=pl.BlockSpec(memory_space=pltpu.VMEM),
        scratch_shapes=[
            pltpu.SemaphoreType.DMA((2, count // 2, pieces)),
            pltpu.SemaphoreType.DMA((2, count // 2, pieces)),
        ],
        compiler_params=pltpu.CompilerParams(collective_id=collective_id, has_side_effects=True),
    )(block)


def ring_sum_kernel(p_ref, o_ref, sums_in, sums_out, sems, *, count, axis, other, pieces):
    me = lax.axis_index(axis)
    row = lax.axis_index(other)
    right, left = greet_neighbours(me, row, count)
    width = p_ref.shape[2] // pieces

    def own(offset, part):
        return p_ref[lax.rem(me + offset + 2 * count, count), :, part].astype(jnp.float32)

    copies = {}
    for step in range(1, count // 2 + 1):
        for piece in range(pieces):
            part = pl.ds(piece * width, width)
            reach = ring_reach(count, piece, pieces)
            for toward in (0, 1):
                if step > reach[toward]:
                    continue
                if step == 1:
                    first = reach[0] if toward == 0 else count - reach[1]
                    source = p_ref.at[lax.rem(me + first, count), :, part]
                else:
                    copies[(step - 1, toward, piece)].wait_recv()
                    offset = reach[0] - step + 1 if toward == 0 else step - 1 - reach[1]
                    sums_out[toward, step - 2, :, part] = (
                        sums_in[toward, step - 2, :, part].astype(jnp.float32) + own(offset, part)
                    ).astype(sums_out.dtype)
                    source = sums_out.at[toward, step - 2, :, part]
                copy = pltpu.make_async_remote_copy(
                    src_ref=source,
                    dst_ref=sums_in.at[toward, step - 1, :, part],
                    send_sem=sems.at[0, toward, step - 1, piece],
                    recv_sem=sems.at[1, toward, step - 1, piece],
                    device_id=(row, right if toward == 0 else left),
                    device_id_type=pl.DeviceIdType.MESH,
                )
                copy.start()
                copies[(step, toward, piece)] = copy
    for piece in range(pieces):
        reach = ring_reach(count, piece, pieces)
        copies[(reach[0], 0, piece)].wait_recv()
        copies[(reach[1], 1, piece)].wait_recv()
    for copy in copies.values():
        copy.wait_send()
    for piece in range(pieces):
        part = pl.ds(piece * width, width)
        reach = ring_reach(count, piece, pieces)
        for toward in (0, 1):
            o_ref[toward, :, part] = sums_in[toward, reach[toward] - 1, :, part]


def kernel_reduce_scatter(partial, axis, other, collective_id, pieces=4):
    count = lax.axis_size(axis)
    blocks = partial.reshape((count, partial.shape[0] // count) + partial.shape[1:])
    block = blocks.shape[1:]
    reach = count // 2
    arrived = pl.pallas_call(
        functools.partial(
            ring_sum_kernel, count=count, axis=axis, other=other, pieces=pieces
        ),
        out_shape=jax.ShapeDtypeStruct((2,) + block, partial.dtype),
        in_specs=[pl.BlockSpec(memory_space=pltpu.VMEM)],
        out_specs=pl.BlockSpec(memory_space=pltpu.VMEM),
        scratch_shapes=[
            pltpu.VMEM((2, reach) + block, partial.dtype),
            pltpu.VMEM((2, reach) + block, partial.dtype),
            pltpu.SemaphoreType.DMA((2, 2, reach, pieces)),
        ],
        compiler_params=pltpu.CompilerParams(collective_id=collective_id, has_side_effects=True),
    )(blocks)
    own = lax.dynamic_index_in_dim(blocks, lax.axis_index(axis), 0, keepdims=False)
    total = own.astype(jnp.float32) + arrived[0].astype(jnp.float32)
    return (total + arrived[1].astype(jnp.float32)).astype(partial.dtype)


def project_rows(rows, weight):
    flat = rows.reshape(-1, rows.shape[-1])
    return jnp.dot(flat, weight, preferred_element_type=jnp.float32).astype(jnp.bfloat16)


def local(
    hidden,
    norm_gain,
    query_weight,
    key_weight,
    value_weight,
    out_weight,
    encodings,
    row_place,
    neighbour_ids,
    neighbour_counts,
):
    ctx_count = lax.axis_size("ctx")
    ctx_index = lax.axis_index("ctx")
    tok_dev = hidden.shape[0]
    rows_dev = encodings.shape[0]
    slice_tokens = encodings.shape[1]
    enc_width = encodings.shape[2]
    span_dev = tok_dev // CH
    head_width = query_weight.shape[1]
    head_count = head_width // HS
    slot_cap = -(-rows_dev // ctx_count)
    whole = lax.all_gather(hidden, "tp", axis=1, tiled=True)
    values_wide = whole.astype(jnp.float32)
    mean_square = jnp.mean(values_wide * values_wide, axis=1, keepdims=True)
    normed = (values_wide * lax.rsqrt(mean_square + epsilon) * norm_gain[None, :]).astype(
        jnp.bfloat16
    )
    query_full = lax.all_to_all(
        jnp.broadcast_to(query_weight[None], (ctx_count,) + query_weight.shape),
        "ctx",
        split_axis=0,
        concat_axis=0,
        tiled=True,
    ).reshape(-1, query_weight.shape[1])
    query_sum = jnp.dot(normed, query_full, preferred_element_type=jnp.float32)
    queries = (query_sum * HS ** (-0.5)).astype(jnp.bfloat16)
    matches = neighbour_ids.reshape(-1)[:, None] == jnp.arange(row_place.shape[0])[None, :]
    storage = jnp.sum(jnp.where(matches, row_place[None, :], 0), axis=1).reshape(
        ctx_count, rows_dev
    )
    sources = storage // rows_dev
    local_rows = storage % rows_dev
    from_here = sources == ctx_index
    rank_position = jnp.cumsum(from_here.astype(jnp.int32), axis=1) - 1
    picked_rows = from_here & (rank_position == 0)
    pick_list = [jnp.sum(jnp.where(picked_rows, local_rows, 0), axis=1)]
    fill_list = [jnp.any(picked_rows, axis=1)]
    pick_index = jnp.stack(pick_list, axis=1)
    fill_mask = jnp.stack(fill_list, axis=1)
    outgoing = encodings[pick_index] * fill_mask[:, :, None, None].astype(jnp.bfloat16)
    incoming = lax.all_to_all(outgoing, "ctx", split_axis=0, concat_axis=0, tiled=True)
    own_sources = lax.dynamic_index_in_dim(sources, ctx_index, 0, keepdims=False)
    slot_order = jnp.arange(rows_dev)
    earlier = (own_sources[:, None] == own_sources[None, :]) & (
        slot_order[None, :] < slot_order[:, None]
    )
    own_rank = jnp.sum(earlier.astype(jnp.int32), axis=1)
    flat_index = own_sources * slot_cap + own_rank
    picked = incoming.reshape(ctx_count * slot_cap, slice_tokens, enc_width)[flat_index]
    row_total = picked.shape[0]
    full_rows = jnp.swapaxes(kernel_gather(picked, "tp", "ctx", 0), 0, 1).reshape(
        picked.shape[0], -1, picked.shape[2]
    )
    keys = project_rows(full_rows, key_weight).reshape(row_total, -1, head_width)
    values = project_rows(full_rows, value_weight).reshape(row_total, -1, head_width)
    neighbour_len = keys.shape[1]
    prior = shifted(
        jnp.stack([keys[row_total - KNB :], values[row_total - KNB :]]), "ctx", 1
    )
    key_blocks = jnp.concatenate([prior[0], keys], axis=0).reshape(
        span_dev + 1, KNB * neighbour_len, head_width
    )
    value_blocks = jnp.concatenate([prior[1], values], axis=0).reshape(
        span_dev + 1, KNB * neighbour_len, head_width
    )
    first_span = ctx_index * span_dev
    local_counts = lax.dynamic_slice_in_dim(neighbour_counts, first_span, span_dev)
    prior_count = lax.dynamic_slice_in_dim(neighbour_counts, jnp.maximum(first_span - 1, 0), 1)
    block_counts = jnp.concatenate([prior_count, local_counts], axis=0)
    padded = jnp.concatenate(
        [
            jnp.zeros((1, head_width), jnp.bfloat16),
            queries,
            jnp.zeros((CH - 1, head_width), jnp.bfloat16),
        ],
        axis=0,
    )
    query_blocks = padded.reshape(span_dev + 1, CH, head_width)
    slot_of_key = jnp.arange(KNB * neighbour_len) // neighbour_len
    live = slot_of_key[None, :] < block_counts[:, None]
    heads = []
    for head in range(head_count):
        lanes = slice(head * HS, (head + 1) * HS)
        scores = jnp.einsum(
            "wqd,wkd->wqk",
            query_blocks[:, :, lanes],
            key_blocks[:, :, lanes],
            preferred_element_type=jnp.float32,
        )
        scores = jnp.where(live[:, None, :], scores, masked_score)
        peak = jnp.max(scores, axis=2, keepdims=True)
        expos = jnp.exp(scores - peak)
        total = jnp.sum(expos, axis=2, keepdims=True)
        weights = expos.astype(jnp.bfloat16)
        blended = jnp.einsum(
            "wqk,wkd->wqd", weights, value_blocks[:, :, lanes], preferred_element_type=jnp.float32
        )
        heads.append(blended / total)
    blended = jnp.concatenate(heads, axis=2)
    blended = blended.reshape((span_dev + 1) * CH, head_width)[1 : tok_dev + 1]
    position = ctx_index * tok_dev + jnp.arange(tok_dev)
    valid = position % LENGTH >= CH - 1
    attended = jnp.where(valid[:, None], blended, jnp.zeros_like(blended)).astype(jnp.bfloat16)
    mixed_part = jnp.dot(attended, out_weight, preferred_element_type=jnp.float32).astype(
        jnp.bfloat16
    )
    return kernel_reduce_scatter(mixed_part, "tp", "ctx", 1)


def solution(mesh):
    return jax.shard_map(
        local,
        mesh=mesh,
        in_specs=(
            P("ctx", "tp"),
            P(),
            P("ctx", "tp"),
            P(None, "tp"),
            P(None, "tp"),
            P("tp", None),
            P("ctx", "tp", None),
            P(),
            P(),
            P(),
        ),
        out_specs=P(("ctx", "tp"), None),
        check_vma=False,
    )
```

```python
import functools

import jax
import jax.numpy as jnp
from jax import lax
from jax.experimental import pallas as pl
from jax.experimental.pallas import tpu as pltpu
from jax.sharding import PartitionSpec as P

HS = 128
CH = 64
KNB = 2
LENGTH = 8192


epsilon = 1e-05
masked_score = -1e30


def shifted(block, axis, distance):
    devices = range(lax.axis_size(axis))
    route = [(i - distance, i) for i in devices if i - distance in devices]
    return lax.ppermute(block, axis, route)


def greet_neighbours(me, row, count):
    right = lax.rem(me + 1, count)
    left = lax.rem(me + count - 1, count)
    barrier = pltpu.get_barrier_semaphore()
    for neighbour in (left, right):
        pl.semaphore_signal(
            barrier, inc=1, device_id=(row, neighbour), device_id_type=pl.DeviceIdType.MESH
        )
    pl.semaphore_wait(barrier, 2)
    return right, left


def ring_reach(count, piece, pieces):
    far = count // 2
    if count % 2 == 0 and piece >= pieces // 2:
        return (far - 1, far)
    return (far, count - 1 - far)


def ring_gather_kernel(x_ref, o_ref, send_sem, recv_sem, *, count, axis, other, pieces):
    me = lax.axis_index(axis)
    row = lax.axis_index(other)
    right, left = greet_neighbours(me, row, count)
    half = count // 2
    size = x_ref.shape[0] // pieces
    o_ref[half] = x_ref[...]
    copies = {}
    for step in range(1, half + 1):
        for piece in range(pieces):
            part = pl.ds(piece * size, size)
            reach = ring_reach(count, piece, pieces)
            for toward in (0, 1):
                if step > reach[toward]:
                    continue
                slot = (half - step) % count if toward == 0 else (half + step) % count
                source = (slot + 1) % count if toward == 0 else (slot - 1) % count
                if step > 1:
                    copies[(step - 1, toward, piece)].wait_recv()
                copy = pltpu.make_async_remote_copy(
                    src_ref=x_ref.at[part] if step == 1 else o_ref.at[source, part],
                    dst_ref=o_ref.at[slot, part],
                    send_sem=send_sem.at[toward, step - 1, piece],
                    recv_sem=recv_sem.at[toward, step - 1, piece],
                    device_id=(row, right if toward == 0 else left),
                    device_id_type=pl.DeviceIdType.MESH,
                )
                copy.start()
                copies[(step, toward, piece)] = copy
    for piece in range(pieces):
        reach = ring_reach(count, piece, pieces)
        copies[(reach[0], 0, piece)].wait_recv()
        copies[(reach[1], 1, piece)].wait_recv()
    for copy in copies.values():
        copy.wait_send()


def kernel_gather(block, axis, other, collective_id, pieces=4):
    count = lax.axis_size(axis)
    return pl.pallas_call(
        functools.partial(
            ring_gather_kernel, count=count, axis=axis, other=other, pieces=pieces
        ),
        out_shape=jax.ShapeDtypeStruct((count,) + block.shape, block.dtype),
        in_specs=[pl.BlockSpec(memory_space=pltpu.VMEM)],
        out_specs=pl.BlockSpec(memory_space=pltpu.VMEM),
        scratch_shapes=[
            pltpu.SemaphoreType.DMA((2, count // 2, pieces)),
            pltpu.SemaphoreType.DMA((2, count // 2, pieces)),
        ],
        compiler_params=pltpu.CompilerParams(collective_id=collective_id, has_side_effects=True),
    )(block)


def ring_sum_kernel(p_ref, o_ref, sums_in, sums_out, sems, *, count, axis, other, pieces):
    me = lax.axis_index(axis)
    row = lax.axis_index(other)
    right, left = greet_neighbours(me, row, count)
    width = p_ref.shape[2] // pieces

    def own(offset, part):
        return p_ref[lax.rem(me + offset + 2 * count, count), :, part].astype(jnp.float32)

    copies = {}
    for step in range(1, count // 2 + 1):
        for piece in range(pieces):
            part = pl.ds(piece * width, width)
            reach = ring_reach(count, piece, pieces)
            for toward in (0, 1):
                if step > reach[toward]:
                    continue
                if step == 1:
                    first = reach[0] if toward == 0 else count - reach[1]
                    source = p_ref.at[lax.rem(me + first, count), :, part]
                else:
                    copies[(step - 1, toward, piece)].wait_recv()
                    offset = reach[0] - step + 1 if toward == 0 else step - 1 - reach[1]
                    sums_out[toward, step - 2, :, part] = (
                        sums_in[toward, step - 2, :, part].astype(jnp.float32) + own(offset, part)
                    ).astype(sums_out.dtype)
                    source = sums_out.at[toward, step - 2, :, part]
                copy = pltpu.make_async_remote_copy(
                    src_ref=source,
                    dst_ref=sums_in.at[toward, step - 1, :, part],
                    send_sem=sems.at[0, toward, step - 1, piece],
                    recv_sem=sems.at[1, toward, step - 1, piece],
                    device_id=(row, right if toward == 0 else left),
                    device_id_type=pl.DeviceIdType.MESH,
                )
                copy.start()
                copies[(step, toward, piece)] = copy
    for piece in range(pieces):
        reach = ring_reach(count, piece, pieces)
        copies[(reach[0], 0, piece)].wait_recv()
        copies[(reach[1], 1, piece)].wait_recv()
    for copy in copies.values():
        copy.wait_send()
    for piece in range(pieces):
        part = pl.ds(piece * width, width)
        reach = ring_reach(count, piece, pieces)
        total = own(0, part) + sums_in[0, reach[0] - 1, :, part].astype(jnp.float32)
        total = total + sums_in[1, reach[1] - 1, :, part].astype(jnp.float32)
        o_ref[:, part] = total.astype(o_ref.dtype)


def kernel_reduce_scatter(partial, axis, other, collective_id, pieces=4):
    count = lax.axis_size(axis)
    blocks = partial.reshape((count, partial.shape[0] // count) + partial.shape[1:])
    block = blocks.shape[1:]
    reach = count // 2
    return pl.pallas_call(
        functools.partial(
            ring_sum_kernel, count=count, axis=axis, other=other, pieces=pieces
        ),
        out_shape=jax.ShapeDtypeStruct(block, partial.dtype),
        in_specs=[pl.BlockSpec(memory_space=pltpu.VMEM)],
        out_specs=pl.BlockSpec(memory_space=pltpu.VMEM),
        scratch_shapes=[
            pltpu.VMEM((2, reach) + block, partial.dtype),
            pltpu.VMEM((2, reach) + block, partial.dtype),
            pltpu.SemaphoreType.DMA((2, 2, reach, pieces)),
        ],
        compiler_params=pltpu.CompilerParams(collective_id=collective_id, has_side_effects=True),
    )(blocks)


def project_rows(rows, weight):
    flat = rows.reshape(-1, rows.shape[-1])
    return jnp.dot(flat, weight, preferred_element_type=jnp.float32).astype(jnp.bfloat16)


def local(
    hidden,
    norm_gain,
    query_weight,
    key_weight,
    value_weight,
    out_weight,
    encodings,
    row_place,
    neighbour_ids,
    neighbour_counts,
):
    ctx_count = lax.axis_size("ctx")
    ctx_index = lax.axis_index("ctx")
    tok_dev = hidden.shape[0]
    rows_dev = encodings.shape[0]
    slice_tokens = encodings.shape[1]
    enc_width = encodings.shape[2]
    span_dev = tok_dev // CH
    head_width = query_weight.shape[1]
    head_count = head_width // HS
    slot_cap = -(-rows_dev // ctx_count)
    local_wide = hidden.astype(jnp.float32)
    square_parts = lax.all_gather(jnp.sum(local_wide * local_wide, axis=1), "tp", axis=1)
    whole = lax.all_gather(hidden, "tp", axis=1, tiled=True)
    values_wide = whole.astype(jnp.float32)
    mean_square = jnp.sum(square_parts, axis=1, keepdims=True) / whole.shape[1]
    normed = (values_wide * lax.rsqrt(mean_square + epsilon) * norm_gain[None, :]).astype(
        jnp.bfloat16
    )
    query_full = lax.all_to_all(
        jnp.broadcast_to(query_weight[None], (ctx_count,) + query_weight.shape),
        "ctx",
        split_axis=0,
        concat_axis=0,
        tiled=True,
    ).reshape(-1, query_weight.shape[1])
    query_sum = jnp.dot(normed, query_full, preferred_element_type=jnp.float32)
    queries = (query_sum * HS ** (-0.5)).astype(jnp.bfloat16)
    matches = neighbour_ids.reshape(-1)[:, None] == jnp.arange(row_place.shape[0])[None, :]
    storage = jnp.sum(jnp.where(matches, row_place[None, :], 0), axis=1).reshape(
        ctx_count, rows_dev
    )
    sources = storage // rows_dev
    local_rows = storage % rows_dev
    from_here = sources == ctx_index
    rank_position = jnp.cumsum(from_here.astype(jnp.int32), axis=1) - 1
    picked_rows = from_here & (rank_position == 0)
    pick_list = [jnp.sum(jnp.where(picked_rows, local_rows, 0), axis=1)]
    fill_list = [jnp.any(picked_rows, axis=1)]
    pick_index = jnp.stack(pick_list, axis=1)
    fill_mask = jnp.stack(fill_list, axis=1)
    outgoing = encodings[pick_index] * fill_mask[:, :, None, None].astype(jnp.bfloat16)
    incoming = lax.all_to_all(outgoing, "ctx", split_axis=0, concat_axis=0, tiled=True)
    own_sources = lax.dynamic_index_in_dim(sources, ctx_index, 0, keepdims=False)
    slot_order = jnp.arange(rows_dev)
    earlier = (own_sources[:, None] == own_sources[None, :]) & (
        slot_order[None, :] < slot_order[:, None]
    )
    own_rank = jnp.sum(earlier.astype(jnp.int32), axis=1)
    flat_index = own_sources * slot_cap + own_rank
    picked = incoming.reshape(ctx_count * slot_cap, slice_tokens, enc_width)[flat_index]
    row_total = picked.shape[0]
    full_rows = jnp.swapaxes(kernel_gather(picked, "tp", "ctx", 0), 0, 1).reshape(
        picked.shape[0], -1, picked.shape[2]
    )
    keys = project_rows(full_rows, key_weight).reshape(row_total, -1, head_width)
    values = project_rows(full_rows, value_weight).reshape(row_total, -1, head_width)
    neighbour_len = keys.shape[1]
    prior = shifted(
        jnp.stack([keys[row_total - KNB :], values[row_total - KNB :]]), "ctx", 1
    )
    key_blocks = jnp.concatenate([prior[0], keys], axis=0).reshape(
        span_dev + 1, KNB * neighbour_len, head_width
    )
    value_blocks = jnp.concatenate([prior[1], values], axis=0).reshape(
        span_dev + 1, KNB * neighbour_len, head_width
    )
    first_span = ctx_index * span_dev
    local_counts = lax.dynamic_slice_in_dim(neighbour_counts, first_span, span_dev)
    prior_count = lax.dynamic_slice_in_dim(neighbour_counts, jnp.maximum(first_span - 1, 0), 1)
    block_counts = jnp.concatenate([prior_count, local_counts], axis=0)
    padded = jnp.concatenate(
        [
            jnp.zeros((1, head_width), jnp.bfloat16),
            queries,
            jnp.zeros((CH - 1, head_width), jnp.bfloat16),
        ],
        axis=0,
    )
    query_blocks = padded.reshape(span_dev + 1, CH, head_width)
    slot_of_key = jnp.arange(KNB * neighbour_len) // neighbour_len
    live = slot_of_key[None, :] < block_counts[:, None]
    heads = []
    for head in range(head_count):
        lanes = slice(head * HS, (head + 1) * HS)
        scores = jnp.einsum(
            "wqd,wkd->wqk",
            query_blocks[:, :, lanes],
            key_blocks[:, :, lanes],
            preferred_element_type=jnp.float32,
        )
        scores = jnp.where(live[:, None, :], scores, masked_score)
        peak = jnp.max(scores, axis=2, keepdims=True)
        expos = jnp.exp(scores - peak)
        total = jnp.sum(expos, axis=2, keepdims=True)
        weights = expos.astype(jnp.bfloat16)
        blended = jnp.einsum(
            "wqk,wkd->wqd", weights, value_blocks[:, :, lanes], preferred_element_type=jnp.float32
        )
        heads.append(blended / total)
    blended = jnp.concatenate(heads, axis=2)
    blended = blended.reshape((span_dev + 1) * CH, head_width)[1 : tok_dev + 1]
    position = ctx_index * tok_dev + jnp.arange(tok_dev)
    valid = position % LENGTH >= CH - 1
    attended = jnp.where(valid[:, None], blended, jnp.zeros_like(blended)).astype(jnp.bfloat16)
    mixed_part = jnp.dot(attended, out_weight, preferred_element_type=jnp.float32).astype(
        jnp.bfloat16
    )
    return kernel_reduce_scatter(mixed_part, "tp", "ctx", 1)


def solution(mesh):
    return jax.shard_map(
        local,
        mesh=mesh,
        in_specs=(
            P("ctx", "tp"),
            P(),
            P("ctx", "tp"),
            P(None, "tp"),
            P(None, "tp"),
            P("tp", None),
            P("ctx", "tp", None),
            P(),
            P(),
            P(),
        ),
        out_specs=P(("ctx", "tp"), None),
        check_vma=False,
    )
```

```python
import functools

import jax
import jax.numpy as jnp
from jax import lax
from jax.experimental import pallas as pl
from jax.experimental.pallas import tpu as pltpu
from jax.sharding import PartitionSpec as P

HS = 128
CH = 64
KNB = 2
LENGTH = 8192


epsilon = 1e-05
masked_score = -1e30


def shifted(block, axis, distance):
    devices = range(lax.axis_size(axis))
    route = [(i - distance, i) for i in devices if i - distance in devices]
    return lax.ppermute(block, axis, route)


def greet_neighbours(me, row, count):
    right = lax.rem(me + 1, count)
    left = lax.rem(me + count - 1, count)
    barrier = pltpu.get_barrier_semaphore()
    for neighbour in (left, right):
        pl.semaphore_signal(
            barrier, inc=1, device_id=(row, neighbour), device_id_type=pl.DeviceIdType.MESH
        )
    pl.semaphore_wait(barrier, 2)
    return right, left


def ring_reach(count, piece, pieces):
    far = count // 2
    if count % 2 == 0 and piece >= pieces // 2:
        return (far - 1, far)
    return (far, count - 1 - far)


def ring_gather_kernel(x_ref, o_ref, send_sem, recv_sem, *, count, axis, other, pieces):
    me = lax.axis_index(axis)
    row = lax.axis_index(other)
    right, left = greet_neighbours(me, row, count)
    half = count // 2
    size = x_ref.shape[0] // pieces
    o_ref[half] = x_ref[...]
    copies = {}
    for step in range(1, half + 1):
        for piece in range(pieces):
            part = pl.ds(piece * size, size)
            reach = ring_reach(count, piece, pieces)
            for toward in (0, 1):
                if step > reach[toward]:
                    continue
                slot = (half - step) % count if toward == 0 else (half + step) % count
                source = (slot + 1) % count if toward == 0 else (slot - 1) % count
                if step > 1:
                    copies[(step - 1, toward, piece)].wait_recv()
                copy = pltpu.make_async_remote_copy(
                    src_ref=x_ref.at[part] if step == 1 else o_ref.at[source, part],
                    dst_ref=o_ref.at[slot, part],
                    send_sem=send_sem.at[toward, step - 1, piece],
                    recv_sem=recv_sem.at[toward, step - 1, piece],
                    device_id=(row, right if toward == 0 else left),
                    device_id_type=pl.DeviceIdType.MESH,
                )
                copy.start()
                copies[(step, toward, piece)] = copy
    for piece in range(pieces):
        reach = ring_reach(count, piece, pieces)
        copies[(reach[0], 0, piece)].wait_recv()
        copies[(reach[1], 1, piece)].wait_recv()
    for copy in copies.values():
        copy.wait_send()


def kernel_gather(block, axis, other, collective_id, pieces=4):
    count = lax.axis_size(axis)
    return pl.pallas_call(
        functools.partial(
            ring_gather_kernel, count=count, axis=axis, other=other, pieces=pieces
        ),
        out_shape=jax.ShapeDtypeStruct((count,) + block.shape, block.dtype),
        in_specs=[pl.BlockSpec(memory_space=pltpu.VMEM)],
        out_specs=pl.BlockSpec(memory_space=pltpu.VMEM),
        scratch_shapes=[
            pltpu.SemaphoreType.DMA((2, count // 2, pieces)),
            pltpu.SemaphoreType.DMA((2, count // 2, pieces)),
        ],
        compiler_params=pltpu.CompilerParams(collective_id=collective_id, has_side_effects=True),
    )(block)


def ring_sum_kernel(p_ref, o_ref, sums_in, sums_out, sems, *, count, axis, other, pieces):
    me = lax.axis_index(axis)
    row = lax.axis_index(other)
    right, left = greet_neighbours(me, row, count)
    width = p_ref.shape[2] // pieces

    def own(offset, part):
        return p_ref[lax.rem(me + offset + 2 * count, count), :, part].astype(jnp.float32)

    copies = {}
    for step in range(1, count // 2 + 1):
        for piece in range(pieces):
            part = pl.ds(piece * width, width)
            reach = ring_reach(count, piece, pieces)
            for toward in (0, 1):
                if step > reach[toward]:
                    continue
                if step == 1:
                    first = reach[0] if toward == 0 else count - reach[1]
                    source = p_ref.at[lax.rem(me + first, count), :, part]
                else:
                    copies[(step - 1, toward, piece)].wait_recv()
                    offset = reach[0] - step + 1 if toward == 0 else step - 1 - reach[1]
                    sums_out[toward, step - 2, :, part] = (
                        sums_in[toward, step - 2, :, part].astype(jnp.float32) + own(offset, part)
                    ).astype(sums_out.dtype)
                    source = sums_out.at[toward, step - 2, :, part]
                copy = pltpu.make_async_remote_copy(
                    src_ref=source,
                    dst_ref=sums_in.at[toward, step - 1, :, part],
                    send_sem=sems.at[0, toward, step - 1, piece],
                    recv_sem=sems.at[1, toward, step - 1, piece],
                    device_id=(row, right if toward == 0 else left),
                    device_id_type=pl.DeviceIdType.MESH,
                )
                copy.start()
                copies[(step, toward, piece)] = copy
    for piece in range(pieces):
        reach = ring_reach(count, piece, pieces)
        copies[(reach[0], 0, piece)].wait_recv()
        copies[(reach[1], 1, piece)].wait_recv()
    for copy in copies.values():
        copy.wait_send()
    for piece in range(pieces):
        part = pl.ds(piece * width, width)
        reach = ring_reach(count, piece, pieces)
        total = own(0, part) + sums_in[0, reach[0] - 1, :, part].astype(jnp.float32)
        total = total + sums_in[1, reach[1] - 1, :, part].astype(jnp.float32)
        o_ref[:, part] = total.astype(o_ref.dtype)


def kernel_reduce_scatter(partial, axis, other, collective_id, pieces=4):
    count = lax.axis_size(axis)
    blocks = partial.reshape((count, partial.shape[0] // count) + partial.shape[1:])
    block = blocks.shape[1:]
    reach = count // 2
    return pl.pallas_call(
        functools.partial(
            ring_sum_kernel, count=count, axis=axis, other=other, pieces=pieces
        ),
        out_shape=jax.ShapeDtypeStruct(block, partial.dtype),
        in_specs=[pl.BlockSpec(memory_space=pltpu.VMEM)],
        out_specs=pl.BlockSpec(memory_space=pltpu.VMEM),
        scratch_shapes=[
            pltpu.VMEM((2, reach) + block, partial.dtype),
            pltpu.VMEM((2, reach) + block, partial.dtype),
            pltpu.SemaphoreType.DMA((2, 2, reach, pieces)),
        ],
        compiler_params=pltpu.CompilerParams(collective_id=collective_id, has_side_effects=True),
    )(blocks)


def project_rows(rows, weight):
    flat = rows.reshape(-1, rows.shape[-1])
    return jnp.dot(flat, weight, preferred_element_type=jnp.float32).astype(jnp.bfloat16)


def local(
    hidden,
    norm_gain,
    query_weight,
    key_weight,
    value_weight,
    out_weight,
    encodings,
    row_place,
    neighbour_ids,
    neighbour_counts,
):
    ctx_count = lax.axis_size("ctx")
    ctx_index = lax.axis_index("ctx")
    tok_dev = hidden.shape[0]
    rows_dev = encodings.shape[0]
    slice_tokens = encodings.shape[1]
    enc_width = encodings.shape[2]
    span_dev = tok_dev // CH
    head_width = query_weight.shape[1]
    head_count = head_width // HS
    slot_cap = -(-rows_dev // ctx_count)
    whole = lax.all_gather(hidden, "tp", axis=1, tiled=True)
    values_wide = whole.astype(jnp.float32)
    mean_square = jnp.mean(values_wide * values_wide, axis=1, keepdims=True)
    normed = (values_wide * lax.rsqrt(mean_square + epsilon) * norm_gain[None, :]).astype(
        jnp.bfloat16
    )
    query_full = lax.all_to_all(
        jnp.broadcast_to(query_weight[None], (ctx_count,) + query_weight.shape),
        "ctx",
        split_axis=0,
        concat_axis=0,
        tiled=True,
    ).reshape(-1, query_weight.shape[1])
    query_sum = jnp.dot(normed, query_full, preferred_element_type=jnp.float32)
    queries = (query_sum * HS ** (-0.5)).astype(jnp.bfloat16)
    matches = neighbour_ids.reshape(-1)[:, None] == jnp.arange(row_place.shape[0])[None, :]
    storage = jnp.sum(jnp.where(matches, row_place[None, :], 0), axis=1).reshape(
        ctx_count, rows_dev
    )
    sources = storage // rows_dev
    local_rows = storage % rows_dev
    from_here = sources == ctx_index
    rank_position = jnp.cumsum(from_here.astype(jnp.int32), axis=1) - 1
    picked_rows = from_here & (rank_position == 0)
    pick_list = [jnp.sum(jnp.where(picked_rows, local_rows, 0), axis=1)]
    fill_list = [jnp.any(picked_rows, axis=1)]
    pick_index = jnp.stack(pick_list, axis=1)
    fill_mask = jnp.stack(fill_list, axis=1)
    outgoing = encodings[pick_index] * fill_mask[:, :, None, None].astype(jnp.bfloat16)
    incoming = lax.all_to_all(outgoing, "ctx", split_axis=0, concat_axis=0, tiled=True)
    own_sources = lax.dynamic_index_in_dim(sources, ctx_index, 0, keepdims=False)
    slot_order = jnp.arange(rows_dev)
    earlier = (own_sources[:, None] == own_sources[None, :]) & (
        slot_order[None, :] < slot_order[:, None]
    )
    own_rank = jnp.sum(earlier.astype(jnp.int32), axis=1)
    flat_index = own_sources * slot_cap + own_rank
    picked = incoming.reshape(ctx_count * slot_cap, slice_tokens, enc_width)[flat_index]
    row_total = picked.shape[0]
    full_rows = jnp.swapaxes(kernel_gather(picked, "tp", "ctx", 0, pieces=2), 0, 1).reshape(
        picked.shape[0], -1, picked.shape[2]
    )
    keys = project_rows(full_rows, key_weight).reshape(row_total, -1, head_width)
    values = project_rows(full_rows, value_weight).reshape(row_total, -1, head_width)
    neighbour_len = keys.shape[1]
    prior = shifted(
        jnp.stack([keys[row_total - KNB :], values[row_total - KNB :]]), "ctx", 1
    )
    key_blocks = jnp.concatenate([prior[0], keys], axis=0).reshape(
        span_dev + 1, KNB * neighbour_len, head_width
    )
    value_blocks = jnp.concatenate([prior[1], values], axis=0).reshape(
        span_dev + 1, KNB * neighbour_len, head_width
    )
    first_span = ctx_index * span_dev
    local_counts = lax.dynamic_slice_in_dim(neighbour_counts, first_span, span_dev)
    prior_count = lax.dynamic_slice_in_dim(neighbour_counts, jnp.maximum(first_span - 1, 0), 1)
    block_counts = jnp.concatenate([prior_count, local_counts], axis=0)
    padded = jnp.concatenate(
        [
            jnp.zeros((1, head_width), jnp.bfloat16),
            queries,
            jnp.zeros((CH - 1, head_width), jnp.bfloat16),
        ],
        axis=0,
    )
    query_blocks = padded.reshape(span_dev + 1, CH, head_width)
    slot_of_key = jnp.arange(KNB * neighbour_len) // neighbour_len
    live = slot_of_key[None, :] < block_counts[:, None]
    heads = []
    for head in range(head_count):
        lanes = slice(head * HS, (head + 1) * HS)
        scores = jnp.einsum(
            "wqd,wkd->wqk",
            query_blocks[:, :, lanes],
            key_blocks[:, :, lanes],
            preferred_element_type=jnp.float32,
        )
        scores = jnp.where(live[:, None, :], scores, masked_score)
        peak = jnp.max(scores, axis=2, keepdims=True)
        expos = jnp.exp(scores - peak)
        total = jnp.sum(expos, axis=2, keepdims=True)
        weights = expos.astype(jnp.bfloat16)
        blended = jnp.einsum(
            "wqk,wkd->wqd", weights, value_blocks[:, :, lanes], preferred_element_type=jnp.float32
        )
        heads.append(blended / total)
    blended = jnp.concatenate(heads, axis=2)
    blended = blended.reshape((span_dev + 1) * CH, head_width)[1 : tok_dev + 1]
    position = ctx_index * tok_dev + jnp.arange(tok_dev)
    valid = position % LENGTH >= CH - 1
    attended = jnp.where(valid[:, None], blended, jnp.zeros_like(blended)).astype(jnp.bfloat16)
    mixed_part = jnp.dot(attended, out_weight, preferred_element_type=jnp.float32).astype(
        jnp.bfloat16
    )
    return kernel_reduce_scatter(mixed_part, "tp", "ctx", 1)


def solution(mesh):
    return jax.shard_map(
        local,
        mesh=mesh,
        in_specs=(
            P("ctx", "tp"),
            P(),
            P("ctx", "tp"),
            P(None, "tp"),
            P(None, "tp"),
            P("tp", None),
            P("ctx", "tp", None),
            P(),
            P(),
            P(),
        ),
        out_specs=P(("ctx", "tp"), None),
        check_vma=False,
    )
```

```python
import functools

import jax
import jax.numpy as jnp
from jax import lax
from jax.experimental import pallas as pl
from jax.experimental.pallas import tpu as pltpu
from jax.sharding import PartitionSpec as P

HS = 128
CH = 64
KNB = 2
LENGTH = 8192


epsilon = 1e-05
masked_score = -1e30


def shifted(block, axis, distance):
    devices = range(lax.axis_size(axis))
    route = [(i - distance, i) for i in devices if i - distance in devices]
    return lax.ppermute(block, axis, route)


def greet_neighbours(me, row, count):
    right = lax.rem(me + 1, count)
    left = lax.rem(me + count - 1, count)
    barrier = pltpu.get_barrier_semaphore()
    for neighbour in (left, right):
        pl.semaphore_signal(
            barrier, inc=1, device_id=(row, neighbour), device_id_type=pl.DeviceIdType.MESH
        )
    pl.semaphore_wait(barrier, 2)
    return right, left


def ring_reach(count, piece, pieces):
    far = count // 2
    if count % 2 == 0 and piece >= pieces // 2:
        return (far - 1, far)
    return (far, count - 1 - far)


def ring_gather_kernel(x_ref, o_ref, send_sem, recv_sem, *, count, axis, other, pieces):
    me = lax.axis_index(axis)
    row = lax.axis_index(other)
    right, left = greet_neighbours(me, row, count)
    half = count // 2
    size = x_ref.shape[0] // pieces
    o_ref[half] = x_ref[...]
    copies = {}
    for step in range(1, half + 1):
        for piece in range(pieces):
            part = pl.ds(piece * size, size)
            reach = ring_reach(count, piece, pieces)
            for toward in (0, 1):
                if step > reach[toward]:
                    continue
                slot = (half - step) % count if toward == 0 else (half + step) % count
                source = (slot + 1) % count if toward == 0 else (slot - 1) % count
                if step > 1:
                    copies[(step - 1, toward, piece)].wait_recv()
                copy = pltpu.make_async_remote_copy(
                    src_ref=x_ref.at[part] if step == 1 else o_ref.at[source, part],
                    dst_ref=o_ref.at[slot, part],
                    send_sem=send_sem.at[toward, step - 1, piece],
                    recv_sem=recv_sem.at[toward, step - 1, piece],
                    device_id=(row, right if toward == 0 else left),
                    device_id_type=pl.DeviceIdType.MESH,
                )
                copy.start()
                copies[(step, toward, piece)] = copy
    for piece in range(pieces):
        reach = ring_reach(count, piece, pieces)
        copies[(reach[0], 0, piece)].wait_recv()
        copies[(reach[1], 1, piece)].wait_recv()
    for copy in copies.values():
        copy.wait_send()


def kernel_gather(block, axis, other, collective_id, pieces=4):
    count = lax.axis_size(axis)
    return pl.pallas_call(
        functools.partial(
            ring_gather_kernel, count=count, axis=axis, other=other, pieces=pieces
        ),
        out_shape=jax.ShapeDtypeStruct((count,) + block.shape, block.dtype),
        in_specs=[pl.BlockSpec(memory_space=pltpu.VMEM)],
        out_specs=pl.BlockSpec(memory_space=pltpu.VMEM),
        scratch_shapes=[
            pltpu.SemaphoreType.DMA((2, count // 2, pieces)),
            pltpu.SemaphoreType.DMA((2, count // 2, pieces)),
        ],
        compiler_params=pltpu.CompilerParams(collective_id=collective_id, has_side_effects=True),
    )(block)


def ring_sum_kernel(p_ref, o_ref, sums_in, sums_out, sems, *, count, axis, other, pieces):
    me = lax.axis_index(axis)
    row = lax.axis_index(other)
    right, left = greet_neighbours(me, row, count)
    width = p_ref.shape[2] // pieces

    def own(offset, part):
        return p_ref[lax.rem(me + offset + 2 * count, count), :, part].astype(jnp.float32)

    copies = {}
    for step in range(1, count // 2 + 1):
        for piece in range(pieces):
            part = pl.ds(piece * width, width)
            reach = ring_reach(count, piece, pieces)
            for toward in (0, 1):
                if step > reach[toward]:
                    continue
                if step == 1:
                    first = reach[0] if toward == 0 else count - reach[1]
                    source = p_ref.at[lax.rem(me + first, count), :, part]
                else:
                    copies[(step - 1, toward, piece)].wait_recv()
                    offset = reach[0] - step + 1 if toward == 0 else step - 1 - reach[1]
                    sums_out[toward, step - 2, :, part] = (
                        sums_in[toward, step - 2, :, part].astype(jnp.float32) + own(offset, part)
                    ).astype(sums_out.dtype)
                    source = sums_out.at[toward, step - 2, :, part]
                copy = pltpu.make_async_remote_copy(
                    src_ref=source,
                    dst_ref=sums_in.at[toward, step - 1, :, part],
                    send_sem=sems.at[0, toward, step - 1, piece],
                    recv_sem=sems.at[1, toward, step - 1, piece],
                    device_id=(row, right if toward == 0 else left),
                    device_id_type=pl.DeviceIdType.MESH,
                )
                copy.start()
                copies[(step, toward, piece)] = copy
    for piece in range(pieces):
        reach = ring_reach(count, piece, pieces)
        copies[(reach[0], 0, piece)].wait_recv()
        copies[(reach[1], 1, piece)].wait_recv()
    for copy in copies.values():
        copy.wait_send()
    for piece in range(pieces):
        part = pl.ds(piece * width, width)
        reach = ring_reach(count, piece, pieces)
        total = own(0, part) + sums_in[0, reach[0] - 1, :, part].astype(jnp.float32)
        total = total + sums_in[1, reach[1] - 1, :, part].astype(jnp.float32)
        o_ref[:, part] = total.astype(o_ref.dtype)


def kernel_reduce_scatter(partial, axis, other, collective_id, pieces=4):
    count = lax.axis_size(axis)
    blocks = partial.reshape((count, partial.shape[0] // count) + partial.shape[1:])
    block = blocks.shape[1:]
    reach = count // 2
    return pl.pallas_call(
        functools.partial(
            ring_sum_kernel, count=count, axis=axis, other=other, pieces=pieces
        ),
        out_shape=jax.ShapeDtypeStruct(block, partial.dtype),
        in_specs=[pl.BlockSpec(memory_space=pltpu.VMEM)],
        out_specs=pl.BlockSpec(memory_space=pltpu.VMEM),
        scratch_shapes=[
            pltpu.VMEM((2, reach) + block, partial.dtype),
            pltpu.VMEM((2, reach) + block, partial.dtype),
            pltpu.SemaphoreType.DMA((2, 2, reach, pieces)),
        ],
        compiler_params=pltpu.CompilerParams(collective_id=collective_id, has_side_effects=True),
    )(blocks)


def project_rows(rows, weight):
    flat = rows.reshape(-1, rows.shape[-1])
    return jnp.dot(flat, weight, preferred_element_type=jnp.float32).astype(jnp.bfloat16)


def local(
    hidden,
    norm_gain,
    query_weight,
    key_weight,
    value_weight,
    out_weight,
    encodings,
    row_place,
    neighbour_ids,
    neighbour_counts,
):
    ctx_count = lax.axis_size("ctx")
    ctx_index = lax.axis_index("ctx")
    tok_dev = hidden.shape[0]
    rows_dev = encodings.shape[0]
    slice_tokens = encodings.shape[1]
    enc_width = encodings.shape[2]
    span_dev = tok_dev // CH
    head_width = query_weight.shape[1]
    head_count = head_width // HS
    slot_cap = -(-rows_dev // ctx_count)
    whole = lax.all_gather(hidden, "tp", axis=1, tiled=True)
    values_wide = whole.astype(jnp.float32)
    mean_square = jnp.mean(values_wide * values_wide, axis=1, keepdims=True)
    normed = (values_wide * lax.rsqrt(mean_square + epsilon) * norm_gain[None, :]).astype(
        jnp.bfloat16
    )
    query_full = lax.all_to_all(
        jnp.broadcast_to(query_weight[None], (ctx_count,) + query_weight.shape),
        "ctx",
        split_axis=0,
        concat_axis=0,
        tiled=True,
    ).reshape(-1, query_weight.shape[1])
    query_sum = jnp.dot(normed, query_full, preferred_element_type=jnp.float32)
    queries = (query_sum * HS ** (-0.5)).astype(jnp.bfloat16)
    matches = neighbour_ids.reshape(-1)[:, None] == jnp.arange(row_place.shape[0])[None, :]
    storage = jnp.sum(jnp.where(matches, row_place[None, :], 0), axis=1).reshape(
        ctx_count, rows_dev
    )
    sources = storage // rows_dev
    local_rows = storage % rows_dev
    from_here = sources == ctx_index
    rank_position = jnp.cumsum(from_here.astype(jnp.int32), axis=1) - 1
    picked_rows = from_here & (rank_position == 0)
    pick_list = [jnp.sum(jnp.where(picked_rows, local_rows, 0), axis=1)]
    fill_list = [jnp.any(picked_rows, axis=1)]
    pick_index = jnp.stack(pick_list, axis=1)
    fill_mask = jnp.stack(fill_list, axis=1)
    outgoing = encodings[pick_index] * fill_mask[:, :, None, None].astype(jnp.bfloat16)
    incoming = lax.all_to_all(outgoing, "ctx", split_axis=0, concat_axis=0, tiled=True)
    own_sources = lax.dynamic_index_in_dim(sources, ctx_index, 0, keepdims=False)
    slot_order = jnp.arange(rows_dev)
    earlier = (own_sources[:, None] == own_sources[None, :]) & (
        slot_order[None, :] < slot_order[:, None]
    )
    own_rank = jnp.sum(earlier.astype(jnp.int32), axis=1)
    flat_index = own_sources * slot_cap + own_rank
    picked = incoming.reshape(ctx_count * slot_cap, slice_tokens, enc_width)[flat_index]
    row_total = picked.shape[0]
    full_rows = jnp.swapaxes(kernel_gather(picked, "tp", "ctx", 0), 0, 1).reshape(
        picked.shape[0], -1, picked.shape[2]
    )
    keys = project_rows(full_rows, key_weight).reshape(row_total, -1, head_width)
    values = project_rows(full_rows, value_weight).reshape(row_total, -1, head_width)
    neighbour_len = keys.shape[1]
    prior = shifted(
        jnp.stack([keys[row_total - KNB :], values[row_total - KNB :]]), "ctx", 1
    )
    key_blocks = jnp.concatenate([prior[0], keys], axis=0).reshape(
        span_dev + 1, KNB * neighbour_len, head_width
    )
    value_blocks = jnp.concatenate([prior[1], values], axis=0).reshape(
        span_dev + 1, KNB * neighbour_len, head_width
    )
    first_span = ctx_index * span_dev
    local_counts = lax.dynamic_slice_in_dim(neighbour_counts, first_span, span_dev)
    prior_count = lax.dynamic_slice_in_dim(neighbour_counts, jnp.maximum(first_span - 1, 0), 1)
    block_counts = jnp.concatenate([prior_count, local_counts], axis=0)
    padded = jnp.concatenate(
        [
            jnp.zeros((1, head_width), jnp.bfloat16),
            queries,
            jnp.zeros((CH - 1, head_width), jnp.bfloat16),
        ],
        axis=0,
    )
    query_blocks = padded.reshape(span_dev + 1, CH, head_width)
    slot_of_key = jnp.arange(KNB * neighbour_len) // neighbour_len
    live = slot_of_key[None, :] < block_counts[:, None]
    heads = []
    for head in range(head_count):
        lanes = slice(head * HS, (head + 1) * HS)
        scores = jnp.einsum(
            "wqd,wkd->wqk",
            query_blocks[:, :, lanes],
            key_blocks[:, :, lanes],
            preferred_element_type=jnp.float32,
        )
        scores = jnp.where(live[:, None, :], scores, masked_score)
        peak = jnp.max(scores, axis=2, keepdims=True)
        expos = jnp.exp(scores - peak)
        total = jnp.sum(expos, axis=2, keepdims=True)
        weights = expos.astype(jnp.bfloat16)
        blended = jnp.einsum(
            "wqk,wkd->wqd", weights, value_blocks[:, :, lanes], preferred_element_type=jnp.float32
        )
        heads.append(blended / total)
    blended = jnp.concatenate(heads, axis=2)
    blended = blended.reshape((span_dev + 1) * CH, head_width)[1 : tok_dev + 1]
    position = ctx_index * tok_dev + jnp.arange(tok_dev)
    valid = position % LENGTH >= CH - 1
    attended = jnp.where(valid[:, None], blended, jnp.zeros_like(blended)).astype(jnp.bfloat16)
    mixed_part = jnp.dot(attended, out_weight, preferred_element_type=jnp.float32).astype(
        jnp.bfloat16
    )
    return kernel_reduce_scatter(mixed_part, "tp", "ctx", 1, pieces=8)


def solution(mesh):
    return jax.shard_map(
        local,
        mesh=mesh,
        in_specs=(
            P("ctx", "tp"),
            P(),
            P("ctx", "tp"),
            P(None, "tp"),
            P(None, "tp"),
            P("tp", None),
            P("ctx", "tp", None),
            P(),
            P(),
            P(),
        ),
        out_specs=P(("ctx", "tp"), None),
        check_vma=False,
    )
```

```python
import functools

import jax
import jax.numpy as jnp
from jax import lax
from jax.experimental import pallas as pl
from jax.experimental.pallas import tpu as pltpu
from jax.sharding import PartitionSpec as P

HS = 128
CH = 64
KNB = 2
LENGTH = 8192


epsilon = 1e-05
masked_score = -1e30


def shifted(block, axis, distance):
    devices = range(lax.axis_size(axis))
    route = [(i - distance, i) for i in devices if i - distance in devices]
    return lax.ppermute(block, axis, route)


def greet_neighbours(me, row, count):
    right = lax.rem(me + 1, count)
    left = lax.rem(me + count - 1, count)
    barrier = pltpu.get_barrier_semaphore()
    for neighbour in (left, right):
        pl.semaphore_signal(
            barrier, inc=1, device_id=(row, neighbour), device_id_type=pl.DeviceIdType.MESH
        )
    pl.semaphore_wait(barrier, 2)
    return right, left


def ring_reach(count, piece, pieces):
    far = count // 2
    if count % 2 == 0 and piece >= pieces // 2:
        return (far - 1, far)
    return (far, count - 1 - far)


def ring_gather_kernel(x_ref, o_ref, send_sem, recv_sem, *, count, axis, other, pieces):
    me = lax.axis_index(axis)
    row = lax.axis_index(other)
    right, left = greet_neighbours(me, row, count)
    half = count // 2
    size = x_ref.shape[0] // pieces
    o_ref[half] = x_ref[...]
    copies = {}
    for step in range(1, half + 1):
        for piece in range(pieces):
            part = pl.ds(piece * size, size)
            reach = ring_reach(count, piece, pieces)
            for toward in (0, 1):
                if step > reach[toward]:
                    continue
                slot = (half - step) % count if toward == 0 else (half + step) % count
                source = (slot + 1) % count if toward == 0 else (slot - 1) % count
                if step > 1:
                    copies[(step - 1, toward, piece)].wait_recv()
                copy = pltpu.make_async_remote_copy(
                    src_ref=x_ref.at[part] if step == 1 else o_ref.at[source, part],
                    dst_ref=o_ref.at[slot, part],
                    send_sem=send_sem.at[toward, step - 1, piece],
                    recv_sem=recv_sem.at[toward, step - 1, piece],
                    device_id=(row, right if toward == 0 else left),
                    device_id_type=pl.DeviceIdType.MESH,
                )
                copy.start()
                copies[(step, toward, piece)] = copy
    for piece in range(pieces):
        reach = ring_reach(count, piece, pieces)
        copies[(reach[0], 0, piece)].wait_recv()
        copies[(reach[1], 1, piece)].wait_recv()
    for copy in copies.values():
        copy.wait_send()


def kernel_gather(block, axis, other, collective_id, pieces=4):
    count = lax.axis_size(axis)
    return pl.pallas_call(
        functools.partial(
            ring_gather_kernel, count=count, axis=axis, other=other, pieces=pieces
        ),
        out_shape=jax.ShapeDtypeStruct((count,) + block.shape, block.dtype),
        in_specs=[pl.BlockSpec(memory_space=pltpu.VMEM)],
        out_specs=pl.BlockSpec(memory_space=pltpu.VMEM),
        scratch_shapes=[
            pltpu.SemaphoreType.DMA((2, count // 2, pieces)),
            pltpu.SemaphoreType.DMA((2, count // 2, pieces)),
        ],
        compiler_params=pltpu.CompilerParams(collective_id=collective_id, has_side_effects=True),
    )(block)


def ring_sum_kernel(p_ref, o_ref, sums_in, sums_out, sems, *, count, axis, other, pieces):
    me = lax.axis_index(axis)
    row = lax.axis_index(other)
    right, left = greet_neighbours(me, row, count)
    width = p_ref.shape[2] // pieces

    def own(offset, part):
        return p_ref[lax.rem(me + offset + 2 * count, count), :, part].astype(jnp.float32)

    copies = {}
    for step in range(1, count // 2 + 1):
        for piece in range(pieces):
            part = pl.ds(piece * width, width)
            reach = ring_reach(count, piece, pieces)
            for toward in (0, 1):
                if step > reach[toward]:
                    continue
                if step == 1:
                    first = reach[0] if toward == 0 else count - reach[1]
                    source = p_ref.at[lax.rem(me + first, count), :, part]
                else:
                    copies[(step - 1, toward, piece)].wait_recv()
                    offset = reach[0] - step + 1 if toward == 0 else step - 1 - reach[1]
                    sums_out[toward, step - 2, :, part] = (
                        sums_in[toward, step - 2, :, part].astype(jnp.float32) + own(offset, part)
                    ).astype(sums_out.dtype)
                    source = sums_out.at[toward, step - 2, :, part]
                copy = pltpu.make_async_remote_copy(
                    src_ref=source,
                    dst_ref=sums_in.at[toward, step - 1, :, part],
                    send_sem=sems.at[0, toward, step - 1, piece],
                    recv_sem=sems.at[1, toward, step - 1, piece],
                    device_id=(row, right if toward == 0 else left),
                    device_id_type=pl.DeviceIdType.MESH,
                )
                copy.start()
                copies[(step, toward, piece)] = copy
    for piece in range(pieces):
        reach = ring_reach(count, piece, pieces)
        copies[(reach[0], 0, piece)].wait_recv()
        copies[(reach[1], 1, piece)].wait_recv()
    for copy in copies.values():
        copy.wait_send()
    for piece in range(pieces):
        part = pl.ds(piece * width, width)
        reach = ring_reach(count, piece, pieces)
        total = own(0, part) + sums_in[0, reach[0] - 1, :, part].astype(jnp.float32)
        total = total + sums_in[1, reach[1] - 1, :, part].astype(jnp.float32)
        o_ref[:, part] = total.astype(o_ref.dtype)


def kernel_reduce_scatter(partial, axis, other, collective_id, pieces=4):
    count = lax.axis_size(axis)
    blocks = partial.reshape((count, partial.shape[0] // count) + partial.shape[1:])
    block = blocks.shape[1:]
    reach = count // 2
    return pl.pallas_call(
        functools.partial(
            ring_sum_kernel, count=count, axis=axis, other=other, pieces=pieces
        ),
        out_shape=jax.ShapeDtypeStruct(block, partial.dtype),
        in_specs=[pl.BlockSpec(memory_space=pltpu.VMEM)],
        out_specs=pl.BlockSpec(memory_space=pltpu.VMEM),
        scratch_shapes=[
            pltpu.VMEM((2, reach) + block, partial.dtype),
            pltpu.VMEM((2, reach) + block, partial.dtype),
            pltpu.SemaphoreType.DMA((2, 2, reach, pieces)),
        ],
        compiler_params=pltpu.CompilerParams(collective_id=collective_id, has_side_effects=True),
    )(blocks)


def project_rows(rows, weight):
    flat = rows.reshape(-1, rows.shape[-1])
    return jnp.dot(flat, weight, preferred_element_type=jnp.float32).astype(jnp.bfloat16)


def local(
    hidden,
    norm_gain,
    query_weight,
    key_weight,
    value_weight,
    out_weight,
    encodings,
    row_place,
    neighbour_ids,
    neighbour_counts,
):
    ctx_count = lax.axis_size("ctx")
    ctx_index = lax.axis_index("ctx")
    tok_dev = hidden.shape[0]
    rows_dev = encodings.shape[0]
    slice_tokens = encodings.shape[1]
    enc_width = encodings.shape[2]
    span_dev = tok_dev // CH
    head_width = query_weight.shape[1]
    head_count = head_width // HS
    slot_cap = -(-rows_dev // ctx_count)
    whole = lax.all_gather(hidden, "tp", axis=1, tiled=True)
    values_wide = whole.astype(jnp.float32)
    mean_square = jnp.mean(values_wide * values_wide, axis=1, keepdims=True)
    normed = (values_wide * lax.rsqrt(mean_square + epsilon) * norm_gain[None, :]).astype(
        jnp.bfloat16
    )
    matches = neighbour_ids.reshape(-1)[:, None] == jnp.arange(row_place.shape[0])[None, :]
    storage = jnp.sum(jnp.where(matches, row_place[None, :], 0), axis=1).reshape(
        ctx_count, rows_dev
    )
    sources = storage // rows_dev
    local_rows = storage % rows_dev
    from_here = sources == ctx_index
    rank_position = jnp.cumsum(from_here.astype(jnp.int32), axis=1) - 1
    picked_rows = from_here & (rank_position == 0)
    pick_list = [jnp.sum(jnp.where(picked_rows, local_rows, 0), axis=1)]
    fill_list = [jnp.any(picked_rows, axis=1)]
    pick_index = jnp.stack(pick_list, axis=1)
    fill_mask = jnp.stack(fill_list, axis=1)
    outgoing = encodings[pick_index] * fill_mask[:, :, None, None].astype(jnp.bfloat16)
    incoming = lax.all_to_all(outgoing, "ctx", split_axis=0, concat_axis=0, tiled=True)
    own_sources = lax.dynamic_index_in_dim(sources, ctx_index, 0, keepdims=False)
    slot_order = jnp.arange(rows_dev)
    earlier = (own_sources[:, None] == own_sources[None, :]) & (
        slot_order[None, :] < slot_order[:, None]
    )
    own_rank = jnp.sum(earlier.astype(jnp.int32), axis=1)
    flat_index = own_sources * slot_cap + own_rank
    picked = incoming.reshape(ctx_count * slot_cap, slice_tokens, enc_width)[flat_index]
    row_total = picked.shape[0]
    full_rows = jnp.swapaxes(kernel_gather(picked, "tp", "ctx", 0), 0, 1).reshape(
        picked.shape[0], -1, picked.shape[2]
    )
    query_source, full_rows = lax.optimization_barrier((query_weight, full_rows))
    query_full = lax.all_to_all(
        jnp.broadcast_to(query_source[None], (ctx_count,) + query_weight.shape),
        "ctx",
        split_axis=0,
        concat_axis=0,
        tiled=True,
    ).reshape(-1, query_weight.shape[1])
    query_sum = jnp.dot(normed, query_full, preferred_element_type=jnp.float32)
    queries = (query_sum * HS ** (-0.5)).astype(jnp.bfloat16)
    keys = project_rows(full_rows, key_weight).reshape(row_total, -1, head_width)
    values = project_rows(full_rows, value_weight).reshape(row_total, -1, head_width)
    neighbour_len = keys.shape[1]
    prior = shifted(
        jnp.stack([keys[row_total - KNB :], values[row_total - KNB :]]), "ctx", 1
    )
    key_blocks = jnp.concatenate([prior[0], keys], axis=0).reshape(
        span_dev + 1, KNB * neighbour_len, head_width
    )
    value_blocks = jnp.concatenate([prior[1], values], axis=0).reshape(
        span_dev + 1, KNB * neighbour_len, head_width
    )
    first_span = ctx_index * span_dev
    local_counts = lax.dynamic_slice_in_dim(neighbour_counts, first_span, span_dev)
    prior_count = lax.dynamic_slice_in_dim(neighbour_counts, jnp.maximum(first_span - 1, 0), 1)
    block_counts = jnp.concatenate([prior_count, local_counts], axis=0)
    padded = jnp.concatenate(
        [
            jnp.zeros((1, head_width), jnp.bfloat16),
            queries,
            jnp.zeros((CH - 1, head_width), jnp.bfloat16),
        ],
        axis=0,
    )
    query_blocks = padded.reshape(span_dev + 1, CH, head_width)
    slot_of_key = jnp.arange(KNB * neighbour_len) // neighbour_len
    live = slot_of_key[None, :] < block_counts[:, None]
    heads = []
    for head in range(head_count):
        lanes = slice(head * HS, (head + 1) * HS)
        scores = jnp.einsum(
            "wqd,wkd->wqk",
            query_blocks[:, :, lanes],
            key_blocks[:, :, lanes],
            preferred_element_type=jnp.float32,
        )
        scores = jnp.where(live[:, None, :], scores, masked_score)
        peak = jnp.max(scores, axis=2, keepdims=True)
        expos = jnp.exp(scores - peak)
        total = jnp.sum(expos, axis=2, keepdims=True)
        weights = expos.astype(jnp.bfloat16)
        blended = jnp.einsum(
            "wqk,wkd->wqd", weights, value_blocks[:, :, lanes], preferred_element_type=jnp.float32
        )
        heads.append(blended / total)
    blended = jnp.concatenate(heads, axis=2)
    blended = blended.reshape((span_dev + 1) * CH, head_width)[1 : tok_dev + 1]
    position = ctx_index * tok_dev + jnp.arange(tok_dev)
    valid = position % LENGTH >= CH - 1
    attended = jnp.where(valid[:, None], blended, jnp.zeros_like(blended)).astype(jnp.bfloat16)
    mixed_part = jnp.dot(attended, out_weight, preferred_element_type=jnp.float32).astype(
        jnp.bfloat16
    )
    return kernel_reduce_scatter(mixed_part, "tp", "ctx", 1)


def solution(mesh):
    return jax.shard_map(
        local,
        mesh=mesh,
        in_specs=(
            P("ctx", "tp"),
            P(),
            P("ctx", "tp"),
            P(None, "tp"),
            P(None, "tp"),
            P("tp", None),
            P("ctx", "tp", None),
            P(),
            P(),
            P(),
        ),
        out_specs=P(("ctx", "tp"), None),
        check_vma=False,
    )
```

```python
import functools

import jax
import jax.numpy as jnp
from jax import lax
from jax.experimental import pallas as pl
from jax.experimental.pallas import tpu as pltpu
from jax.sharding import PartitionSpec as P

HS = 128
CH = 64
KNB = 2
LENGTH = 8192


epsilon = 1e-05
masked_score = -1e30


def shifted(block, axis, distance):
    devices = range(lax.axis_size(axis))
    route = [(i - distance, i) for i in devices if i - distance in devices]
    return lax.ppermute(block, axis, route)


def greet_neighbours(me, row, count):
    right = lax.rem(me + 1, count)
    left = lax.rem(me + count - 1, count)
    barrier = pltpu.get_barrier_semaphore()
    for neighbour in (left, right):
        pl.semaphore_signal(
            barrier, inc=1, device_id=(row, neighbour), device_id_type=pl.DeviceIdType.MESH
        )
    pl.semaphore_wait(barrier, 2)
    return right, left


def ring_reach(count, piece, pieces):
    far = count // 2
    if count % 2 == 0 and piece >= pieces // 2:
        return (far - 1, far)
    return (far, count - 1 - far)


def ring_gather_kernel(x_ref, o_ref, send_sem, recv_sem, *, count, axis, other, pieces):
    me = lax.axis_index(axis)
    row = lax.axis_index(other)
    right, left = greet_neighbours(me, row, count)
    half = count // 2
    size = x_ref.shape[0] // pieces
    o_ref[half] = x_ref[...]
    copies = {}
    for step in range(1, half + 1):
        for piece in range(pieces):
            part = pl.ds(piece * size, size)
            reach = ring_reach(count, piece, pieces)
            for toward in (0, 1):
                if step > reach[toward]:
                    continue
                slot = (half - step) % count if toward == 0 else (half + step) % count
                source = (slot + 1) % count if toward == 0 else (slot - 1) % count
                if step > 1:
                    copies[(step - 1, toward, piece)].wait_recv()
                copy = pltpu.make_async_remote_copy(
                    src_ref=x_ref.at[part] if step == 1 else o_ref.at[source, part],
                    dst_ref=o_ref.at[slot, part],
                    send_sem=send_sem.at[toward, step - 1, piece],
                    recv_sem=recv_sem.at[toward, step - 1, piece],
                    device_id=(row, right if toward == 0 else left),
                    device_id_type=pl.DeviceIdType.MESH,
                )
                copy.start()
                copies[(step, toward, piece)] = copy
    for piece in range(pieces):
        reach = ring_reach(count, piece, pieces)
        copies[(reach[0], 0, piece)].wait_recv()
        copies[(reach[1], 1, piece)].wait_recv()
    for copy in copies.values():
        copy.wait_send()


def kernel_gather(block, axis, other, collective_id, pieces=4):
    count = lax.axis_size(axis)
    return pl.pallas_call(
        functools.partial(
            ring_gather_kernel, count=count, axis=axis, other=other, pieces=pieces
        ),
        out_shape=jax.ShapeDtypeStruct((count,) + block.shape, block.dtype),
        in_specs=[pl.BlockSpec(memory_space=pltpu.VMEM)],
        out_specs=pl.BlockSpec(memory_space=pltpu.VMEM),
        scratch_shapes=[
            pltpu.SemaphoreType.DMA((2, count // 2, pieces)),
            pltpu.SemaphoreType.DMA((2, count // 2, pieces)),
        ],
        compiler_params=pltpu.CompilerParams(collective_id=collective_id, has_side_effects=True),
    )(block)


def ring_sum_kernel(p_ref, o_ref, sums_in, sums_out, sems, *, count, axis, other, pieces):
    me = lax.axis_index(axis)
    row = lax.axis_index(other)
    right, left = greet_neighbours(me, row, count)
    width = p_ref.shape[2] // pieces

    def own(offset, part):
        return p_ref[lax.rem(me + offset + 2 * count, count), :, part].astype(jnp.float32)

    copies = {}
    for step in range(1, count // 2 + 1):
        for piece in range(pieces):
            part = pl.ds(piece * width, width)
            reach = ring_reach(count, piece, pieces)
            for toward in (0, 1):
                if step > reach[toward]:
                    continue
                if step == 1:
                    first = reach[0] if toward == 0 else count - reach[1]
                    source = p_ref.at[lax.rem(me + first, count), :, part]
                else:
                    copies[(step - 1, toward, piece)].wait_recv()
                    offset = reach[0] - step + 1 if toward == 0 else step - 1 - reach[1]
                    sums_out[toward, step - 2, :, part] = (
                        sums_in[toward, step - 2, :, part].astype(jnp.float32) + own(offset, part)
                    ).astype(sums_out.dtype)
                    source = sums_out.at[toward, step - 2, :, part]
                copy = pltpu.make_async_remote_copy(
                    src_ref=source,
                    dst_ref=sums_in.at[toward, step - 1, :, part],
                    send_sem=sems.at[0, toward, step - 1, piece],
                    recv_sem=sems.at[1, toward, step - 1, piece],
                    device_id=(row, right if toward == 0 else left),
                    device_id_type=pl.DeviceIdType.MESH,
                )
                copy.start()
                copies[(step, toward, piece)] = copy
    for piece in range(pieces):
        reach = ring_reach(count, piece, pieces)
        copies[(reach[0], 0, piece)].wait_recv()
        copies[(reach[1], 1, piece)].wait_recv()
    for copy in copies.values():
        copy.wait_send()
    for piece in range(pieces):
        part = pl.ds(piece * width, width)
        reach = ring_reach(count, piece, pieces)
        total = own(0, part) + sums_in[0, reach[0] - 1, :, part].astype(jnp.float32)
        total = total + sums_in[1, reach[1] - 1, :, part].astype(jnp.float32)
        o_ref[:, part] = total.astype(o_ref.dtype)


def kernel_reduce_scatter(partial, axis, other, collective_id, pieces=4):
    count = lax.axis_size(axis)
    blocks = partial.reshape((count, partial.shape[0] // count) + partial.shape[1:])
    block = blocks.shape[1:]
    reach = count // 2
    return pl.pallas_call(
        functools.partial(
            ring_sum_kernel, count=count, axis=axis, other=other, pieces=pieces
        ),
        out_shape=jax.ShapeDtypeStruct(block, partial.dtype),
        in_specs=[pl.BlockSpec(memory_space=pltpu.VMEM)],
        out_specs=pl.BlockSpec(memory_space=pltpu.VMEM),
        scratch_shapes=[
            pltpu.VMEM((2, reach) + block, partial.dtype),
            pltpu.VMEM((2, reach) + block, partial.dtype),
            pltpu.SemaphoreType.DMA((2, 2, reach, pieces)),
        ],
        compiler_params=pltpu.CompilerParams(collective_id=collective_id, has_side_effects=True),
    )(blocks)


def project_rows(rows, weight):
    flat = rows.reshape(-1, rows.shape[-1])
    return jnp.dot(flat, weight, preferred_element_type=jnp.float32).astype(jnp.bfloat16)


def local(
    hidden,
    norm_gain,
    query_weight,
    key_weight,
    value_weight,
    out_weight,
    encodings,
    row_place,
    neighbour_ids,
    neighbour_counts,
):
    ctx_count = lax.axis_size("ctx")
    ctx_index = lax.axis_index("ctx")
    tok_dev = hidden.shape[0]
    rows_dev = encodings.shape[0]
    slice_tokens = encodings.shape[1]
    enc_width = encodings.shape[2]
    span_dev = tok_dev // CH
    head_width = query_weight.shape[1]
    head_count = head_width // HS
    slot_cap = -(-rows_dev // ctx_count)
    whole = lax.all_gather(hidden, "tp", axis=1, tiled=True)
    values_wide = whole.astype(jnp.float32)
    mean_square = jnp.mean(values_wide * values_wide, axis=1, keepdims=True)
    normed = (values_wide * lax.rsqrt(mean_square + epsilon) * norm_gain[None, :]).astype(
        jnp.bfloat16
    )
    query_full = lax.all_to_all(
        jnp.broadcast_to(query_weight[None], (ctx_count,) + query_weight.shape),
        "ctx",
        split_axis=0,
        concat_axis=0,
        tiled=True,
    ).reshape(-1, query_weight.shape[1])
    query_sum = jnp.dot(normed, query_full, preferred_element_type=jnp.float32)
    queries = (query_sum * HS ** (-0.5)).astype(jnp.bfloat16)
    matches = neighbour_ids.reshape(-1)[:, None] == jnp.arange(row_place.shape[0])[None, :]
    storage = jnp.sum(jnp.where(matches, row_place[None, :], 0), axis=1).reshape(
        ctx_count, rows_dev
    )
    sources = storage // rows_dev
    local_rows = storage % rows_dev
    from_here = sources == ctx_index
    rank_position = jnp.cumsum(from_here.astype(jnp.int32), axis=1) - 1
    picked_rows = from_here & (rank_position == 0)
    pick_list = [jnp.sum(jnp.where(picked_rows, local_rows, 0), axis=1)]
    fill_list = [jnp.any(picked_rows, axis=1)]
    pick_index = jnp.stack(pick_list, axis=1)
    fill_mask = jnp.stack(fill_list, axis=1)
    outgoing = encodings[pick_index] * fill_mask[:, :, None, None].astype(jnp.bfloat16)
    incoming = lax.all_to_all(outgoing, "ctx", split_axis=0, concat_axis=0, tiled=True)
    own_sources = lax.dynamic_index_in_dim(sources, ctx_index, 0, keepdims=False)
    slot_order = jnp.arange(rows_dev)
    earlier = (own_sources[:, None] == own_sources[None, :]) & (
        slot_order[None, :] < slot_order[:, None]
    )
    own_rank = jnp.sum(earlier.astype(jnp.int32), axis=1)
    flat_index = own_sources * slot_cap + own_rank
    picked = incoming.reshape(ctx_count * slot_cap, slice_tokens, enc_width)[flat_index]
    row_total = picked.shape[0]
    full_rows = jnp.swapaxes(kernel_gather(picked, "tp", "ctx", 0, pieces=8), 0, 1).reshape(
        picked.shape[0], -1, picked.shape[2]
    )
    keys = project_rows(full_rows, key_weight).reshape(row_total, -1, head_width)
    values = project_rows(full_rows, value_weight).reshape(row_total, -1, head_width)
    neighbour_len = keys.shape[1]
    prior = shifted(
        jnp.stack([keys[row_total - KNB :], values[row_total - KNB :]]), "ctx", 1
    )
    key_blocks = jnp.concatenate([prior[0], keys], axis=0).reshape(
        span_dev + 1, KNB * neighbour_len, head_width
    )
    value_blocks = jnp.concatenate([prior[1], values], axis=0).reshape(
        span_dev + 1, KNB * neighbour_len, head_width
    )
    first_span = ctx_index * span_dev
    local_counts = lax.dynamic_slice_in_dim(neighbour_counts, first_span, span_dev)
    prior_count = lax.dynamic_slice_in_dim(neighbour_counts, jnp.maximum(first_span - 1, 0), 1)
    block_counts = jnp.concatenate([prior_count, local_counts], axis=0)
    padded = jnp.concatenate(
        [
            jnp.zeros((1, head_width), jnp.bfloat16),
            queries,
            jnp.zeros((CH - 1, head_width), jnp.bfloat16),
        ],
        axis=0,
    )
    query_blocks = padded.reshape(span_dev + 1, CH, head_width)
    slot_of_key = jnp.arange(KNB * neighbour_len) // neighbour_len
    live = slot_of_key[None, :] < block_counts[:, None]
    heads = []
    for head in range(head_count):
        lanes = slice(head * HS, (head + 1) * HS)
        scores = jnp.einsum(
            "wqd,wkd->wqk",
            query_blocks[:, :, lanes],
            key_blocks[:, :, lanes],
            preferred_element_type=jnp.float32,
        )
        scores = jnp.where(live[:, None, :], scores, masked_score)
        peak = jnp.max(scores, axis=2, keepdims=True)
        expos = jnp.exp(scores - peak)
        total = jnp.sum(expos, axis=2, keepdims=True)
        weights = expos.astype(jnp.bfloat16)
        blended = jnp.einsum(
            "wqk,wkd->wqd", weights, value_blocks[:, :, lanes], preferred_element_type=jnp.float32
        )
        heads.append(blended / total)
    blended = jnp.concatenate(heads, axis=2)
    blended = blended.reshape((span_dev + 1) * CH, head_width)[1 : tok_dev + 1]
    position = ctx_index * tok_dev + jnp.arange(tok_dev)
    valid = position % LENGTH >= CH - 1
    attended = jnp.where(valid[:, None], blended, jnp.zeros_like(blended)).astype(jnp.bfloat16)
    mixed_part = jnp.dot(attended, out_weight, preferred_element_type=jnp.float32).astype(
        jnp.bfloat16
    )
    return kernel_reduce_scatter(mixed_part, "tp", "ctx", 1)


def solution(mesh):
    return jax.shard_map(
        local,
        mesh=mesh,
        in_specs=(
            P("ctx", "tp"),
            P(),
            P("ctx", "tp"),
            P(None, "tp"),
            P(None, "tp"),
            P("tp", None),
            P("ctx", "tp", None),
            P(),
            P(),
            P(),
        ),
        out_specs=P(("ctx", "tp"), None),
        check_vma=False,
    )
```

```python
import functools

import jax
import jax.numpy as jnp
from jax import lax
from jax.experimental import pallas as pl
from jax.experimental.pallas import tpu as pltpu
from jax.sharding import PartitionSpec as P

HS = 128
CH = 64
KNB = 2
LENGTH = 8192


epsilon = 1e-05
masked_score = -1e30


def shifted(block, axis, distance):
    devices = range(lax.axis_size(axis))
    route = [(i - distance, i) for i in devices if i - distance in devices]
    return lax.ppermute(block, axis, route)


def greet_neighbours(me, row, count):
    right = lax.rem(me + 1, count)
    left = lax.rem(me + count - 1, count)
    barrier = pltpu.get_barrier_semaphore()
    for neighbour in (left, right):
        pl.semaphore_signal(
            barrier, inc=1, device_id=(row, neighbour), device_id_type=pl.DeviceIdType.MESH
        )
    pl.semaphore_wait(barrier, 2)
    return right, left


def ring_reach(count, piece, pieces):
    far = count // 2
    if count % 2 == 0 and piece >= pieces // 2:
        return (far - 1, far)
    return (far, count - 1 - far)


def ring_gather_kernel(x_ref, o_ref, send_sem, recv_sem, *, count, axis, other, pieces):
    me = lax.axis_index(axis)
    row = lax.axis_index(other)
    right, left = greet_neighbours(me, row, count)
    half = count // 2
    size = x_ref.shape[0] // pieces
    o_ref[half] = x_ref[...]
    copies = {}
    for step in range(1, half + 1):
        for piece in range(pieces):
            part = pl.ds(piece * size, size)
            reach = ring_reach(count, piece, pieces)
            for toward in (0, 1):
                if step > reach[toward]:
                    continue
                slot = (half - step) % count if toward == 0 else (half + step) % count
                source = (slot + 1) % count if toward == 0 else (slot - 1) % count
                if step > 1:
                    copies[(step - 1, toward, piece)].wait_recv()
                copy = pltpu.make_async_remote_copy(
                    src_ref=x_ref.at[part] if step == 1 else o_ref.at[source, part],
                    dst_ref=o_ref.at[slot, part],
                    send_sem=send_sem.at[toward, step - 1, piece],
                    recv_sem=recv_sem.at[toward, step - 1, piece],
                    device_id=(row, right if toward == 0 else left),
                    device_id_type=pl.DeviceIdType.MESH,
                )
                copy.start()
                copies[(step, toward, piece)] = copy
    for piece in range(pieces):
        reach = ring_reach(count, piece, pieces)
        copies[(reach[0], 0, piece)].wait_recv()
        copies[(reach[1], 1, piece)].wait_recv()
    for copy in copies.values():
        copy.wait_send()


def kernel_gather(block, axis, other, collective_id, pieces=4):
    count = lax.axis_size(axis)
    return pl.pallas_call(
        functools.partial(
            ring_gather_kernel, count=count, axis=axis, other=other, pieces=pieces
        ),
        out_shape=jax.ShapeDtypeStruct((count,) + block.shape, block.dtype),
        in_specs=[pl.BlockSpec(memory_space=pltpu.VMEM)],
        out_specs=pl.BlockSpec(memory_space=pltpu.VMEM),
        scratch_shapes=[
            pltpu.SemaphoreType.DMA((2, count // 2, pieces)),
            pltpu.SemaphoreType.DMA((2, count // 2, pieces)),
        ],
        compiler_params=pltpu.CompilerParams(collective_id=collective_id, has_side_effects=True),
    )(block)


def ring_sum_kernel(p_ref, o_ref, sums_in, sums_out, sems, *, count, axis, other, pieces):
    me = lax.axis_index(axis)
    row = lax.axis_index(other)
    right, left = greet_neighbours(me, row, count)
    width = p_ref.shape[2] // pieces

    def own(offset, part):
        return p_ref[lax.rem(me + offset + 2 * count, count), :, part].astype(jnp.float32)

    copies = {}
    for step in range(1, count // 2 + 1):
        for piece in range(pieces):
            part = pl.ds(piece * width, width)
            reach = ring_reach(count, piece, pieces)
            for toward in (0, 1):
                if step > reach[toward]:
                    continue
                if step == 1:
                    first = reach[0] if toward == 0 else count - reach[1]
                    source = p_ref.at[lax.rem(me + first, count), :, part]
                else:
                    copies[(step - 1, toward, piece)].wait_recv()
                    offset = reach[0] - step + 1 if toward == 0 else step - 1 - reach[1]
                    sums_out[toward, step - 2, :, part] = (
                        sums_in[toward, step - 2, :, part].astype(jnp.float32) + own(offset, part)
                    ).astype(sums_out.dtype)
                    source = sums_out.at[toward, step - 2, :, part]
                copy = pltpu.make_async_remote_copy(
                    src_ref=source,
                    dst_ref=sums_in.at[toward, step - 1, :, part],
                    send_sem=sems.at[0, toward, step - 1, piece],
                    recv_sem=sems.at[1, toward, step - 1, piece],
                    device_id=(row, right if toward == 0 else left),
                    device_id_type=pl.DeviceIdType.MESH,
                )
                copy.start()
                copies[(step, toward, piece)] = copy
    for piece in range(pieces):
        reach = ring_reach(count, piece, pieces)
        copies[(reach[0], 0, piece)].wait_recv()
        copies[(reach[1], 1, piece)].wait_recv()
    for copy in copies.values():
        copy.wait_send()
    for piece in range(pieces):
        part = pl.ds(piece * width, width)
        reach = ring_reach(count, piece, pieces)
        total = own(0, part) + sums_in[0, reach[0] - 1, :, part].astype(jnp.float32)
        total = total + sums_in[1, reach[1] - 1, :, part].astype(jnp.float32)
        o_ref[:, part] = total.astype(o_ref.dtype)


def kernel_reduce_scatter(partial, axis, other, collective_id, pieces=4):
    count = lax.axis_size(axis)
    blocks = partial.reshape((count, partial.shape[0] // count) + partial.shape[1:])
    block = blocks.shape[1:]
    reach = count // 2
    return pl.pallas_call(
        functools.partial(
            ring_sum_kernel, count=count, axis=axis, other=other, pieces=pieces
        ),
        out_shape=jax.ShapeDtypeStruct(block, partial.dtype),
        in_specs=[pl.BlockSpec(memory_space=pltpu.VMEM)],
        out_specs=pl.BlockSpec(memory_space=pltpu.VMEM),
        scratch_shapes=[
            pltpu.VMEM((2, reach) + block, partial.dtype),
            pltpu.VMEM((2, reach) + block, partial.dtype),
            pltpu.SemaphoreType.DMA((2, 2, reach, pieces)),
        ],
        compiler_params=pltpu.CompilerParams(collective_id=collective_id, has_side_effects=True),
    )(blocks)


def project_rows(rows, weight):
    flat = rows.reshape(-1, rows.shape[-1])
    return jnp.dot(flat, weight, preferred_element_type=jnp.float32).astype(jnp.bfloat16)


def local(
    hidden,
    norm_gain,
    query_weight,
    key_weight,
    value_weight,
    out_weight,
    encodings,
    row_place,
    neighbour_ids,
    neighbour_counts,
):
    ctx_count = lax.axis_size("ctx")
    ctx_index = lax.axis_index("ctx")
    tok_dev = hidden.shape[0]
    rows_dev = encodings.shape[0]
    slice_tokens = encodings.shape[1]
    enc_width = encodings.shape[2]
    span_dev = tok_dev // CH
    head_width = query_weight.shape[1]
    head_count = head_width // HS
    slot_cap = -(-rows_dev // ctx_count)
    whole = lax.all_gather(hidden, "tp", axis=1, tiled=True)
    values_wide = whole.astype(jnp.float32)
    mean_square = jnp.mean(values_wide * values_wide, axis=1, keepdims=True)
    normed = (values_wide * lax.rsqrt(mean_square + epsilon) * norm_gain[None, :]).astype(
        jnp.bfloat16
    )
    query_full = lax.all_to_all(
        jnp.broadcast_to(query_weight[None], (ctx_count,) + query_weight.shape),
        "ctx",
        split_axis=0,
        concat_axis=0,
        tiled=True,
    ).reshape(-1, query_weight.shape[1])
    query_sum = jnp.dot(normed, query_full, preferred_element_type=jnp.float32)
    queries = (query_sum * HS ** (-0.5)).astype(jnp.bfloat16)
    matches = neighbour_ids.reshape(-1)[:, None] == jnp.arange(row_place.shape[0])[None, :]
    storage = jnp.sum(jnp.where(matches, row_place[None, :], 0), axis=1).reshape(
        ctx_count, rows_dev
    )
    sources = storage // rows_dev
    local_rows = storage % rows_dev
    from_here = sources == ctx_index
    rank_position = jnp.cumsum(from_here.astype(jnp.int32), axis=1) - 1
    picked_rows = from_here & (rank_position == 0)
    pick_list = [jnp.sum(jnp.where(picked_rows, local_rows, 0), axis=1)]
    fill_list = [jnp.any(picked_rows, axis=1)]
    pick_index = jnp.stack(pick_list, axis=1)
    fill_mask = jnp.stack(fill_list, axis=1)
    outgoing = encodings[pick_index] * fill_mask[:, :, None, None].astype(jnp.bfloat16)
    incoming = lax.all_to_all(outgoing, "ctx", split_axis=0, concat_axis=0, tiled=True)
    own_sources = lax.dynamic_index_in_dim(sources, ctx_index, 0, keepdims=False)
    slot_order = jnp.arange(rows_dev)
    earlier = (own_sources[:, None] == own_sources[None, :]) & (
        slot_order[None, :] < slot_order[:, None]
    )
    own_rank = jnp.sum(earlier.astype(jnp.int32), axis=1)
    flat_index = own_sources * slot_cap + own_rank
    picked = incoming.reshape(ctx_count * slot_cap, slice_tokens, enc_width)[flat_index]
    row_total = picked.shape[0]
    full_rows = jnp.swapaxes(kernel_gather(picked, "tp", "ctx", 0), 0, 1).reshape(
        picked.shape[0], -1, picked.shape[2]
    )
    keys = project_rows(full_rows, key_weight).reshape(row_total, -1, head_width)
    values = project_rows(full_rows, value_weight).reshape(row_total, -1, head_width)
    neighbour_len = keys.shape[1]
    prior = shifted(
        jnp.stack([keys[row_total - KNB :], values[row_total - KNB :]]), "ctx", 1
    )
    key_blocks = jnp.concatenate([prior[0], keys], axis=0).reshape(
        span_dev + 1, KNB * neighbour_len, head_width
    )
    value_blocks = jnp.concatenate([prior[1], values], axis=0).reshape(
        span_dev + 1, KNB * neighbour_len, head_width
    )
    first_span = ctx_index * span_dev
    local_counts = lax.dynamic_slice_in_dim(neighbour_counts, first_span, span_dev)
    prior_count = lax.dynamic_slice_in_dim(neighbour_counts, jnp.maximum(first_span - 1, 0), 1)
    block_counts = jnp.concatenate([prior_count, local_counts], axis=0)
    padded = jnp.concatenate(
        [
            jnp.zeros((1, head_width), jnp.bfloat16),
            queries,
            jnp.zeros((CH - 1, head_width), jnp.bfloat16),
        ],
        axis=0,
    )
    query_blocks = padded.reshape(span_dev + 1, CH, head_width)
    slot_of_key = jnp.arange(KNB * neighbour_len) // neighbour_len
    live = slot_of_key[None, :] < block_counts[:, None]
    heads = []
    for head in range(head_count):
        lanes = slice(head * HS, (head + 1) * HS)
        scores = jnp.einsum(
            "wqd,wkd->wqk",
            query_blocks[:, :, lanes],
            key_blocks[:, :, lanes],
            preferred_element_type=jnp.float32,
        )
        scores = jnp.where(live[:, None, :], scores, masked_score)
        peak = jnp.max(scores, axis=2, keepdims=True)
        expos = jnp.exp(scores - peak)
        total = jnp.sum(expos, axis=2, keepdims=True)
        weights = expos.astype(jnp.bfloat16)
        blended = jnp.einsum(
            "wqk,wkd->wqd", weights, value_blocks[:, :, lanes], preferred_element_type=jnp.float32
        )
        heads.append(blended / total)
    blended = jnp.concatenate(heads, axis=2)
    blended = blended.reshape((span_dev + 1) * CH, head_width)[1 : tok_dev + 1]
    position = ctx_index * tok_dev + jnp.arange(tok_dev)
    valid = position % LENGTH >= CH - 1
    attended = jnp.where(valid[:, None], blended, jnp.zeros_like(blended)).astype(jnp.bfloat16)
    mixed_part = jnp.dot(attended, out_weight, preferred_element_type=jnp.float32).astype(
        jnp.bfloat16
    )
    return kernel_reduce_scatter(mixed_part, "tp", "ctx", 1, pieces=2)


def solution(mesh):
    return jax.shard_map(
        local,
        mesh=mesh,
        in_specs=(
            P("ctx", "tp"),
            P(),
            P("ctx", "tp"),
            P(None, "tp"),
            P(None, "tp"),
            P("tp", None),
            P("ctx", "tp", None),
            P(),
            P(),
            P(),
        ),
        out_specs=P(("ctx", "tp"), None),
        check_vma=False,
    )
```

```python
import functools

import jax
import jax.numpy as jnp
from jax import lax
from jax.experimental import pallas as pl
from jax.experimental.pallas import tpu as pltpu
from jax.sharding import PartitionSpec as P

HS = 128
CH = 64
KNB = 2
LENGTH = 8192


epsilon = 1e-05
masked_score = -1e30


def shifted(block, axis, distance):
    devices = range(lax.axis_size(axis))
    route = [(i - distance, i) for i in devices if i - distance in devices]
    return lax.ppermute(block, axis, route)


def greet_neighbours(me, row, count):
    right = lax.rem(me + 1, count)
    left = lax.rem(me + count - 1, count)
    barrier = pltpu.get_barrier_semaphore()
    for neighbour in (left, right):
        pl.semaphore_signal(
            barrier, inc=1, device_id=(row, neighbour), device_id_type=pl.DeviceIdType.MESH
        )
    pl.semaphore_wait(barrier, 2)
    return right, left


def ring_reach(count, piece, pieces):
    far = count // 2
    if count % 2 == 0 and piece >= pieces // 2:
        return (far - 1, far)
    return (far, count - 1 - far)


def ring_gather_kernel(x_ref, o_ref, send_sem, recv_sem, *, count, axis, other, pieces):
    me = lax.axis_index(axis)
    row = lax.axis_index(other)
    right, left = greet_neighbours(me, row, count)
    half = count // 2
    size = x_ref.shape[0] // pieces
    o_ref[half] = x_ref[...]
    copies = {}
    for step in range(1, half + 1):
        for piece in range(pieces):
            part = pl.ds(piece * size, size)
            reach = ring_reach(count, piece, pieces)
            for toward in (0, 1):
                if step > reach[toward]:
                    continue
                slot = (half - step) % count if toward == 0 else (half + step) % count
                source = (slot + 1) % count if toward == 0 else (slot - 1) % count
                if step > 1:
                    copies[(step - 1, toward, piece)].wait_recv()
                copy = pltpu.make_async_remote_copy(
                    src_ref=x_ref.at[part] if step == 1 else o_ref.at[source, part],
                    dst_ref=o_ref.at[slot, part],
                    send_sem=send_sem.at[toward, step - 1, piece],
                    recv_sem=recv_sem.at[toward, step - 1, piece],
                    device_id=(row, right if toward == 0 else left),
                    device_id_type=pl.DeviceIdType.MESH,
                )
                copy.start()
                copies[(step, toward, piece)] = copy
    for piece in range(pieces):
        reach = ring_reach(count, piece, pieces)
        copies[(reach[0], 0, piece)].wait_recv()
        copies[(reach[1], 1, piece)].wait_recv()
    for copy in copies.values():
        copy.wait_send()


def kernel_gather(block, axis, other, collective_id, pieces=4):
    count = lax.axis_size(axis)
    return pl.pallas_call(
        functools.partial(
            ring_gather_kernel, count=count, axis=axis, other=other, pieces=pieces
        ),
        out_shape=jax.ShapeDtypeStruct((count,) + block.shape, block.dtype),
        in_specs=[pl.BlockSpec(memory_space=pltpu.VMEM)],
        out_specs=pl.BlockSpec(memory_space=pltpu.VMEM),
        scratch_shapes=[
            pltpu.SemaphoreType.DMA((2, count // 2, pieces)),
            pltpu.SemaphoreType.DMA((2, count // 2, pieces)),
        ],
        compiler_params=pltpu.CompilerParams(collective_id=collective_id, has_side_effects=True),
    )(block)


def ring_sum_kernel(p_ref, o_ref, sums_in, sums_out, sems, *, count, axis, other, pieces):
    me = lax.axis_index(axis)
    row = lax.axis_index(other)
    right, left = greet_neighbours(me, row, count)
    width = p_ref.shape[2] // pieces

    def own(offset, part):
        return p_ref[lax.rem(me + offset + 2 * count, count), :, part].astype(jnp.float32)

    copies = {}
    for step in range(1, count // 2 + 1):
        for piece in range(pieces):
            part = pl.ds(piece * width, width)
            reach = ring_reach(count, piece, pieces)
            for toward in (0, 1):
                if step > reach[toward]:
                    continue
                if step == 1:
                    first = reach[0] if toward == 0 else count - reach[1]
                    source = p_ref.at[lax.rem(me + first, count), :, part]
                else:
                    copies[(step - 1, toward, piece)].wait_recv()
                    offset = reach[0] - step + 1 if toward == 0 else step - 1 - reach[1]
                    sums_out[toward, step - 2, :, part] = (
                        sums_in[toward, step - 2, :, part].astype(jnp.float32) + own(offset, part)
                    ).astype(sums_out.dtype)
                    source = sums_out.at[toward, step - 2, :, part]
                copy = pltpu.make_async_remote_copy(
                    src_ref=source,
                    dst_ref=sums_in.at[toward, step - 1, :, part],
                    send_sem=sems.at[0, toward, step - 1, piece],
                    recv_sem=sems.at[1, toward, step - 1, piece],
                    device_id=(row, right if toward == 0 else left),
                    device_id_type=pl.DeviceIdType.MESH,
                )
                copy.start()
                copies[(step, toward, piece)] = copy
    for piece in range(pieces):
        reach = ring_reach(count, piece, pieces)
        copies[(reach[0], 0, piece)].wait_recv()
        copies[(reach[1], 1, piece)].wait_recv()
    for copy in copies.values():
        copy.wait_send()
    for piece in range(pieces):
        part = pl.ds(piece * width, width)
        reach = ring_reach(count, piece, pieces)
        total = own(0, part) + sums_in[0, reach[0] - 1, :, part].astype(jnp.float32)
        total = total + sums_in[1, reach[1] - 1, :, part].astype(jnp.float32)
        o_ref[:, part] = total.astype(o_ref.dtype)


def kernel_reduce_scatter(partial, axis, other, collective_id, pieces=4):
    count = lax.axis_size(axis)
    blocks = partial.reshape((count, partial.shape[0] // count) + partial.shape[1:])
    block = blocks.shape[1:]
    reach = count // 2
    return pl.pallas_call(
        functools.partial(
            ring_sum_kernel, count=count, axis=axis, other=other, pieces=pieces
        ),
        out_shape=jax.ShapeDtypeStruct(block, partial.dtype),
        in_specs=[pl.BlockSpec(memory_space=pltpu.VMEM)],
        out_specs=pl.BlockSpec(memory_space=pltpu.VMEM),
        scratch_shapes=[
            pltpu.VMEM((2, reach) + block, partial.dtype),
            pltpu.VMEM((2, reach) + block, partial.dtype),
            pltpu.SemaphoreType.DMA((2, 2, reach, pieces)),
        ],
        compiler_params=pltpu.CompilerParams(collective_id=collective_id, has_side_effects=True),
    )(blocks)


def project_rows(rows, weight):
    flat = rows.reshape(-1, rows.shape[-1])
    return jnp.dot(flat, weight, preferred_element_type=jnp.float32).astype(jnp.bfloat16)


def local(
    hidden,
    norm_gain,
    query_weight,
    key_weight,
    value_weight,
    out_weight,
    encodings,
    row_place,
    neighbour_ids,
    neighbour_counts,
):
    ctx_count = lax.axis_size("ctx")
    ctx_index = lax.axis_index("ctx")
    tok_dev = hidden.shape[0]
    rows_dev = encodings.shape[0]
    slice_tokens = encodings.shape[1]
    enc_width = encodings.shape[2]
    span_dev = tok_dev // CH
    head_width = query_weight.shape[1]
    head_count = head_width // HS
    slot_cap = -(-rows_dev // ctx_count)
    whole = lax.all_gather(hidden, "tp", axis=1, tiled=True)
    values_wide = whole.astype(jnp.float32)
    mean_square = jnp.mean(values_wide * values_wide, axis=1, keepdims=True)
    normed = (values_wide * lax.rsqrt(mean_square + epsilon) * norm_gain[None, :]).astype(
        jnp.bfloat16
    )
    query_full = lax.all_to_all(
        jnp.broadcast_to(query_weight[None], (ctx_count,) + query_weight.shape),
        "ctx",
        split_axis=0,
        concat_axis=0,
        tiled=True,
    ).reshape(-1, query_weight.shape[1])
    query_sum = jnp.dot(normed, query_full, preferred_element_type=jnp.float32)
    queries = (query_sum * HS ** (-0.5)).astype(jnp.bfloat16)
    matches = neighbour_ids.reshape(-1)[:, None] == jnp.arange(row_place.shape[0])[None, :]
    storage = jnp.sum(jnp.where(matches, row_place[None, :], 0), axis=1).reshape(
        ctx_count, rows_dev
    )
    sources = storage // rows_dev
    local_rows = storage % rows_dev
    from_here = sources == ctx_index
    rank_position = jnp.cumsum(from_here.astype(jnp.int32), axis=1) - 1
    picked_rows = from_here & (rank_position == 0)
    pick_list = [jnp.sum(jnp.where(picked_rows, local_rows, 0), axis=1)]
    pick_index = jnp.stack(pick_list, axis=1)
    outgoing = encodings[pick_index]
    incoming = lax.all_to_all(outgoing, "ctx", split_axis=0, concat_axis=0, tiled=True)
    own_sources = lax.dynamic_index_in_dim(sources, ctx_index, 0, keepdims=False)
    slot_order = jnp.arange(rows_dev)
    earlier = (own_sources[:, None] == own_sources[None, :]) & (
        slot_order[None, :] < slot_order[:, None]
    )
    own_rank = jnp.sum(earlier.astype(jnp.int32), axis=1)
    flat_index = own_sources * slot_cap + own_rank
    picked = incoming.reshape(ctx_count * slot_cap, slice_tokens, enc_width)[flat_index]
    row_total = picked.shape[0]
    full_rows = jnp.swapaxes(kernel_gather(picked, "tp", "ctx", 0), 0, 1).reshape(
        picked.shape[0], -1, picked.shape[2]
    )
    keys = project_rows(full_rows, key_weight).reshape(row_total, -1, head_width)
    values = project_rows(full_rows, value_weight).reshape(row_total, -1, head_width)
    neighbour_len = keys.shape[1]
    prior = shifted(
        jnp.stack([keys[row_total - KNB :], values[row_total - KNB :]]), "ctx", 1
    )
    key_blocks = jnp.concatenate([prior[0], keys], axis=0).reshape(
        span_dev + 1, KNB * neighbour_len, head_width
    )
    value_blocks = jnp.concatenate([prior[1], values], axis=0).reshape(
        span_dev + 1, KNB * neighbour_len, head_width
    )
    first_span = ctx_index * span_dev
    local_counts = lax.dynamic_slice_in_dim(neighbour_counts, first_span, span_dev)
    prior_count = lax.dynamic_slice_in_dim(neighbour_counts, jnp.maximum(first_span - 1, 0), 1)
    block_counts = jnp.concatenate([prior_count, local_counts], axis=0)
    padded = jnp.concatenate(
        [
            jnp.zeros((1, head_width), jnp.bfloat16),
            queries,
            jnp.zeros((CH - 1, head_width), jnp.bfloat16),
        ],
        axis=0,
    )
    query_blocks = padded.reshape(span_dev + 1, CH, head_width)
    slot_of_key = jnp.arange(KNB * neighbour_len) // neighbour_len
    live = slot_of_key[None, :] < block_counts[:, None]
    heads = []
    for head in range(head_count):
        lanes = slice(head * HS, (head + 1) * HS)
        scores = jnp.einsum(
            "wqd,wkd->wqk",
            query_blocks[:, :, lanes],
            key_blocks[:, :, lanes],
            preferred_element_type=jnp.float32,
        )
        scores = jnp.where(live[:, None, :], scores, masked_score)
        peak = jnp.max(scores, axis=2, keepdims=True)
        expos = jnp.exp(scores - peak)
        total = jnp.sum(expos, axis=2, keepdims=True)
        weights = expos.astype(jnp.bfloat16)
        blended = jnp.einsum(
            "wqk,wkd->wqd", weights, value_blocks[:, :, lanes], preferred_element_type=jnp.float32
        )
        heads.append(blended / total)
    blended = jnp.concatenate(heads, axis=2)
    blended = blended.reshape((span_dev + 1) * CH, head_width)[1 : tok_dev + 1]
    position = ctx_index * tok_dev + jnp.arange(tok_dev)
    valid = position % LENGTH >= CH - 1
    attended = jnp.where(valid[:, None], blended, jnp.zeros_like(blended)).astype(jnp.bfloat16)
    mixed_part = jnp.dot(attended, out_weight, preferred_element_type=jnp.float32).astype(
        jnp.bfloat16
    )
    return kernel_reduce_scatter(mixed_part, "tp", "ctx", 1)


def solution(mesh):
    return jax.shard_map(
        local,
        mesh=mesh,
        in_specs=(
            P("ctx", "tp"),
            P(),
            P("ctx", "tp"),
            P(None, "tp"),
            P(None, "tp"),
            P("tp", None),
            P("ctx", "tp", None),
            P(),
            P(),
            P(),
        ),
        out_specs=P(("ctx", "tp"), None),
        check_vma=False,
    )
```
